768 devices in a mesh: gx: 48 (over x, z_lo, core), gy: 16 (over z_hi, y).
Axes of the slice: x: 4, y: 8, z: 12 (z_hi: 2, z_lo: 6; z = z_hi * 6 + z_lo), core: 2. Of those that a mesh axis runs over, the one named last changes fastest.
Arguments:
- fine_now: float32 [3, 384, 256, 128], P(None, 'gx', 'gy'), may hold values from -6 to 6
- fine_prev: float32 [3, 384, 256, 128], P(None, 'gx', 'gy'), may hold values from -6 to 6
- coarse_now: float32 [3, 192, 128, 128], P(None, 'gx', 'gy'), may hold values from -6 to 6
- coarse_prev: float32 [3, 192, 128, 128], P(None, 'gx', 'gy'), may hold values from -6 to 6
- fine_rho: float32 [384, 256, 128], P('gx', 'gy'), may hold values from 1 to 3
- fine_mu: float32 [384, 256, 128], P('gx', 'gy'), may hold values from 0.3 to 1.5
- fine_lam: float32 [384, 256, 128], P('gx', 'gy'), may hold values from 0.3 to 1.5
- fine_metric: float32 [384, 256, 128], P('gx', 'gy'), may hold values from 0.5 to 2
- coarse_rho: float32 [192, 128, 128], P('gx', 'gy'), may hold values from 1 to 3
- coarse_mu: float32 [192, 128, 128], P('gx', 'gy'), may hold values from 0.3 to 1.5
- coarse_lam: float32 [192, 128, 128], P('gx', 'gy'), may hold values from 0.3 to 1.5
- coarse_metric: float32 [192, 128, 128], P('gx', 'gy'), may hold values from 0.5 to 2
- couple_index: int32 [384, 256, 16], P('gx', 'gy'), may hold values from 0 to 95, as said below
- couple_weight: float32 [384, 256, 16], P('gx', 'gy'), may hold values from 0 to 0.125
Outputs:
- fine_field: float32 [3, 384, 256, 128], P(None, 'gx', 'gy')
- coarse_field: float32 [3, 192, 128, 128], P(None, 'gx', 'gy')
The draws below stay inside these ranges and needn't reach their ends.
Inputs may be any that keep to these rules, and one draw needn't show every extreme that they name: `couple_index`: the sixteen indices of a fine point are a 4 x 4 patch of neighbouring coarse cells of its block's widened top plane, lying within 2 coarse cells of the point's own coarse cell.
All inputs are finite; a program needn't handle non-finite values.
Results may differ from the reference program's by a relative error of at most 0.0001.
Values sent between devices are 32-bit elements; how exact they have to be, the bound alone decides.
No kernel may reach another device: no remote copies, remote signals or barrier semaphores. Data moves between devices by JAX's collectives and lax.ppermute only.
A program may use at most 32 MiB of HBM per device.

```python
import math
import jax
import jax.numpy as jnp
import numpy as np
from jax import lax

CXF = 8
CYF = 16
NZ = 128
COUPLE = 16
CXC = 4
CYC = 8
NXF = 384
NYF = 256
NXC = 192
NYC = 128


def draw_couple_index(key, part):
    key_row, key_col = jax.random.split(key)
    row_local = jnp.arange(NXF, dtype=jnp.int32) % CXF
    col_local = jnp.arange(NYF, dtype=jnp.int32) % CYF
    shift_row = jax.random.randint(key_row, (NXF, NYF), -1, 1, dtype=jnp.int32)
    shift_col = jax.random.randint(key_col, (NXF, NYF), -1, 1, dtype=jnp.int32)
    shift_row = jnp.where(row_local[:, None] == 0, -1, jnp.where(row_local[:, None] == CXF - 1, 0, shift_row))
    shift_col = jnp.where(col_local[None, :] == 0, -1, jnp.where(col_local[None, :] == CYF - 1, 0, shift_col))
    base_row = row_local[:, None] // 2 + 1 + shift_row
    base_col = col_local[None, :] // 2 + 1 + shift_col
    spread = jnp.arange(4, dtype=jnp.int32)
    grid_row = base_row[:, :, None, None] + spread[None, None, :, None]
    grid_col = base_col[:, :, None, None] + spread[None, None, None, :]
    return (grid_row * (CYC + 4) + grid_col).reshape(NXF, NYF, COUPLE).astype(jnp.int32)


def steps_of(stream_key, dims, pieces, least, high):
    def one(position, shards_of):
        heights = jax.random.uniform(jax.random.fold_in(jax.random.fold_in(stream_key, 6), position), (shards_of,), jnp.float32, least / len(pieces), high / len(pieces))
        return jnp.repeat(jnp.exp(heights), dims[position] // shards_of).reshape((-1,) + (1,) * (len(dims) - position - 1))

    factor_of = one(*pieces[0])
    for cut in pieces[1:]:
        factor_of = factor_of * one(*cut)
    return factor_of


def gaussian(stream_key, shape, scale, bound, shards=(), kind=jnp.bfloat16):
    gain = steps_of(stream_key, shape, shards, -0.22, 0.18) if shards else 1.0
    result = jax.random.normal(stream_key, shape, jnp.float32) * scale * gain
    return jnp.minimum(jnp.maximum(result, -bound), bound).astype(kind)


def setup_inputs(seed: int = 0) -> dict:
    arg_keys = jax.random.split(jax.random.key(seed), 15)
    return {
        "fine_now": gaussian(arg_keys[0], (3, NXF, NYF, NZ), 1.0, 6.0, ((1, 48), (2, 16)), jnp.float32),
        "fine_prev": gaussian(arg_keys[1], (3, NXF, NYF, NZ), 1.0, 6.0, ((1, 48), (2, 16)), jnp.float32),
        "coarse_now": gaussian(arg_keys[2], (3, NXC, NYC, NZ), 1.0, 6.0, ((1, 48), (2, 16)), jnp.float32),
        "coarse_prev": gaussian(arg_keys[3], (3, NXC, NYC, NZ), 1.0, 6.0, ((1, 48), (2, 16)), jnp.float32),
        "fine_rho": jnp.clip(jnp.exp(math.log(3.0) - 1.0986123 * jax.random.uniform(arg_keys[4], (NXF, NYF, NZ), jnp.float32) ** steps_of(arg_keys[4], (NXF, NYF, NZ), ((0, 48), (1, 16)), -0.2, 0.2)), 1.0, 3.0),
        "fine_mu": jnp.clip(jnp.exp(math.log(1.5) - 1.60943787 * jax.random.uniform(arg_keys[5], (NXF, NYF, NZ), jnp.float32) ** steps_of(arg_keys[5], (NXF, NYF, NZ), ((0, 48), (1, 16)), -0.2, 0.2)), 0.3, 1.5),
        "fine_lam": jnp.clip(jnp.exp(math.log(1.5) - 1.60943787 * jax.random.uniform(arg_keys[6], (NXF, NYF, NZ), jnp.float32) ** steps_of(arg_keys[6], (NXF, NYF, NZ), ((0, 48), (1, 16)), -0.2, 0.2)), 0.3, 1.5),
        "fine_metric": jnp.clip(jnp.exp(math.log(2.0) - 1.3862944 * jax.random.uniform(arg_keys[7], (NXF, NYF, NZ), jnp.float32) ** steps_of(arg_keys[7], (NXF, NYF, NZ), ((0, 48), (1, 16)), -0.2, 0.2)), 0.5, 2.0),
        "coarse_rho": jnp.clip(jnp.exp(math.log(3.0) - 1.0986123 * jax.random.uniform(arg_keys[8], (NXC, NYC, NZ), jnp.float32) ** steps_of(arg_keys[8], (NXC, NYC, NZ), ((0, 48), (1, 16)), -0.2, 0.2)), 1.0, 3.0),
        "coarse_mu": jnp.clip(jnp.exp(math.log(1.5) - 1.60943787 * jax.random.uniform(arg_keys[9], (NXC, NYC, NZ), jnp.float32) ** steps_of(arg_keys[9], (NXC, NYC, NZ), ((0, 48), (1, 16)), -0.2, 0.2)), 0.3, 1.5),
        "coarse_lam": jnp.clip(jnp.exp(math.log(1.5) - 1.60943787 * jax.random.uniform(arg_keys[10], (NXC, NYC, NZ), jnp.float32) ** steps_of(arg_keys[10], (NXC, NYC, NZ), ((0, 48), (1, 16)), -0.2, 0.2)), 0.3, 1.5),
        "coarse_metric": jnp.clip(jnp.exp(math.log(2.0) - 1.3862944 * jax.random.uniform(arg_keys[11], (NXC, NYC, NZ), jnp.float32) ** steps_of(arg_keys[11], (NXC, NYC, NZ), ((0, 48), (1, 16)), -0.2, 0.2)), 0.5, 2.0),
        "couple_index": draw_couple_index(jax.random.fold_in(arg_keys[14], 71), 0),
        "couple_weight": jnp.clip(0.125 * jax.random.uniform(arg_keys[13], (NXF, NYF, COUPLE), jnp.float32) ** steps_of(arg_keys[13], (NXF, NYF, COUPLE), ((0, 48), (1, 16)), -0.2, 0.2), 0.0, 0.125),
    }


time_step = 0.25


def vertical_table(layers):
    matrix = np.zeros((layers, layers))
    for centre in range(2, layers - 2):
        matrix[centre, centre - 2] = 1.0 / 12.0
        matrix[centre, centre - 1] = -8.0 / 12.0
        matrix[centre, centre + 1] = 8.0 / 12.0
        matrix[centre, centre + 2] = -1.0 / 12.0
    matrix[0, 0] = -1.5
    matrix[0, 1] = 2.0
    matrix[0, 2] = -0.5
    matrix[1, 0] = -0.5
    matrix[1, 2] = 0.5
    matrix[layers - 2, layers - 3] = -0.5
    matrix[layers - 2, layers - 1] = 0.5
    matrix[layers - 1, layers - 3] = 0.5
    matrix[layers - 1, layers - 2] = -2.0
    matrix[layers - 1, layers - 1] = 1.5
    return jnp.asarray(matrix.T, jnp.float32)


def vertical(values, depth_table):
    return jnp.matmul(values, depth_table, precision=lax.Precision.HIGHEST)


def stencil_sum(source, along, weights):
    extent = source.shape[along] - 4
    running = None
    for offset in range(5):
        if weights[offset] != 0.0:
            contrib = weights[offset] * lax.slice_in_dim(source, offset, offset + extent, axis=along)
            running = contrib if running is None else running + contrib
    return running


def advance(widened, lifted, present, earlier, metric, density, shear, lame_first, depth_table, spacing):
    first_taps = [c / (12.0 * spacing) for c in (1.0, -8.0, 0.0, 8.0, -1.0)]
    second_taps = [c / (12.0 * spacing * spacing) for c in (-1.0, 16.0, -30.0, 16.0, -1.0)]
    curve_x = stencil_sum(widened[:, :, 2:-2], 1, second_taps)
    curve_y = stencil_sum(widened[:, 2:-2], 2, second_taps)
    cross_one = stencil_sum(stencil_sum(widened[1], 1, first_taps), 0, first_taps)
    cross_zero = stencil_sum(stencil_sum(widened[0], 0, first_taps), 1, first_taps)
    lifted_dx = stencil_sum(lifted[:, 2:-2], 0, first_taps)
    lifted_dy = stencil_sum(lifted[2:-2], 1, first_taps)
    along_x = stencil_sum(widened[0, :, 2:-2], 0, first_taps)
    along_y = stencil_sum(widened[1, 2:-2], 1, first_taps)
    lifted_in = lifted[2:-2, 2:-2]
    slopes = metric * vertical(present[0:2], depth_table)
    stacked = jnp.concatenate([slopes, lifted_in[None], (along_x + along_y + lifted_in)[None]], 0)
    bent_terms = metric * vertical(stacked, depth_table)
    laplace = curve_x + curve_y + bent_terms[0:3]
    grad_div = jnp.stack([curve_x[0] + cross_one + lifted_dx, cross_zero + curve_y[1] + lifted_dy, bent_terms[3]], 0)
    acceleration = (shear * laplace + (lame_first + shear) * grad_div) / density
    return 2.0 * present - earlier + (time_step * time_step) * acceleration


def interpolate(flat_plane, targets, mixing):
    return jnp.sum(flat_plane[:, targets] * mixing, axis=-1)


def reference(fine_now, fine_prev, coarse_now, coarse_prev, fine_rho, fine_mu, fine_lam, fine_metric, coarse_rho, coarse_mu, coarse_lam, coarse_metric, couple_index, couple_weight):
    depth_table = vertical_table(NZ)
    margin_pad = ((2, 2), (2, 2), (0, 0))
    fine_edge = jnp.pad(fine_metric, margin_pad)
    coarse_edge = jnp.pad(coarse_metric, margin_pad)
    row_start = jnp.arange(NXF, dtype=jnp.int32) // CXF * CXC
    col_start = jnp.arange(NYF, dtype=jnp.int32) // CYF * CYC
    global_row = row_start[:, None, None] + couple_index // (CYC + 4)
    global_col = col_start[None, :, None] + couple_index % (CYC + 4)
    flat_index = (global_row * (NYC + 4) + global_col).astype(jnp.int32)
    for marching in range(2):
        fine_wide = jnp.pad(fine_now, ((0, 0),) + margin_pad)
        fine_lift = fine_edge * vertical(fine_wide[2], depth_table)
        fine_next = advance(fine_wide, fine_lift, fine_now, fine_prev, fine_metric, fine_rho, fine_mu, fine_lam, depth_table, 1.0)
        coarse_wide = jnp.pad(coarse_now, ((0, 0),) + margin_pad)
        coarse_lift = coarse_edge * vertical(coarse_wide[2], depth_table)
        coarse_next = advance(coarse_wide, coarse_lift, coarse_now, coarse_prev, coarse_metric, coarse_rho, coarse_mu, coarse_lam, depth_table, 2.0)
        top_plane = jnp.pad(coarse_next[:, :, :, NZ - 1], ((0, 0), (2, 2), (2, 2)))
        interface_values = interpolate(top_plane.reshape(3, -1), flat_index, couple_weight)
        fine_next = fine_next.at[:, :, :, 0].set(interface_values)
        fine_prev, fine_now = fine_now, fine_next
        coarse_prev, coarse_now = coarse_now, coarse_next
    return (fine_now, coarse_now)
```

```python
import jax
import jax.numpy as jnp
import numpy as np
from jax import lax
from jax.experimental import pallas as pl
from jax.experimental.pallas import tpu as pltpu
from jax.sharding import PartitionSpec as P


DT2 = 0.0625
NL = 128
Y_ROWS, A_ROWS, C_ROWS, R_ROWS = 400, 736, 528, 160
YB, YC, YD = 128, 224, 320
AB, AC, AD = 256, 448, 576
CB_, CC, CS = 64, 88, 264
F32 = jnp.float32


def vertical_matrix():
    m = np.zeros((NL, NL))
    for k in range(2, NL - 2):
        m[k, k - 2], m[k, k - 1], m[k, k + 1], m[k, k + 2] = 1, -8, 8, -1
    m[0, 0:3] = -18, 24, -6
    m[1, 0], m[1, 2] = -6, 6
    m[NL - 2, NL - 3], m[NL - 2, NL - 1] = -6, 6
    m[NL - 1, NL - 3 :] = 6, -24, 18
    return np.concatenate([m.T, m.T], 0)


def odd(axis):
    return lax.axis_index(axis) % 2


def rows(v):
    return v.reshape(-1, NL)


def pack_own(fn, fp, fr, fm, fl, fj, cn, cp, cr, cm, cl, cj, ix, wt, yn, yf, an, af, fo, co):
    inv = DT2 / fr[...]
    fo[0] = fm[...] * inv
    fo[1] = (fl[...] + fm[...]) * inv
    inv = DT2 / cr[...]
    co[0] = cm[...] * inv
    co[1] = (cl[...] + cm[...]) * inv
    lane = lax.broadcasted_iota(jnp.int32, (128, NL), 1)
    index = ix[...].reshape(128, 16)
    weight = wt[...].reshape(128, 16)
    slot = index + 2 + 4 * ((index * 171) >> 11)
    acc = jnp.zeros((128, NL), F32)
    for k in range(16):
        acc = acc + jnp.where(lane == slot[:, k : k + 1], weight[:, k : k + 1], 0.0)
    fo[2] = acc.reshape(8, 16, NL)

    def fine_u(i, x):
        return fn[i, x] if i < 3 else fj[x] * (1.0 / 12.0)

    def coarse_u(i, x):
        return cn[i, x] if i < 3 else cj[x] * (1.0 / 12.0)

    def y_edge(out, low):
        for i in range(4):
            for x in range(8):
                v = fine_u(i, x)
                out[i * 32 + x * 4 : i * 32 + x * 4 + 4] = v[0:4] if low else v[12:16]
        for i in range(6):
            for x in range(8):
                v = fp[i, x] if i < 3 else fo[i - 3, x]
                v = v[0:2] if low else v[14:16]
                if i == 5:
                    v = pltpu.roll(v, 8 if low else 120, 1)
                out[YB + i * 16 + x * 2 : YB + i * 16 + x * 2 + 2] = v
        for i in range(4):
            for x in range(4):
                v = coarse_u(i, x)
                out[YC + i * 24 + x * 6 : YC + i * 24 + x * 6 + 6] = v[0:6] if low else v[2:8]
        for i in range(5):
            for x in range(4):
                v = cp[i, x] if i < 3 else co[i - 3, x]
                out[YD + i * 16 + x * 4 : YD + i * 16 + x * 4 + 4] = v[0:4] if low else v[4:8]

    def x_edge(out, low):
        x0 = 0 if low else 4
        for i in range(4):
            v = fn[i, x0 : x0 + 4] if i < 3 else fj[x0 : x0 + 4] * (1.0 / 12.0)
            out[i * 64 : i * 64 + 64] = rows(v)
        x0 = 0 if low else 6
        for i in range(6):
            v = fp[i, x0 : x0 + 2] if i < 3 else fo[i - 3, x0 : x0 + 2]
            out[AB + i * 32 : AB + i * 32 + 32] = rows(v)
        for i in range(4):
            v = cn[i] if i < 3 else cj[...] * (1.0 / 12.0)
            out[AC + i * 32 : AC + i * 32 + 32] = rows(v)
        for i in range(5):
            v = cp[i] if i < 3 else co[i - 3]
            out[AD + i * 32 : AD + i * 32 + 32] = rows(v)

    ox, oy = odd("gx"), odd("gy")

    @pl.when(oy == 0)
    def _():
        y_edge(yn, False)
        y_edge(yf, True)

    @pl.when(oy == 1)
    def _():
        y_edge(yn, True)
        y_edge(yf, False)

    @pl.when(ox == 0)
    def _():
        x_edge(an, False)
        x_edge(af, True)

    @pl.when(ox == 1)
    def _():
        x_edge(an, True)
        x_edge(af, False)


def pack_corner(src, out, base, low):
    for i in range(4):
        o = i * 32 + (0 if low else 16)
        out[base + i * 16 : base + i * 16 + 16] = src[o : o + 16]
    for i in range(6):
        o = YB + i * 16 + (0 if low else 12)
        out[base + CB_ + i * 4 : base + CB_ + i * 4 + 4] = src[o : o + 4]
    out[base + CC : base + CS] = src[YC:Y_ROWS]


def pack_near(rn, rf, out):
    ox = odd("gx")

    @pl.when(ox == 0)
    def _():
        pack_corner(rn, out, 0, False)
        pack_corner(rf, out, CS, False)

    @pl.when(ox == 1)
    def _():
        pack_corner(rn, out, 0, True)
        pack_corner(rf, out, CS, True)


def pack_relay(a, c, out, base, x0):
    for i in range(4):
        out[base + i * 16 : base + i * 16 + 16] = a[AC + i * 32 + x0 * 8 : AC + i * 32 + x0 * 8 + 16]
    for s in range(2):
        for i in range(4):
            o = s * CS + CC + i * 24 + x0 * 6
            t = base + 64 + s * 48 + i * 12
            out[t : t + 12] = c[o : o + 12]


def pack_far(rn, rf, a, c, out):
    ox = odd("gx")

    @pl.when(ox == 0)
    def _():
        pack_corner(rn, out, 0, True)
        pack_corner(rf, out, CS, True)
        pack_relay(a, c.at[1], out, C_ROWS, 0)

    @pl.when(ox == 1)
    def _():
        pack_corner(rn, out, 0, False)
        pack_corner(rf, out, CS, False)
        pack_relay(a, c.at[0], out, C_ROWS, 2)


def pack_second(a, c, out):
    ox = odd("gx")

    @pl.when(ox == 0)
    def _():
        pack_relay(a, c, out, 0, 2)

    @pl.when(ox == 1)
    def _():
        pack_relay(a, c, out, 0, 0)


def vertical(v, table):
    hi = v.astype(jnp.bfloat16)
    lo = (v - hi.astype(F32)).astype(jnp.bfloat16)
    return jnp.dot(jnp.concatenate([hi, lo], 1), table, preferred_element_type=F32)


def first(m2, m1, p1, p2, scale):
    return (m2 - p2) * (scale / 12.0) + (p1 - m1) * (scale * 8.0 / 12.0)


def second(m2, m1, c, p1, p2, scale):
    return (m1 + p1) * (scale * 16.0 / 12.0) - (m2 + p2) * (scale / 12.0) - c * (scale * 2.5)


def shifted(v):
    return [pltpu.roll(v, s % 24, 0) for s in (2, 1, -1, -2)]


def advance(n, u, j, prev, a, b, lift, work, table, spacing, store):
    s1, s2 = 1.0 / spacing, 1.0 / (spacing * spacing)
    half = (n + 4) // 2
    for x0 in (0, half):
        g = vertical(rows(u(2, x0, half)), table)
        lift[x0 : x0 + half] = (rows(j(x0, half)) * g).reshape(half, 24, NL)
    for c in range(2):
        g = vertical(rows(u(c, 2, n)), table)
        work[c, 0:n] = (rows(j(2, n)) * g).reshape(n, 24, NL)
    for x in range(n):
        f0 = [u(0, x + k, None) for k in (0, 1, 3, 4)]
        m2, m1, p1, p2 = shifted(u(1, x + 2, None))
        work[3, x] = first(*f0, s1) + first(m2, m1, p1, p2, s1) + lift[x + 2]
    work[2, 0:n] = lift[2 : 2 + n]
    for c in range(4):
        g = vertical(rows(work[c, 0:n]), table)
        work[c, 0:n] = (rows(j(2, n)) * g).reshape(n, 24, NL)
    for x in range(n):
        col = [[u(c, x + k, None) for k in range(5)] for c in range(3)]
        lf = [lift[x + k] for k in range(5)]
        sh = [shifted(col[c][2]) for c in range(3)]
        xx = [second(*col[c], s2) for c in range(3)]
        yy = [second(sh[c][0], sh[c][1], col[c][2], sh[c][2], sh[c][3], s2) for c in range(3)]
        dx0 = first(col[0][0], col[0][1], col[0][3], col[0][4], s1)
        dx1 = first(col[1][0], col[1][1], col[1][3], col[1][4], s1)
        g0 = xx[0] + first(*shifted(dx1), s1) + first(lf[0], lf[1], lf[3], lf[4], s1)
        g1 = yy[1] + first(*shifted(dx0), s1) + first(*shifted(lf[2]), s1)
        g2 = work[3, x]
        av, bv = a(x), b(x)
        for c, g in enumerate((g0, g1, g2)):
            lap = xx[c] + yy[c] + work[c, x]
            store(c, x, 2.0 * col[c][2] - prev(c, x) + av * lap + bv * g)


def main(
    fn, fp, fj, fo, cn, cp, cj, co, yn, yf, an, af, gn, bf, g2, table_ref,
    fine_out, coarse_out, fe, fb, ce, cb, f1, c1, lift, work, tops, face,
):
    ox, oy = odd("gx"), odd("gy")
    ce[:, :, 0:8] = jnp.zeros((4, 16, 8, NL), F32)
    ce[:, :, 16:24] = jnp.zeros((4, 16, 8, NL), F32)
    cb[:, :, 0:8] = jnp.zeros((5, 12, 8, NL), F32)
    cb[:, :, 16:24] = jnp.zeros((5, 12, 8, NL), F32)
    fb[:, :, 0:8] = jnp.zeros((6, 12, 8, NL), F32)
    fb[:, :, 16:24] = jnp.zeros((6, 12, 8, NL), F32)
    for x in range(8):
        for i in range(3):
            fe[i, 4 + x, 4:20] = fn[i, x]
            fb[i, 2 + x, 4:20] = fp[i, x]
            fb[3 + i, 2 + x, 4:20] = fo[i, x]
        fe[3, 4 + x, 4:20] = fj[x] * (1.0 / 12.0)
    for x in range(4):
        for i in range(3):
            ce[i, 6 + x, 8:16] = cn[i, x]
            cb[i, 4 + x, 8:16] = cp[i, x]
        for i in range(2):
            cb[3 + i, 4 + x, 8:16] = co[i, x]
        ce[3, 6 + x, 8:16] = cj[x] * (1.0 / 12.0)
    near, far = ox == 0, ox == 1
    other = 1 - ox
    sides = (
        (an, gn.at[other], g2.at[other], near, 0),
        (af, bf, bf, far, C_ROWS),
    )
    for a, c, r, high, base in sides:
        f4 = jnp.where(high, 12, 0)
        f2 = jnp.where(high, 10, 0)
        c4 = jnp.where(high, 10, 2)
        c2 = jnp.where(high, 14, 0)
        b4 = jnp.where(high, 8, 0)
        for i in range(4):
            for x in range(4):
                fe[i, f4 + x, 4:20] = a[i * 64 + x * 16 : i * 64 + x * 16 + 16]
                ce[i, c4 + x, 8:16] = a[AC + i * 32 + x * 8 : AC + i * 32 + x * 8 + 8]
            for x in range(2):
                ce[i, c2 + x, 8:16] = r[base + i * 16 + x * 8 : base + i * 16 + x * 8 + 8]
        for i in range(6):
            for x in range(2):
                fb[i, f2 + x, 4:20] = a[AB + i * 32 + x * 16 : AB + i * 32 + x * 16 + 16]
        for i in range(5):
            for x in range(4):
                cb[i, b4 + x, 8:16] = a[AD + i * 32 + x * 8 : AD + i * 32 + x * 8 + 8]

    def y_side(src, s, high):
        t4, t2, t6, t3 = (20, 20, 16, 16) if high else (0, 2, 2, 4)
        for i in range(4):
            for x in range(8):
                fe[i, 4 + x, t4 : t4 + 4] = src[i * 32 + x * 4 : i * 32 + x * 4 + 4]
            for x in range(4):
                o = YC + i * 24 + x * 6
                ce[i, 6 + x, t6 : t6 + 6] = src[o : o + 6]
        for i in range(6):
            for x in range(8):
                o = YB + i * 16 + x * 2
                fb[i, 2 + x, t2 : t2 + 2] = src[o : o + 2]
        for i in range(5):
            for x in range(4):
                o = YD + i * 16 + x * 4
                cb[i, 4 + x, t3 : t3 + 4] = src[o : o + 4]
        for a, c, r, hx, base in sides:
            f4 = jnp.where(hx, 12, 0)
            f2 = jnp.where(hx, 10, 0)
            c4 = jnp.where(hx, 10, 2)
            c2 = jnp.where(hx, 14, 0)
            b4 = jnp.where(hx, 8, 0)
            q = s * CS
            for i in range(4):
                for x in range(4):
                    o = q + i * 16 + x * 4
                    fe[i, f4 + x, t4 : t4 + 4] = c[o : o + 4]
                    o = q + CC + i * 24 + x * 6
                    ce[i, c4 + x, t6 : t6 + 6] = c[o : o + 6]
                for x in range(2):
                    o = base + 64 + s * 48 + i * 12 + x * 6
                    ce[i, c2 + x, t6 : t6 + 6] = r[o : o + 6]
            for i in range(6):
                for x in range(2):
                    o = q + CB_ + i * 4 + x * 2
                    fb[i, f2 + x, t2 : t2 + 2] = c[o : o + 2]
            for i in range(5):
                for x in range(4):
                    o = q + CC + 96 + i * 16 + x * 4
                    cb[i, b4 + x, t3 : t3 + 4] = c[o : o + 4]

    @pl.when(oy == 0)
    def _():
        y_side(yn, 0, True)
        y_side(yf, 1, False)

    @pl.when(oy == 1)
    def _():
        y_side(yn, 0, False)
        y_side(yf, 1, True)

    table = table_ref[...]
    lane = lax.broadcasted_iota(jnp.int32, (24, NL), 1)

    def view(ref, i, off):
        def get(x, count):
            return ref[i, x + off] if count is None else ref[i, x + off : x + off + count]

        return get

    def views(ref, off):
        def get(i, x, count=None):
            return view(ref, i, off)(x, count)

        return get

    def gather_top(src, n, t0):
        for x in range(n):
            v = jnp.where(lane == 0, pltpu.roll(src[0, x], 1, 1), 0.0)
            v = jnp.where(lane == 1, pltpu.roll(src[1, x], 2, 1), v)
            v = jnp.where(lane == 2, pltpu.roll(src[2, x], 3, 1), v)
            tops[t0 + x] = v[4:20]

    def mixed(x0, n, t0):
        w = rows(fb[5, x0 : x0 + n])
        plane = tops[t0 : t0 + 8].reshape(128, NL)
        return jnp.dot(w, plane, precision=lax.Precision.HIGHEST, preferred_element_type=F32).reshape(n, 24, NL)

    def with_face(c, x, v):
        return jnp.where(lane == 0, pltpu.roll(face[x], (NL - c) % NL, 1), v)

    tops[0:2] = jnp.zeros((2, 16, NL), F32)
    tops[14:16] = jnp.zeros((2, 16, NL), F32)

    def store_c1(c, x, v):
        c1[c, x] = v

    advance(12, views(ce, 0), view(ce, 3, 0), views(cb, 0), view_row(cb, 3, 0), view_row(cb, 4, 0),
            lift, work, table, 2.0, store_c1)
    gather_top(c1, 12, 2)
    face[0:2] = mixed(0, 2, 0)
    face[2:10] = mixed(2, 8, 4)
    face[10:12] = mixed(10, 2, 8)

    def store_f1(c, x, v):
        f1[c, x] = with_face(c, x, v)

    advance(12, views(fe, 0), view(fe, 3, 0), views(fb, 0), view_row(fb, 3, 0), view_row(fb, 4, 0),
            lift, work, table, 1.0, store_f1)

    def store_c2(c, x, v):
        cb[c, x] = v
        if 2 <= x < 6:
            coarse_out[c, x - 2] = v[8:16]

    advance(8, views(c1, 0), view(ce, 3, 2), views(ce, 4), view_row(cb, 3, 2), view_row(cb, 4, 2),
            lift, work, table, 2.0, store_c2)
    gather_top(cb, 8, 4)
    face[0:8] = mixed(2, 8, 4)

    def store_f2(c, x, v):
        fine_out[c, x] = with_face(c, x, v)[4:20]

    advance(8, views(f1, 0), view(fe, 3, 2), views(fe, 4), view_row(fb, 3, 2), view_row(fb, 4, 2),
            lift, work, table, 1.0, store_f2)


def view_row(ref, i, off):
    def get(x):
        return ref[i, x + off]

    return get


def pairs(size, start):
    out = []
    for i in range(start, size - 1, 2):
        out += [(i, i + 1), (i + 1, i)]
    return out


INTERPRET = False


def call(body, shapes, *operands, scratch=()):
    return pl.pallas_call(
        body,
        out_shape=[jax.ShapeDtypeStruct(s, F32) for s in shapes],
        scratch_shapes=[pltpu.VMEM(s, F32) for s in scratch],
        compiler_params=pltpu.CompilerParams(vmem_limit_bytes=56 << 20),
        interpret=INTERPRET,
    )(*operands)


def on_device(
    fine_now, fine_prev, coarse_now, coarse_prev, fine_rho, fine_mu, fine_lam, fine_metric,
    coarse_rho, coarse_mu, coarse_lam, coarse_metric, couple_index, couple_weight,
):
    gx, gy = lax.axis_size("gx"), lax.axis_size("gy")
    near_x, far_x, near_y, far_y = pairs(gx, 0), pairs(gx, 1), pairs(gy, 0), pairs(gy, 1)
    groups = [[i, i + 1] for i in range(0, gx, 2)]
    table = jnp.asarray(vertical_matrix(), jnp.bfloat16)

    yn, yf, an, af, fo, co = call(
        pack_own,
        [(Y_ROWS, NL)] * 2 + [(A_ROWS, NL)] * 2 + [(3, 8, 16, NL), (2, 4, 8, NL)],
        fine_now, fine_prev, fine_rho, fine_mu, fine_lam, fine_metric,
        coarse_now, coarse_prev, coarse_rho, coarse_mu, coarse_lam, coarse_metric,
        couple_index, couple_weight,
    )
    yn = lax.ppermute(yn, "gy", near_y)
    yf = lax.ppermute(yf, "gy", far_y)
    af = lax.ppermute(af, "gx", far_x)
    an = lax.ppermute(an, "gx", near_x)
    (cn,) = call(pack_near, [(C_ROWS, NL)], yn, yf)
    gn = lax.all_gather(cn, "gx", axis_index_groups=groups)
    (bf,) = call(pack_far, [(C_ROWS + R_ROWS, NL)], yn, yf, an, gn)
    bf = lax.ppermute(bf, "gx", far_x)
    (r2,) = call(pack_second, [(R_ROWS, NL)], af, bf)
    g2 = lax.all_gather(r2, "gx", axis_index_groups=groups)
    return tuple(
        call(
            main,
            [(3, 8, 16, NL), (3, 4, 8, NL)],
            fine_now, fine_prev, fine_metric, fo, coarse_now, coarse_prev, coarse_metric, co,
            yn, yf, an, af, gn, bf, g2, table,
            scratch=[
                (4, 16, 24, NL), (6, 12, 24, NL), (4, 16, 24, NL), (5, 12, 24, NL),
                (3, 12, 24, NL), (3, 12, 24, NL), (16, 24, NL), (4, 12, 24, NL), (16, 16, NL), (12, 24, NL),
            ],
        )
    )


def solution(mesh):
    wide, flat = P(None, "gx", "gy", None), P("gx", "gy", None)
    return jax.shard_map(
        on_device,
        mesh=mesh,
        in_specs=(wide,) * 4 + (flat,) * 10,
        out_specs=(wide, wide),
        check_vma=False,
    )
```

```python
import jax
import jax.numpy as jnp
import numpy as np
from jax import lax
from jax.experimental import pallas as pl
from jax.experimental.pallas import tpu as pltpu
from jax.sharding import PartitionSpec as P


DT2 = 0.0625
NL = 128
Y_ROWS, A_ROWS, C_ROWS, R_ROWS, O_ROWS = 400, 736, 528, 160, 64
YB, YC, YD = 128, 224, 320
AB, AC, AD = 256, 448, 576
CB_, CC, CS = 64, 88, 264
F32 = jnp.float32


def vertical_matrix():
    m = np.zeros((NL, NL))
    for k in range(2, NL - 2):
        m[k, k - 2], m[k, k - 1], m[k, k + 1], m[k, k + 2] = 1, -8, 8, -1
    m[0, 0:3] = -18, 24, -6
    m[1, 0], m[1, 2] = -6, 6
    m[NL - 2, NL - 3], m[NL - 2, NL - 1] = -6, 6
    m[NL - 1, NL - 3 :] = 6, -24, 18
    return np.concatenate([m.T, m.T], 0)


def odd(axis):
    return lax.axis_index(axis) % 2


def rows(v):
    return v.reshape(-1, NL)


def y_edge(out, low, fn, fp, fj, fo, cn, cp, cj, co):
    for i in range(4):
        for x in range(8):
            v = fn[i, x] if i < 3 else fj[x] * (1.0 / 12.0)
            out[i * 32 + x * 4 : i * 32 + x * 4 + 4] = v[0:4] if low else v[12:16]
    for i in range(6):
        for x in range(8):
            v = fp[i, x] if i < 3 else fo[i - 3, x]
            v = v[0:2] if low else v[14:16]
            if i == 5:
                v = pltpu.roll(v, 8 if low else 120, 1)
            out[YB + i * 16 + x * 2 : YB + i * 16 + x * 2 + 2] = v
    for i in range(4):
        for x in range(4):
            v = cn[i, x] if i < 3 else cj[x] * (1.0 / 12.0)
            out[YC + i * 24 + x * 6 : YC + i * 24 + x * 6 + 6] = v[0:6] if low else v[2:8]
    for i in range(5):
        for x in range(4):
            v = cp[i, x] if i < 3 else co[i - 3, x]
            out[YD + i * 16 + x * 4 : YD + i * 16 + x * 4 + 4] = v[0:4] if low else v[4:8]


def pack_y(fn, fp, fr, fm, fl, fj, cn, cp, cr, cm, cl, cj, ix, wt, yf, yn, ro, fo, co):
    inv = DT2 / fr[...]
    fo[0] = fm[...] * inv
    fo[1] = (fl[...] + fm[...]) * inv
    inv = DT2 / cr[...]
    co[0] = cm[...] * inv
    co[1] = (cl[...] + cm[...]) * inv
    lane = lax.broadcasted_iota(jnp.int32, (128, NL), 1)
    index = ix[...].reshape(128, 16)
    weight = wt[...].reshape(128, 16)
    slot = index + 2 + 4 * ((index * 171) >> 11)
    acc = jnp.zeros((128, NL), F32)
    for k in range(16):
        acc = acc + jnp.where(lane == slot[:, k : k + 1], weight[:, k : k + 1], 0.0)
    fo[2] = acc.reshape(8, 16, NL)
    oy = odd("gy")

    @pl.when(oy == 0)
    def _():
        y_edge(yf, True, fn, fp, fj, fo, cn, cp, cj, co)
        y_edge(yn, False, fn, fp, fj, fo, cn, cp, cj, co)

    @pl.when(oy == 1)
    def _():
        y_edge(yf, False, fn, fp, fj, fo, cn, cp, cj, co)
        y_edge(yn, True, fn, fp, fj, fo, cn, cp, cj, co)
    yf[Y_ROWS:] = jnp.zeros((8, NL), F32)
    x0 = 2 - 2 * odd("gx")
    for i in range(4):
        v = cn[i, pl.ds(x0, 2)] if i < 3 else cj[pl.ds(x0, 2)] * (1.0 / 12.0)
        ro[i * 16 : i * 16 + 16] = rows(v)


def pack_x(fn, fp, fj, fo, cn, cp, cj, co, an, af):
    def x_edge(out, low):
        x0 = 0 if low else 4
        for i in range(4):
            v = fn[i, x0 : x0 + 4] if i < 3 else fj[x0 : x0 + 4] * (1.0 / 12.0)
            out[i * 64 : i * 64 + 64] = rows(v)
        x0 = 0 if low else 6
        for i in range(6):
            v = fp[i, x0 : x0 + 2] if i < 3 else fo[i - 3, x0 : x0 + 2]
            out[AB + i * 32 : AB + i * 32 + 32] = rows(v)
        for i in range(4):
            v = cn[i] if i < 3 else cj[...] * (1.0 / 12.0)
            out[AC + i * 32 : AC + i * 32 + 32] = rows(v)
        for i in range(5):
            v = cp[i] if i < 3 else co[i - 3]
            out[AD + i * 32 : AD + i * 32 + 32] = rows(v)

    ox = odd("gx")

    @pl.when(ox == 0)
    def _():
        x_edge(an, False)
        x_edge(af, True)

    @pl.when(ox == 1)
    def _():
        x_edge(an, True)
        x_edge(af, False)


def pack_corner(src, out, base, low):
    for i in range(4):
        o = i * 32 + (0 if low else 16)
        out[base + i * 16 : base + i * 16 + 16] = src[o : o + 16]
    for i in range(6):
        o = YB + i * 16 + (0 if low else 12)
        out[base + CB_ + i * 4 : base + CB_ + i * 4 + 4] = src[o : o + 4]
    out[base + CC : base + CS] = src[YC:Y_ROWS]


def pack_near(rn, rf, ro, out):
    out[C_ROWS : C_ROWS + O_ROWS] = ro[...]
    ox = odd("gx")

    @pl.when(ox == 0)
    def _():
        pack_corner(rn, out, 0, False)
        pack_corner(rf, out, CS, False)

    @pl.when(ox == 1)
    def _():
        pack_corner(rn, out, 0, True)
        pack_corner(rf, out, CS, True)


def pack_relay(a, c, out, base, x0):
    for i in range(4):
        o = C_ROWS + i * 16 if a is None else AC + i * 32 + x0 * 8
        out[base + i * 16 : base + i * 16 + 16] = (c if a is None else a)[o : o + 16]
    for s in range(2):
        for i in range(4):
            o = s * CS + CC + i * 24 + x0 * 6
            t = base + 64 + s * 48 + i * 12
            out[t : t + 12] = c[o : o + 12]


def pack_far(rn, rf, c, out):
    ox = odd("gx")

    @pl.when(ox == 0)
    def _():
        pack_corner(rn, out, 0, True)
        pack_corner(rf, out, CS, True)
        pack_relay(None, c.at[1], out, C_ROWS, 0)

    @pl.when(ox == 1)
    def _():
        pack_corner(rn, out, 0, False)
        pack_corner(rf, out, CS, False)
        pack_relay(None, c.at[0], out, C_ROWS, 2)


def pack_second(a, c, out):
    ox = odd("gx")

    @pl.when(ox == 0)
    def _():
        pack_relay(a, c, out, 0, 2)

    @pl.when(ox == 1)
    def _():
        pack_relay(a, c, out, 0, 0)


def vertical(v, table):
    hi = v.astype(jnp.bfloat16)
    lo = (v - hi.astype(F32)).astype(jnp.bfloat16)
    return jnp.dot(jnp.concatenate([hi, lo], 1), table, preferred_element_type=F32)


def first(m2, m1, p1, p2, scale):
    return (m2 - p2) * (scale / 12.0) + (p1 - m1) * (scale * 8.0 / 12.0)


def second(m2, m1, c, p1, p2, scale):
    return (m1 + p1) * (scale * 16.0 / 12.0) - (m2 + p2) * (scale / 12.0) - c * (scale * 2.5)


def shifted(v):
    return [pltpu.roll(v, s % 24, 0) for s in (2, 1, -1, -2)]


def advance(n, u, j, prev, a, b, lift, work, table, spacing, store):
    s1, s2 = 1.0 / spacing, 1.0 / (spacing * spacing)
    half = (n + 4) // 2
    for x0 in (0, half):
        g = vertical(rows(u(2, x0, half)), table)
        lift[x0 : x0 + half] = (rows(j(x0, half)) * g).reshape(half, 24, NL)
    for c in range(2):
        g = vertical(rows(u(c, 2, n)), table)
        work[c, 0:n] = (rows(j(2, n)) * g).reshape(n, 24, NL)
    for x in range(n):
        f0 = [u(0, x + k, None) for k in (0, 1, 3, 4)]
        m2, m1, p1, p2 = shifted(u(1, x + 2, None))
        work[3, x] = first(*f0, s1) + first(m2, m1, p1, p2, s1) + lift[x + 2]
    work[2, 0:n] = lift[2 : 2 + n]
    for c in range(4):
        g = vertical(rows(work[c, 0:n]), table)
        work[c, 0:n] = (rows(j(2, n)) * g).reshape(n, 24, NL)
    for x in range(n):
        col = [[u(c, x + k, None) for k in range(5)] for c in range(3)]
        lf = [lift[x + k] for k in range(5)]
        sh = [shifted(col[c][2]) for c in range(3)]
        xx = [second(*col[c], s2) for c in range(3)]
        yy = [second(sh[c][0], sh[c][1], col[c][2], sh[c][2], sh[c][3], s2) for c in range(3)]
        dx0 = first(col[0][0], col[0][1], col[0][3], col[0][4], s1)
        dx1 = first(col[1][0], col[1][1], col[1][3], col[1][4], s1)
        g0 = xx[0] + first(*shifted(dx1), s1) + first(lf[0], lf[1], lf[3], lf[4], s1)
        g1 = yy[1] + first(*shifted(dx0), s1) + first(*shifted(lf[2]), s1)
        g2 = work[3, x]
        av, bv = a(x), b(x)
        for c, g in enumerate((g0, g1, g2)):
            lap = xx[c] + yy[c] + work[c, x]
            store(c, x, 2.0 * col[c][2] - prev(c, x) + av * lap + bv * g)


def main(
    fn, fp, fj, fo, cn, cp, cj, co, yn, yf, an, af, gn, bf, g2, table_ref,
    fine_out, coarse_out, fe, fb, ce, cb, f1, c1, lift, work, tops, face,
):
    ox, oy = odd("gx"), odd("gy")
    ce[:, :, 0:8] = jnp.zeros((4, 16, 8, NL), F32)
    ce[:, :, 16:24] = jnp.zeros((4, 16, 8, NL), F32)
    cb[:, :, 0:8] = jnp.zeros((5, 12, 8, NL), F32)
    cb[:, :, 16:24] = jnp.zeros((5, 12, 8, NL), F32)
    fb[:, :, 0:8] = jnp.zeros((6, 12, 8, NL), F32)
    fb[:, :, 16:24] = jnp.zeros((6, 12, 8, NL), F32)
    for x in range(8):
        for i in range(3):
            fe[i, 4 + x, 4:20] = fn[i, x]
            fb[i, 2 + x, 4:20] = fp[i, x]
            fb[3 + i, 2 + x, 4:20] = fo[i, x]
        fe[3, 4 + x, 4:20] = fj[x] * (1.0 / 12.0)
    for x in range(4):
        for i in range(3):
            ce[i, 6 + x, 8:16] = cn[i, x]
            cb[i, 4 + x, 8:16] = cp[i, x]
        for i in range(2):
            cb[3 + i, 4 + x, 8:16] = co[i, x]
        ce[3, 6 + x, 8:16] = cj[x] * (1.0 / 12.0)
    near, far = ox == 0, ox == 1
    other = 1 - ox
    sides = (
        (an, gn.at[other], g2.at[other], near, 0),
        (af, bf, bf, far, C_ROWS),
    )
    for a, c, r, high, base in sides:
        f4 = jnp.where(high, 12, 0)
        f2 = jnp.where(high, 10, 0)
        c4 = jnp.where(high, 10, 2)
        c2 = jnp.where(high, 14, 0)
        b4 = jnp.where(high, 8, 0)
        for i in range(4):
            for x in range(4):
                fe[i, f4 + x, 4:20] = a[i * 64 + x * 16 : i * 64 + x * 16 + 16]
                ce[i, c4 + x, 8:16] = a[AC + i * 32 + x * 8 : AC + i * 32 + x * 8 + 8]
            for x in range(2):
                ce[i, c2 + x, 8:16] = r[base + i * 16 + x * 8 : base + i * 16 + x * 8 + 8]
        for i in range(6):
            for x in range(2):
                fb[i, f2 + x, 4:20] = a[AB + i * 32 + x * 16 : AB + i * 32 + x * 16 + 16]
        for i in range(5):
            for x in range(4):
                cb[i, b4 + x, 8:16] = a[AD + i * 32 + x * 8 : AD + i * 32 + x * 8 + 8]

    def y_side(src, s, high):
        t4, t2, t6, t3 = (20, 20, 16, 16) if high else (0, 2, 2, 4)
        for i in range(4):
            for x in range(8):
                fe[i, 4 + x, t4 : t4 + 4] = src[i * 32 + x * 4 : i * 32 + x * 4 + 4]
            for x in range(4):
                o = YC + i * 24 + x * 6
                ce[i, 6 + x, t6 : t6 + 6] = src[o : o + 6]
        for i in range(6):
            for x in range(8):
                o = YB + i * 16 + x * 2
                fb[i, 2 + x, t2 : t2 + 2] = src[o : o + 2]
        for i in range(5):
            for x in range(4):
                o = YD + i * 16 + x * 4
                cb[i, 4 + x, t3 : t3 + 4] = src[o : o + 4]
        for a, c, r, hx, base in sides:
            f4 = jnp.where(hx, 12, 0)
            f2 = jnp.where(hx, 10, 0)
            c4 = jnp.where(hx, 10, 2)
            c2 = jnp.where(hx, 14, 0)
            b4 = jnp.where(hx, 8, 0)
            q = s * CS
            for i in range(4):
                for x in range(4):
                    o = q + i * 16 + x * 4
                    fe[i, f4 + x, t4 : t4 + 4] = c[o : o + 4]
                    o = q + CC + i * 24 + x * 6
                    ce[i, c4 + x, t6 : t6 + 6] = c[o : o + 6]
                for x in range(2):
                    o = base + 64 + s * 48 + i * 12 + x * 6
                    ce[i, c2 + x, t6 : t6 + 6] = r[o : o + 6]
            for i in range(6):
                for x in range(2):
                    o = q + CB_ + i * 4 + x * 2
                    fb[i, f2 + x, t2 : t2 + 2] = c[o : o + 2]
            for i in range(5):
                for x in range(4):
                    o = q + CC + 96 + i * 16 + x * 4
                    cb[i, b4 + x, t3 : t3 + 4] = c[o : o + 4]

    @pl.when(oy == 0)
    def _():
        y_side(yn, 0, True)
        y_side(yf, 1, False)

    @pl.when(oy == 1)
    def _():
        y_side(yn, 0, False)
        y_side(yf, 1, True)

    table = table_ref[...]
    lane = lax.broadcasted_iota(jnp.int32, (24, NL), 1)

    def view(ref, i, off):
        def get(x, count):
            return ref[i, x + off] if count is None else ref[i, x + off : x + off + count]

        return get

    def views(ref, off):
        def get(i, x, count=None):
            return view(ref, i, off)(x, count)

        return get

    def gather_top(src, n, t0):
        for x in range(n):
            v = jnp.where(lane == 0, pltpu.roll(src[0, x], 1, 1), 0.0)
            v = jnp.where(lane == 1, pltpu.roll(src[1, x], 2, 1), v)
            v = jnp.where(lane == 2, pltpu.roll(src[2, x], 3, 1), v)
            tops[t0 + x] = v[4:20]

    def mixed(x0, n, t0):
        w = rows(fb[5, x0 : x0 + n])
        plane = tops[t0 : t0 + 8].reshape(128, NL)
        return jnp.dot(w, plane, precision=lax.Precision.HIGHEST, preferred_element_type=F32).reshape(n, 24, NL)

    def with_face(c, x, v):
        return jnp.where(lane == 0, pltpu.roll(face[x], (NL - c) % NL, 1), v)

    tops[0:2] = jnp.zeros((2, 16, NL), F32)
    tops[14:16] = jnp.zeros((2, 16, NL), F32)

    def store_c1(c, x, v):
        c1[c, x] = v

    advance(12, views(ce, 0), view(ce, 3, 0), views(cb, 0), view_row(cb, 3, 0), view_row(cb, 4, 0),
            lift, work, table, 2.0, store_c1)
    gather_top(c1, 12, 2)
    face[0:2] = mixed(0, 2, 0)
    face[2:10] = mixed(2, 8, 4)
    face[10:12] = mixed(10, 2, 8)

    def store_f1(c, x, v):
        f1[c, x] = with_face(c, x, v)

    advance(12, views(fe, 0), view(fe, 3, 0), views(fb, 0), view_row(fb, 3, 0), view_row(fb, 4, 0),
            lift, work, table, 1.0, store_f1)

    def store_c2(c, x, v):
        cb[c, x] = v
        if 2 <= x < 6:
            coarse_out[c, x - 2] = v[8:16]

    advance(8, views(c1, 0), view(ce, 3, 2), views(ce, 4), view_row(cb, 3, 2), view_row(cb, 4, 2),
            lift, work, table, 2.0, store_c2)
    gather_top(cb, 8, 4)
    face[0:8] = mixed(2, 8, 4)

    def store_f2(c, x, v):
        fine_out[c, x] = with_face(c, x, v)[4:20]

    advance(8, views(f1, 0), view(fe, 3, 2), views(fe, 4), view_row(fb, 3, 2), view_row(fb, 4, 2),
            lift, work, table, 1.0, store_f2)


def view_row(ref, i, off):
    def get(x):
        return ref[i, x + off]

    return get


def pairs(size, start):
    out = []
    for i in range(start, size - 1, 2):
        out += [(i, i + 1), (i + 1, i)]
    return out


INTERPRET = False


def call(body, shapes, *operands, scratch=(), local=True):
    vmem = pl.BlockSpec(memory_space=pltpu.VMEM)
    return pl.pallas_call(
        body,
        out_shape=[pltpu.VMEM(s, F32) if local else jax.ShapeDtypeStruct(s, F32) for s in shapes],
        in_specs=[vmem] * len(operands),
        out_specs=[vmem] * len(shapes),
        scratch_shapes=[pltpu.VMEM(s, F32) for s in scratch],
        compiler_params=pltpu.CompilerParams(vmem_limit_bytes=56 << 20),
        interpret=INTERPRET,
    )(*operands)


def keep(v):
    return v if INTERPRET else pltpu.with_memory_space_constraint(v, pltpu.VMEM)


def on_device(
    fine_now, fine_prev, coarse_now, coarse_prev, fine_rho, fine_mu, fine_lam, fine_metric,
    coarse_rho, coarse_mu, coarse_lam, coarse_metric, couple_index, couple_weight,
):
    gx, gy = lax.axis_size("gx"), lax.axis_size("gy")
    near_x, far_x, near_y, far_y = pairs(gx, 0), pairs(gx, 1), pairs(gy, 0), pairs(gy, 1)
    groups = [[i, i + 1] for i in range(0, gx, 2)]
    table = jnp.asarray(vertical_matrix(), jnp.bfloat16)

    yf, yn, ro, fo, co = call(
        pack_y,
        [(Y_ROWS + 8, NL), (Y_ROWS, NL), (O_ROWS, NL), (3, 8, 16, NL), (2, 4, 8, NL)],
        fine_now, fine_prev, fine_rho, fine_mu, fine_lam, fine_metric,
        coarse_now, coarse_prev, coarse_rho, coarse_mu, coarse_lam, coarse_metric,
        couple_index, couple_weight,
    )
    fo, co, ro = keep(fo), keep(co), keep(ro)
    yf = keep(lax.ppermute(yf, "gy", far_y))
    yn = keep(lax.ppermute(yn, "gy", near_y))
    an, af = call(
        pack_x,
        [(A_ROWS, NL)] * 2,
        fine_now, fine_prev, fine_metric, fo, coarse_now, coarse_prev, coarse_metric, co,
    )
    an = keep(lax.ppermute(an, "gx", near_x))
    af = keep(lax.ppermute(af, "gx", far_x))
    (cn,) = call(pack_near, [(C_ROWS + O_ROWS, NL)], yn, yf, ro)
    gn = keep(lax.all_gather(cn, "gx", axis_index_groups=groups))
    (bf,) = call(pack_far, [(C_ROWS + R_ROWS, NL)], yn, yf, gn)
    bf = keep(lax.ppermute(bf, "gx", far_x))
    (r2,) = call(pack_second, [(R_ROWS, NL)], af, bf)
    g2 = keep(lax.all_gather(r2, "gx", axis_index_groups=groups))
    return tuple(
        call(
            main,
            [(3, 8, 16, NL), (3, 4, 8, NL)],
            fine_now, fine_prev, fine_metric, fo, coarse_now, coarse_prev, coarse_metric, co,
            yn, yf, an, af, gn, bf, g2, table,
            local=False,
            scratch=[
                (4, 16, 24, NL), (6, 12, 24, NL), (4, 16, 24, NL), (5, 12, 24, NL),
                (3, 12, 24, NL), (3, 12, 24, NL), (16, 24, NL), (4, 12, 24, NL), (16, 16, NL), (12, 24, NL),
            ],
        )
    )


def solution(mesh):
    wide, flat = P(None, "gx", "gy", None), P("gx", "gy", None)
    return jax.shard_map(
        on_device,
        mesh=mesh,
        in_specs=(wide,) * 4 + (flat,) * 10,
        out_specs=(wide, wide),
        check_vma=False,
    )
```

```python
import jax
import jax.numpy as jnp
import numpy as np
from jax import lax
from jax.experimental import pallas as pl
from jax.experimental.pallas import tpu as pltpu
from jax.sharding import PartitionSpec as P


DT2 = 0.0625
NL = 128
Y_ROWS, A_ROWS, C_ROWS, R_ROWS, O_ROWS = 336, 664, 400, 24, 8
YB, YC, YD, YT = 128, 224, 288, 328
AB, AC, AD, AT = 256, 448, 576, 656
CB_, CC, CD, CT, CS = 64, 88, 152, 192, 200
F32 = jnp.float32


def vertical_matrix():
    m = np.zeros((NL, NL))
    for k in range(2, NL - 2):
        m[k, k - 2], m[k, k - 1], m[k, k + 1], m[k, k + 2] = 1, -8, 8, -1
    m[0, 0:3] = -18, 24, -6
    m[1, 0], m[1, 2] = -6, 6
    m[NL - 2, NL - 3], m[NL - 2, NL - 1] = -6, 6
    m[NL - 1, NL - 3 :] = 6, -24, 18
    return np.concatenate([m.T, m.T], 0)


class Joined:
    def __init__(self, one, two):
        self.one, self.two = one, two

    def at(self, s):
        if s.stop <= AB:
            return self.one, s
        return self.two, slice(s.start - AB, s.stop - AB)

    def __getitem__(self, s):
        ref, s = self.at(s)
        return ref[s]

    def __setitem__(self, s, v):
        ref, s = self.at(s)
        ref[s] = v


def odd(axis):
    return lax.axis_index(axis) % 2


def rows(v):
    return v.reshape(-1, NL)


def tops_of(groups, first_slot=0):
    lane = lax.broadcasted_iota(jnp.int32, (8, NL), 1)
    acc = jnp.zeros((8, NL), F32)
    for k, v in enumerate(groups, first_slot):
        acc = jnp.where(lane // 8 == k, pltpu.roll(v, (8 * k + 8) % NL, 1), acc)
    return acc


def top_of(packed, slot):
    lane = lax.broadcasted_iota(jnp.int32, (8, NL), 1)
    return jnp.where(lane >= NL - 8, pltpu.roll(packed, (NL - 8 - 8 * slot) % NL, 1), 0.0)


def y_edge(out, stage, low, fn, fp, fj, fo, cn, cp, cj, co):
    for i in range(4):
        for x in range(8):
            v = fn[i, x] if i < 3 else fj[x] * (1.0 / 12.0)
            out[i * 32 + x * 4 : i * 32 + x * 4 + 4] = v[0:4] if low else v[12:16]
    for i in range(6):
        for x in range(8):
            v = fp[i, x] if i < 3 else fo[i - 3, x]
            v = v[0:2] if low else v[14:16]
            if i == 5:
                v = pltpu.roll(v, 8 if low else 120, 1)
            out[YB + i * 16 + x * 2 : YB + i * 16 + x * 2 + 2] = v
    for i in range(4):
        for x in range(4):
            v = cn[i, x] if i < 3 else cj[x] * (1.0 / 12.0)
            out[YC + i * 16 + x * 4 : YC + i * 16 + x * 4 + 4] = v[0:4] if low else v[4:8]
            stage[i * 8 + x * 2 : i * 8 + x * 2 + 2] = v[4:6] if low else v[2:4]
    for i in range(5):
        for x in range(4):
            v = cp[i, x] if i < 3 else co[i - 3, x]
            out[YD + i * 8 + x * 2 : YD + i * 8 + x * 2 + 2] = v[0:2] if low else v[6:8]
            stage[32 + i * 8 + x * 2 : 32 + i * 8 + x * 2 + 2] = v[2:4] if low else v[4:6]
    out[YT:Y_ROWS] = tops_of([stage[k * 8 : k * 8 + 8] for k in range(9)])


def pack_y(fn, fp, fj, fo, cn, cp, cj, co, yf, yn, ro, stage):
    oy = odd("gy")

    @pl.when(oy == 0)
    def _():
        y_edge(yf, stage, True, fn, fp, fj, fo, cn, cp, cj, co)
        y_edge(yn, stage, False, fn, fp, fj, fo, cn, cp, cj, co)

    @pl.when(oy == 1)
    def _():
        y_edge(yf, stage, False, fn, fp, fj, fo, cn, cp, cj, co)
        y_edge(yn, stage, True, fn, fp, fj, fo, cn, cp, cj, co)
    yf[Y_ROWS:] = jnp.zeros((8, NL), F32)
    x0 = 2 - 2 * odd("gx")
    ro[...] = tops_of([cn[i, x0 + x] if i < 3 else cj[x0 + x] * (1.0 / 12.0) for i in range(4) for x in range(2)])


def pack_x(fn, fp, fr, fm, fl, fj, cn, cp, cr, cm, cl, cj, ix, wt, an, am, af, fo, co):
    inv = DT2 / fr[...]
    fo[0] = fm[...] * inv
    fo[1] = (fl[...] + fm[...]) * inv
    inv = DT2 / cr[...]
    co[0] = cm[...] * inv
    co[1] = (cl[...] + cm[...]) * inv
    lane = lax.broadcasted_iota(jnp.int32, (128, NL), 1)
    index = ix[...].reshape(128, 16)
    weight = wt[...].reshape(128, 16)
    slot = index + 2 + 4 * ((index * 171) >> 11)
    acc = jnp.zeros((128, NL), F32)
    for k in range(16):
        acc = acc + jnp.where(lane == slot[:, k : k + 1], weight[:, k : k + 1], 0.0)
    fo[2] = acc.reshape(8, 16, NL)

    near = Joined(an, am)

    def x_edge(out, low):
        x0 = 0 if low else 4
        for i in range(4):
            v = fn[i, x0 : x0 + 4] if i < 3 else fj[x0 : x0 + 4] * (1.0 / 12.0)
            out[i * 64 : i * 64 + 64] = rows(v)
        x0 = 0 if low else 6
        for i in range(6):
            v = fp[i, x0 : x0 + 2] if i < 3 else fo[i - 3, x0 : x0 + 2]
            out[AB + i * 32 : AB + i * 32 + 32] = rows(v)
        for i in range(4):
            v = cn[i] if i < 3 else cj[...] * (1.0 / 12.0)
            out[AC + i * 32 : AC + i * 32 + 32] = rows(v)
        x0, x1 = (0, 2) if low else (2, 0)
        for i in range(5):
            v = cp[i, x0 : x0 + 2] if i < 3 else co[i - 3, x0 : x0 + 2]
            out[AD + i * 16 : AD + i * 16 + 16] = rows(v)
        out[AT:A_ROWS] = tops_of([cp[i, x1 + x] if i < 3 else co[i - 3, x1 + x] for i in range(5) for x in range(2)])

    ox = odd("gx")

    @pl.when(ox == 0)
    def _():
        x_edge(near, False)
        x_edge(af, True)

    @pl.when(ox == 1)
    def _():
        x_edge(near, True)
        x_edge(af, False)


def pack_corner(src, out, base, low):
    for i in range(4):
        o = i * 32 + (0 if low else 16)
        out[base + i * 16 : base + i * 16 + 16] = src[o : o + 16]
    for i in range(6):
        o = YB + i * 16 + (0 if low else 12)
        out[base + CB_ + i * 4 : base + CB_ + i * 4 + 4] = src[o : o + 4]
    out[base + CC : base + CS] = src[YC:Y_ROWS]


def pack_near(rn, rf, ro, out):
    out[C_ROWS : C_ROWS + O_ROWS] = ro[...]
    ox = odd("gx")

    @pl.when(ox == 0)
    def _():
        pack_corner(rn, out, 0, False)
        pack_corner(rf, out, CS, False)

    @pl.when(ox == 1)
    def _():
        pack_corner(rn, out, 0, True)
        pack_corner(rf, out, CS, True)


def pack_relay(own, c, out, base, x0):
    corners = [c[o : o + 8] for s in range(2) for i in range(4) for o in [s * CS + CC + i * 16 + x0 * 4]]
    out[base : base + 8] = own + tops_of(corners, 8)
    out[base + 8 : base + 16] = c[CT:CS]
    out[base + 16 : base + 24] = c[CS + CT : 2 * CS]


def pack_far(rn, rf, c, out):
    ox = odd("gx")

    @pl.when(ox == 0)
    def _():
        pack_corner(rn, out, 0, True)
        pack_corner(rf, out, CS, True)
        pack_relay(c[1, C_ROWS : C_ROWS + 8], c.at[1], out, C_ROWS, 0)

    @pl.when(ox == 1)
    def _():
        pack_corner(rn, out, 0, False)
        pack_corner(rf, out, CS, False)
        pack_relay(c[0, C_ROWS : C_ROWS + 8], c.at[0], out, C_ROWS, 2)


def pack_second(a, c, out):
    ox = odd("gx")

    def facing(x0):
        own = [a[o : o + 8] for i in range(4) for x in range(2) for o in [AC + i * 32 + (x0 + x) * 8]]
        pack_relay(tops_of(own), c, out, 0, x0)

    @pl.when(ox == 0)
    def _():
        facing(2)

    @pl.when(ox == 1)
    def _():
        facing(0)


def vertical(v, table):
    hi = v.astype(jnp.bfloat16)
    lo = (v - hi.astype(F32)).astype(jnp.bfloat16)
    return jnp.dot(jnp.concatenate([hi, lo], 1), table, preferred_element_type=F32)


def first(m2, m1, p1, p2, scale):
    return (m2 - p2) * (scale / 12.0) + (p1 - m1) * (scale * 8.0 / 12.0)


def second(m2, m1, c, p1, p2, scale):
    return (m1 + p1) * (scale * 16.0 / 12.0) - (m2 + p2) * (scale / 12.0) - c * (scale * 2.5)


def shifted(v):
    return [pltpu.roll(v, s % 24, 0) for s in (2, 1, -1, -2)]


def advance(n, u, j, prev, a, b, lift, work, table, spacing, store):
    s1, s2 = 1.0 / spacing, 1.0 / (spacing * spacing)
    half = (n + 4) // 2
    for x0 in (0, half):
        g = vertical(rows(u(2, x0, half)), table)
        lift[x0 : x0 + half] = (rows(j(x0, half)) * g).reshape(half, 24, NL)
    for c in range(2):
        g = vertical(rows(u(c, 2, n)), table)
        work[c, 0:n] = (rows(j(2, n)) * g).reshape(n, 24, NL)
    for x in range(n):
        f0 = [u(0, x + k, None) for k in (0, 1, 3, 4)]
        m2, m1, p1, p2 = shifted(u(1, x + 2, None))
        work[3, x] = first(*f0, s1) + first(m2, m1, p1, p2, s1) + lift[x + 2]
    work[2, 0:n] = lift[2 : 2 + n]
    for c in range(4):
        g = vertical(rows(work[c, 0:n]), table)
        work[c, 0:n] = (rows(j(2, n)) * g).reshape(n, 24, NL)
    for x in range(n):
        col = [[u(c, x + k, None) for k in range(5)] for c in range(3)]
        lf = [lift[x + k] for k in range(5)]
        sh = [shifted(col[c][2]) for c in range(3)]
        xx = [second(*col[c], s2) for c in range(3)]
        yy = [second(sh[c][0], sh[c][1], col[c][2], sh[c][2], sh[c][3], s2) for c in range(3)]
        dx0 = first(col[0][0], col[0][1], col[0][3], col[0][4], s1)
        dx1 = first(col[1][0], col[1][1], col[1][3], col[1][4], s1)
        g0 = xx[0] + first(*shifted(dx1), s1) + first(lf[0], lf[1], lf[3], lf[4], s1)
        g1 = yy[1] + first(*shifted(dx0), s1) + first(*shifted(lf[2]), s1)
        g2 = work[3, x]
        av, bv = a(x), b(x)
        for c, g in enumerate((g0, g1, g2)):
            lap = xx[c] + yy[c] + work[c, x]
            store(c, x, 2.0 * col[c][2] - prev(c, x) + av * lap + bv * g)


def main(
    fn, fp, fj, fo, cn, cp, cj, co, yn, yf, an, am, af, gn, bf, g2, table_ref,
    fine_out, coarse_out, fe, fb, ce, cb, f1, c1, lift, work, tops, face,
):
    ox, oy = odd("gx"), odd("gy")
    ce[:, :, 0:8] = jnp.zeros((4, 16, 8, NL), F32)
    ce[:, :, 16:24] = jnp.zeros((4, 16, 8, NL), F32)
    cb[:, :, 0:8] = jnp.zeros((5, 12, 8, NL), F32)
    cb[:, :, 16:24] = jnp.zeros((5, 12, 8, NL), F32)
    fb[:, :, 0:8] = jnp.zeros((6, 12, 8, NL), F32)
    fb[:, :, 16:24] = jnp.zeros((6, 12, 8, NL), F32)
    for x in range(8):
        for i in range(3):
            fe[i, 4 + x, 4:20] = fn[i, x]
            fb[i, 2 + x, 4:20] = fp[i, x]
            fb[3 + i, 2 + x, 4:20] = fo[i, x]
        fe[3, 4 + x, 4:20] = fj[x] * (1.0 / 12.0)
    for x in range(4):
        for i in range(3):
            ce[i, 6 + x, 8:16] = cn[i, x]
            cb[i, 4 + x, 8:16] = cp[i, x]
        for i in range(2):
            cb[3 + i, 4 + x, 8:16] = co[i, x]
        ce[3, 6 + x, 8:16] = cj[x] * (1.0 / 12.0)
    near, far = ox == 0, ox == 1
    other = 1 - ox
    sides = (
        (Joined(an, am), gn.at[other], g2.at[other], near, 0),
        (af, bf, bf, far, C_ROWS),
    )
    for a, c, r, high, base in sides:
        f4 = jnp.where(high, 12, 0)
        f2 = jnp.where(high, 10, 0)
        c4 = jnp.where(high, 10, 2)
        c2 = jnp.where(high, 14, 0)
        b2 = jnp.where(high, 8, 2)
        b4 = jnp.where(high, 10, 0)
        own, top = r[base : base + 8], a[AT:A_ROWS]
        for i in range(4):
            for x in range(4):
                fe[i, f4 + x, 4:20] = a[i * 64 + x * 16 : i * 64 + x * 16 + 16]
                ce[i, c4 + x, 8:16] = a[AC + i * 32 + x * 8 : AC + i * 32 + x * 8 + 8]
            for x in range(2):
                ce[i, c2 + x, 8:16] = top_of(own, i * 2 + x)
        for i in range(6):
            for x in range(2):
                fb[i, f2 + x, 4:20] = a[AB + i * 32 + x * 16 : AB + i * 32 + x * 16 + 16]
        for i in range(5):
            for x in range(2):
                cb[i, b2 + x, 8:16] = a[AD + i * 16 + x * 8 : AD + i * 16 + x * 8 + 8]
                cb[i, b4 + x, 8:16] = top_of(top, i * 2 + x)

    def y_side(src, s, high):
        t4, t2 = (20, 20) if high else (0, 2)
        k4, k2, k1, k3 = (16, 20, 16, 18) if high else (4, 2, 6, 4)
        top = src[YT:Y_ROWS]
        for i in range(4):
            for x in range(8):
                fe[i, 4 + x, t4 : t4 + 4] = src[i * 32 + x * 4 : i * 32 + x * 4 + 4]
            v = top_of(top, i)
            for x in range(4):
                o = YC + i * 16 + x * 4
                ce[i, 6 + x, k4 : k4 + 4] = src[o : o + 4]
                ce[i, 6 + x, k2 : k2 + 2] = v[x * 2 : x * 2 + 2]
        for i in range(6):
            for x in range(8):
                o = YB + i * 16 + x * 2
                fb[i, 2 + x, t2 : t2 + 2] = src[o : o + 2]
        for i in range(5):
            v = top_of(top, 4 + i)
            for x in range(4):
                o = YD + i * 8 + x * 2
                cb[i, 4 + x, k1 : k1 + 2] = src[o : o + 2]
                cb[i, 4 + x, k3 : k3 + 2] = v[x * 2 : x * 2 + 2]
        for a, c, r, hx, base in sides:
            f4 = jnp.where(hx, 12, 0)
            f2 = jnp.where(hx, 10, 0)
            c4 = jnp.where(hx, 10, 2)
            c2 = jnp.where(hx, 14, 0)
            b4 = jnp.where(hx, 8, 0)
            q = s * CS
            top = c[q + CT : q + CS]
            beyond = r[base : base + 8]
            beyond_top = r[base + 8 + s * 8 : base + 16 + s * 8]
            for i in range(4):
                v = top_of(top, i)
                for x in range(4):
                    o = q + i * 16 + x * 4
                    fe[i, f4 + x, t4 : t4 + 4] = c[o : o + 4]
                    o = q + CC + i * 16 + x * 4
                    ce[i, c4 + x, k4 : k4 + 4] = c[o : o + 4]
                    ce[i, c4 + x, k2 : k2 + 2] = v[x * 2 : x * 2 + 2]
                v = top_of(beyond, 8 + s * 4 + i)
                w = top_of(beyond_top, i)
                w = jnp.where(hx, w, pltpu.roll(w, 4, 0))
                for x in range(2):
                    ce[i, c2 + x, k4 : k4 + 4] = v[x * 4 : x * 4 + 4]
                    ce[i, c2 + x, k2 : k2 + 2] = w[x * 2 : x * 2 + 2]
            for i in range(6):
                for x in range(2):
                    o = q + CB_ + i * 4 + x * 2
                    fb[i, f2 + x, t2 : t2 + 2] = c[o : o + 2]
            for i in range(5):
                v = top_of(top, 4 + i)
                for x in range(4):
                    o = q + CD + i * 8 + x * 2
                    cb[i, b4 + x, k1 : k1 + 2] = c[o : o + 2]
                    cb[i, b4 + x, k3 : k3 + 2] = v[x * 2 : x * 2 + 2]

    @pl.when(oy == 0)
    def _():
        y_side(yn, 0, True)
        y_side(yf, 1, False)

    @pl.when(oy == 1)
    def _():
        y_side(yn, 0, False)
        y_side(yf, 1, True)

    table = table_ref[...]
    lane = lax.broadcasted_iota(jnp.int32, (24, NL), 1)

    def view(ref, i, off):
        def get(x, count):
            return ref[i, x + off] if count is None else ref[i, x + off : x + off + count]

        return get

    def views(ref, off):
        def get(i, x, count=None):
            return view(ref, i, off)(x, count)

        return get

    def gather_top(src, n, t0):
        for x in range(n):
            v = jnp.where(lane == 0, pltpu.roll(src[0, x], 1, 1), 0.0)
            v = jnp.where(lane == 1, pltpu.roll(src[1, x], 2, 1), v)
            v = jnp.where(lane == 2, pltpu.roll(src[2, x], 3, 1), v)
            tops[t0 + x] = v[4:20]

    def mixed(x0, n, t0):
        w = rows(fb[5, x0 : x0 + n])
        plane = tops[t0 : t0 + 8].reshape(128, NL)
        return jnp.dot(w, plane, precision=lax.Precision.HIGHEST, preferred_element_type=F32).reshape(n, 24, NL)

    def with_face(c, x, v):
        return jnp.where(lane == 0, pltpu.roll(face[x], (NL - c) % NL, 1), v)

    tops[0:2] = jnp.zeros((2, 16, NL), F32)
    tops[14:16] = jnp.zeros((2, 16, NL), F32)

    def store_c1(c, x, v):
        c1[c, x] = v

    advance(12, views(ce, 0), view(ce, 3, 0), views(cb, 0), view_row(cb, 3, 0), view_row(cb, 4, 0),
            lift, work, table, 2.0, store_c1)
    gather_top(c1, 12, 2)
    face[0:2] = mixed(0, 2, 0)
    face[2:10] = mixed(2, 8, 4)
    face[10:12] = mixed(10, 2, 8)

    def store_f1(c, x, v):
        f1[c, x] = with_face(c, x, v)

    advance(12, views(fe, 0), view(fe, 3, 0), views(fb, 0), view_row(fb, 3, 0), view_row(fb, 4, 0),
            lift, work, table, 1.0, store_f1)

    def store_c2(c, x, v):
        cb[c, x] = v
        if 2 <= x < 6:
            coarse_out[c, x - 2] = v[8:16]

    advance(8, views(c1, 0), view(ce, 3, 2), views(ce, 4), view_row(cb, 3, 2), view_row(cb, 4, 2),
            lift, work, table, 2.0, store_c2)
    gather_top(cb, 8, 4)
    face[0:8] = mixed(2, 8, 4)

    def store_f2(c, x, v):
        fine_out[c, x] = with_face(c, x, v)[4:20]

    advance(8, views(f1, 0), view(fe, 3, 2), views(fe, 4), view_row(fb, 3, 2), view_row(fb, 4, 2),
            lift, work, table, 1.0, store_f2)


def view_row(ref, i, off):
    def get(x):
        return ref[i, x + off]

    return get


def pairs(size, start):
    out = []
    for i in range(start, size - 1, 2):
        out += [(i, i + 1), (i + 1, i)]
    return out


INTERPRET = False


def call(body, shapes, *operands, scratch=(), local=True):
    vmem = pl.BlockSpec(memory_space=pltpu.VMEM)
    return pl.pallas_call(
        body,
        out_shape=[pltpu.VMEM(s, F32) if local else jax.ShapeDtypeStruct(s, F32) for s in shapes],
        in_specs=[vmem] * len(operands),
        out_specs=[vmem] * len(shapes),
        scratch_shapes=[pltpu.VMEM(s, F32) for s in scratch],
        compiler_params=pltpu.CompilerParams(vmem_limit_bytes=56 << 20),
        interpret=INTERPRET,
    )(*operands)


def keep(v):
    return v if INTERPRET else pltpu.with_memory_space_constraint(v, pltpu.VMEM)


def on_device(
    fine_now, fine_prev, coarse_now, coarse_prev, fine_rho, fine_mu, fine_lam, fine_metric,
    coarse_rho, coarse_mu, coarse_lam, coarse_metric, couple_index, couple_weight,
):
    gx, gy = lax.axis_size("gx"), lax.axis_size("gy")
    near_x, far_x, near_y, far_y = pairs(gx, 0), pairs(gx, 1), pairs(gy, 0), pairs(gy, 1)
    groups = [[i, i + 1] for i in range(0, gx, 2)]
    table = jnp.asarray(vertical_matrix(), jnp.bfloat16)

    an, am, af, fo, co = call(
        pack_x,
        [(AB, NL), (A_ROWS - AB, NL), (A_ROWS, NL)] + [(3, 8, 16, NL), (2, 4, 8, NL)],
        fine_now, fine_prev, fine_rho, fine_mu, fine_lam, fine_metric,
        coarse_now, coarse_prev, coarse_rho, coarse_mu, coarse_lam, coarse_metric,
        couple_index, couple_weight,
    )
    fo, co = keep(fo), keep(co)
    af = keep(lax.ppermute(af, "gx", far_x))
    yf, yn, ro = call(
        pack_y,
        [(Y_ROWS + 8, NL), (Y_ROWS, NL), (O_ROWS, NL)],
        fine_now, fine_prev, fine_metric, fo, coarse_now, coarse_prev, coarse_metric, co,
        scratch=[(72, NL)],
    )
    ro = keep(ro)
    yf = keep(lax.ppermute(yf, "gy", far_y))
    yn = keep(lax.ppermute(yn, "gy", near_y))
    an = keep(lax.ppermute(an, "gx", near_x))
    am = keep(lax.ppermute(am, "gx", near_x))
    (cn,) = call(pack_near, [(C_ROWS + O_ROWS, NL)], yn, yf, ro)
    gn = keep(lax.all_gather(cn, "gx", axis_index_groups=groups))
    (bf,) = call(pack_far, [(C_ROWS + R_ROWS, NL)], yn, yf, gn)
    bf = keep(lax.ppermute(bf, "gx", far_x))
    (r2,) = call(pack_second, [(R_ROWS, NL)], af, bf)
    g2 = keep(lax.all_gather(r2, "gx", axis_index_groups=groups))
    return tuple(
        call(
            main,
            [(3, 8, 16, NL), (3, 4, 8, NL)],
            fine_now, fine_prev, fine_metric, fo, coarse_now, coarse_prev, coarse_metric, co,
            yn, yf, an, am, af, gn, bf, g2, table,
            local=False,
            scratch=[
                (4, 16, 24, NL), (6, 12, 24, NL), (4, 16, 24, NL), (5, 12, 24, NL),
                (3, 12, 24, NL), (3, 12, 24, NL), (16, 24, NL), (4, 12, 24, NL), (16, 16, NL), (12, 24, NL),
            ],
        )
    )


def solution(mesh):
    wide, flat = P(None, "gx", "gy", None), P("gx", "gy", None)
    return jax.shard_map(
        on_device,
        mesh=mesh,
        in_specs=(wide,) * 4 + (flat,) * 10,
        out_specs=(wide, wide),
        check_vma=False,
    )
```

```python
import jax
import jax.numpy as jnp
import numpy as np
from jax import lax
from jax.experimental import pallas as pl
from jax.experimental.pallas import tpu as pltpu
from jax.sharding import PartitionSpec as P


DT2 = 0.0625
NL = 128
Y_ROWS, A_ROWS, C_ROWS, R_ROWS, O_ROWS = 336, 664, 400, 24, 8
YB, YC, YD, YT = 128, 224, 288, 328
AB, AC, AD, AT = 256, 448, 576, 656
CB_, CC, CD, CT, CS = 64, 88, 152, 192, 200
F32 = jnp.float32


def vertical_matrix():
    m = np.zeros((NL, NL))
    for k in range(2, NL - 2):
        m[k, k - 2], m[k, k - 1], m[k, k + 1], m[k, k + 2] = 1, -8, 8, -1
    m[0, 0:3] = -18, 24, -6
    m[1, 0], m[1, 2] = -6, 6
    m[NL - 2, NL - 3], m[NL - 2, NL - 1] = -6, 6
    m[NL - 1, NL - 3 :] = 6, -24, 18
    return np.concatenate([m.T, m.T], 0)


class Joined:
    def __init__(self, one, two):
        self.one, self.two = one, two

    def at(self, s):
        if s.stop <= AB:
            return self.one, s
        return self.two, slice(s.start - AB, s.stop - AB)

    def __getitem__(self, s):
        ref, s = self.at(s)
        return ref[s]

    def __setitem__(self, s, v):
        ref, s = self.at(s)
        ref[s] = v


def odd(axis):
    return lax.axis_index(axis) % 2


def rows(v):
    return v.reshape(-1, NL)


def tops_of(groups, first_slot=0):
    lane = lax.broadcasted_iota(jnp.int32, (8, NL), 1)
    acc = jnp.zeros((8, NL), F32)
    for k, v in enumerate(groups, first_slot):
        acc = jnp.where(lane // 8 == k, pltpu.roll(v, (8 * k + 8) % NL, 1), acc)
    return acc


def top_of(packed, slot):
    lane = lax.broadcasted_iota(jnp.int32, (8, NL), 1)
    return jnp.where(lane >= NL - 8, pltpu.roll(packed, (NL - 8 - 8 * slot) % NL, 1), 0.0)


def y_edge(out, stage, low, fn, fp, fj, fo, cn, cp, cj, co):
    for i in range(4):
        for x in range(8):
            v = fn[i, x] if i < 3 else fj[x] * (1.0 / 12.0)
            out[i * 32 + x * 4 : i * 32 + x * 4 + 4] = v[0:4] if low else v[12:16]
    for i in range(6):
        for x in range(8):
            v = fp[i, x] if i < 3 else fo[i - 3, x]
            v = v[0:2] if low else v[14:16]
            if i == 5:
                v = pltpu.roll(v, 8 if low else 120, 1)
            out[YB + i * 16 + x * 2 : YB + i * 16 + x * 2 + 2] = v
    for i in range(4):
        for x in range(4):
            v = cn[i, x] if i < 3 else cj[x] * (1.0 / 12.0)
            out[YC + i * 16 + x * 4 : YC + i * 16 + x * 4 + 4] = v[0:4] if low else v[4:8]
            stage[i * 8 + x * 2 : i * 8 + x * 2 + 2] = v[4:6] if low else v[2:4]
    for i in range(5):
        for x in range(4):
            v = cp[i, x] if i < 3 else co[i - 3, x]
            out[YD + i * 8 + x * 2 : YD + i * 8 + x * 2 + 2] = v[0:2] if low else v[6:8]
            stage[32 + i * 8 + x * 2 : 32 + i * 8 + x * 2 + 2] = v[2:4] if low else v[4:6]
    out[YT:Y_ROWS] = tops_of([stage[k * 8 : k * 8 + 8] for k in range(9)])


def pack_y(
    fn, fp, fr, fm, fl, fj, cn, cp, cr, cm, cl, cj, ix, wt,
    fe, fb, ce, cb, yf, yn, ro, stage, fo, co,
):
    inv = DT2 / fr[...]
    fo[0] = fm[...] * inv
    fo[1] = (fl[...] + fm[...]) * inv
    inv = DT2 / cr[...]
    co[0] = cm[...] * inv
    co[1] = (cl[...] + cm[...]) * inv
    lane = lax.broadcasted_iota(jnp.int32, (128, NL), 1)
    index = ix[...].reshape(128, 16)
    weight = wt[...].reshape(128, 16)
    slot = index + 2 + 4 * ((index * 171) >> 11)
    acc = jnp.zeros((128, NL), F32)
    for k in range(16):
        acc = acc + jnp.where(lane == slot[:, k : k + 1], weight[:, k : k + 1], 0.0)
    fo[2] = acc.reshape(8, 16, NL)
    oy = odd("gy")

    @pl.when(oy == 0)
    def _():
        y_edge(yf, stage, True, fn, fp, fj, fo, cn, cp, cj, co)
        y_edge(yn, stage, False, fn, fp, fj, fo, cn, cp, cj, co)

    @pl.when(oy == 1)
    def _():
        y_edge(yf, stage, False, fn, fp, fj, fo, cn, cp, cj, co)
        y_edge(yn, stage, True, fn, fp, fj, fo, cn, cp, cj, co)

    yf[Y_ROWS:] = jnp.zeros((8, NL), F32)
    x0 = 2 - 2 * odd("gx")
    ro[...] = tops_of([cn[i, x0 + x] if i < 3 else cj[x0 + x] * (1.0 / 12.0) for i in range(4) for x in range(2)])
    for half in (slice(0, 8), slice(16, 24)):
        ce[:, :, half] = jnp.zeros((4, 16, 8, NL), F32)
        cb[:, :, half] = jnp.zeros((5, 12, 8, NL), F32)
        fb[:, :, half] = jnp.zeros((6, 12, 8, NL), F32)
    for x in range(8):
        for i in range(3):
            fe[i, 4 + x, 4:20] = fn[i, x]
            fb[i, 2 + x, 4:20] = fp[i, x]
            fb[3 + i, 2 + x, 4:20] = fo[i, x]
        fe[3, 4 + x, 4:20] = fj[x] * (1.0 / 12.0)
    for x in range(4):
        for i in range(3):
            ce[i, 6 + x, 8:16] = cn[i, x]
            cb[i, 4 + x, 8:16] = cp[i, x]
        for i in range(2):
            cb[3 + i, 4 + x, 8:16] = co[i, x]
        ce[3, 6 + x, 8:16] = cj[x] * (1.0 / 12.0)


def pack_x(fe, fb, ce, cb, an, am, af):
    near = Joined(an, am)

    def x_edge(out, low):
        x0 = 4 if low else 8
        for i in range(4):
            out[i * 64 : i * 64 + 64] = rows(fe[i, x0 : x0 + 4, 4:20])
        x0 = 2 if low else 8
        for i in range(6):
            out[AB + i * 32 : AB + i * 32 + 32] = rows(fb[i, x0 : x0 + 2, 4:20])
        for i in range(4):
            out[AC + i * 32 : AC + i * 32 + 32] = rows(ce[i, 6:10, 8:16])
        x0, x1 = (4, 6) if low else (6, 4)
        for i in range(5):
            out[AD + i * 16 : AD + i * 16 + 16] = rows(cb[i, x0 : x0 + 2, 8:16])
        out[AT:A_ROWS] = tops_of([cb[i, x1 + x, 8:16] for i in range(5) for x in range(2)])

    ox = odd("gx")

    @pl.when(ox == 0)
    def _():
        x_edge(near, False)
        x_edge(af, True)

    @pl.when(ox == 1)
    def _():
        x_edge(near, True)
        x_edge(af, False)


def pack_corner(src, out, base, low):
    for i in range(4):
        o = i * 32 + (0 if low else 16)
        out[base + i * 16 : base + i * 16 + 16] = src[o : o + 16]
    for i in range(6):
        o = YB + i * 16 + (0 if low else 12)
        out[base + CB_ + i * 4 : base + CB_ + i * 4 + 4] = src[o : o + 4]
    out[base + CC : base + CS] = src[YC:Y_ROWS]


def pack_near(rn, rf, ro, out):
    out[C_ROWS : C_ROWS + O_ROWS] = ro[...]
    ox = odd("gx")

    @pl.when(ox == 0)
    def _():
        pack_corner(rn, out, 0, False)
        pack_corner(rf, out, CS, False)

    @pl.when(ox == 1)
    def _():
        pack_corner(rn, out, 0, True)
        pack_corner(rf, out, CS, True)


def pack_relay(own, c, out, base, x0):
    corners = [c[o : o + 8] for s in range(2) for i in range(4) for o in [s * CS + CC + i * 16 + x0 * 4]]
    out[base : base + 8] = own + tops_of(corners, 8)
    out[base + 8 : base + 16] = c[CT:CS]
    out[base + 16 : base + 24] = c[CS + CT : 2 * CS]


def pack_far(rn, rf, c, out):
    ox = odd("gx")

    @pl.when(ox == 0)
    def _():
        pack_corner(rn, out, 0, True)
        pack_corner(rf, out, CS, True)
        pack_relay(c[1, C_ROWS : C_ROWS + 8], c.at[1], out, C_ROWS, 0)

    @pl.when(ox == 1)
    def _():
        pack_corner(rn, out, 0, False)
        pack_corner(rf, out, CS, False)
        pack_relay(c[0, C_ROWS : C_ROWS + 8], c.at[0], out, C_ROWS, 2)


def pack_second(a, c, out):
    ox = odd("gx")

    def facing(x0):
        own = [a[o : o + 8] for i in range(4) for x in range(2) for o in [AC + i * 32 + (x0 + x) * 8]]
        pack_relay(tops_of(own), c, out, 0, x0)

    @pl.when(ox == 0)
    def _():
        facing(2)

    @pl.when(ox == 1)
    def _():
        facing(0)


def vertical(v, table):
    hi = v.astype(jnp.bfloat16)
    lo = (v - hi.astype(F32)).astype(jnp.bfloat16)
    return jnp.dot(jnp.concatenate([hi, lo], 1), table, preferred_element_type=F32)


def first(m2, m1, p1, p2, scale):
    return (m2 - p2) * (scale / 12.0) + (p1 - m1) * (scale * 8.0 / 12.0)


def second(m2, m1, c, p1, p2, scale):
    return (m1 + p1) * (scale * 16.0 / 12.0) - (m2 + p2) * (scale / 12.0) - c * (scale * 2.5)


def shifted(v):
    return [pltpu.roll(v, s % 24, 0) for s in (2, 1, -1, -2)]


def advance(n, u, j, prev, a, b, lift, work, table, spacing, store):
    s1, s2 = 1.0 / spacing, 1.0 / (spacing * spacing)
    half = (n + 4) // 2
    for x0 in (0, half):
        g = vertical(rows(u(2, x0, half)), table)
        lift[x0 : x0 + half] = (rows(j(x0, half)) * g).reshape(half, 24, NL)
    for c in range(2):
        g = vertical(rows(u(c, 2, n)), table)
        work[c, 0:n] = (rows(j(2, n)) * g).reshape(n, 24, NL)
    for x in range(n):
        f0 = [u(0, x + k, None) for k in (0, 1, 3, 4)]
        m2, m1, p1, p2 = shifted(u(1, x + 2, None))
        work[3, x] = first(*f0, s1) + first(m2, m1, p1, p2, s1) + lift[x + 2]
    work[2, 0:n] = lift[2 : 2 + n]
    for c in range(4):
        g = vertical(rows(work[c, 0:n]), table)
        work[c, 0:n] = (rows(j(2, n)) * g).reshape(n, 24, NL)
    for x in range(n):
        col = [[u(c, x + k, None) for k in range(5)] for c in range(3)]
        lf = [lift[x + k] for k in range(5)]
        sh = [shifted(col[c][2]) for c in range(3)]
        xx = [second(*col[c], s2) for c in range(3)]
        yy = [second(sh[c][0], sh[c][1], col[c][2], sh[c][2], sh[c][3], s2) for c in range(3)]
        dx0 = first(col[0][0], col[0][1], col[0][3], col[0][4], s1)
        dx1 = first(col[1][0], col[1][1], col[1][3], col[1][4], s1)
        g0 = xx[0] + first(*shifted(dx1), s1) + first(lf[0], lf[1], lf[3], lf[4], s1)
        g1 = yy[1] + first(*shifted(dx0), s1) + first(*shifted(lf[2]), s1)
        g2 = work[3, x]
        av, bv = a(x), b(x)
        for c, g in enumerate((g0, g1, g2)):
            lap = xx[c] + yy[c] + work[c, x]
            store(c, x, 2.0 * col[c][2] - prev(c, x) + av * lap + bv * g)


def bases(high):
    return (
        jnp.where(high, 12, 0), jnp.where(high, 10, 0), jnp.where(high, 10, 2), jnp.where(high, 14, 0),
        jnp.where(high, 8, 0), jnp.where(high, 8, 2), jnp.where(high, 10, 0),
    )


def y_places(high):
    return (20, 20, 16, 20, 16, 18) if high else (0, 2, 4, 2, 6, 4)


def unpack_y(src, high, fe, fb, ce, cb):
    t4, t2, k4, k2, k1, k3 = y_places(high)
    top = src[YT:Y_ROWS]
    for i in range(4):
        for x in range(8):
            fe[i, 4 + x, t4 : t4 + 4] = src[i * 32 + x * 4 : i * 32 + x * 4 + 4]
        v = top_of(top, i)
        for x in range(4):
            o = YC + i * 16 + x * 4
            ce[i, 6 + x, k4 : k4 + 4] = src[o : o + 4]
            ce[i, 6 + x, k2 : k2 + 2] = v[x * 2 : x * 2 + 2]
    for i in range(6):
        for x in range(8):
            o = YB + i * 16 + x * 2
            fb[i, 2 + x, t2 : t2 + 2] = src[o : o + 2]
    for i in range(5):
        v = top_of(top, 4 + i)
        for x in range(4):
            o = YD + i * 8 + x * 2
            cb[i, 4 + x, k1 : k1 + 2] = src[o : o + 2]
            cb[i, 4 + x, k3 : k3 + 2] = v[x * 2 : x * 2 + 2]


def unpack_corner(c, s, hx, high, fe, fb, ce, cb):
    t4, t2, k4, k2, k1, k3 = y_places(high)
    f4, f2, c4, _, b4, _, _ = bases(hx)
    q = s * CS
    top = c[q + CT : q + CS]
    for i in range(4):
        v = top_of(top, i)
        for x in range(4):
            o = q + i * 16 + x * 4
            fe[i, f4 + x, t4 : t4 + 4] = c[o : o + 4]
            o = q + CC + i * 16 + x * 4
            ce[i, c4 + x, k4 : k4 + 4] = c[o : o + 4]
            ce[i, c4 + x, k2 : k2 + 2] = v[x * 2 : x * 2 + 2]
    for i in range(6):
        for x in range(2):
            o = q + CB_ + i * 4 + x * 2
            fb[i, f2 + x, t2 : t2 + 2] = c[o : o + 2]
    for i in range(5):
        v = top_of(top, 4 + i)
        for x in range(4):
            o = q + CD + i * 8 + x * 2
            cb[i, b4 + x, k1 : k1 + 2] = c[o : o + 2]
            cb[i, b4 + x, k3 : k3 + 2] = v[x * 2 : x * 2 + 2]


def unpack_x(a, hx, fe, fb, ce, cb):
    f4, f2, c4, _, _, b2, b4 = bases(hx)
    top = a[AT:A_ROWS]
    for i in range(4):
        for x in range(4):
            fe[i, f4 + x, 4:20] = a[i * 64 + x * 16 : i * 64 + x * 16 + 16]
            ce[i, c4 + x, 8:16] = a[AC + i * 32 + x * 8 : AC + i * 32 + x * 8 + 8]
    for i in range(6):
        for x in range(2):
            fb[i, f2 + x, 4:20] = a[AB + i * 32 + x * 16 : AB + i * 32 + x * 16 + 16]
    for i in range(5):
        for x in range(2):
            cb[i, b2 + x, 8:16] = a[AD + i * 16 + x * 8 : AD + i * 16 + x * 8 + 8]
            cb[i, b4 + x, 8:16] = top_of(top, i * 2 + x)


def unpack_relay(r, base, hx, near_high, ce):
    c2 = bases(hx)[3]
    beyond = r[base : base + 8]
    for i in range(4):
        for x in range(2):
            ce[i, c2 + x, 8:16] = top_of(beyond, i * 2 + x)
        for s, high in ((0, near_high), (1, not near_high)):
            _, _, k4, k2, _, _ = y_places(high)
            v = top_of(beyond, 8 + s * 4 + i)
            w = top_of(r[base + 8 + s * 8 : base + 16 + s * 8], i)
            w = jnp.where(hx, w, pltpu.roll(w, 4, 0))
            for x in range(2):
                ce[i, c2 + x, k4 : k4 + 4] = v[x * 4 : x * 4 + 4]
                ce[i, c2 + x, k2 : k2 + 2] = w[x * 2 : x * 2 + 2]


def fill(_, __, ___, ____, yn, yf, gn, _____, fe, fb, ce, cb):
    ox, oy = odd("gx"), odd("gy")
    c, hx = gn.at[1 - ox], ox == 0

    def sides(near_high):
        for s, src, high in ((0, yn, near_high), (1, yf, not near_high)):
            unpack_y(src, high, fe, fb, ce, cb)
            unpack_corner(c, s, hx, high, fe, fb, ce, cb)

    @pl.when(oy == 0)
    def _():
        sides(True)

    @pl.when(oy == 1)
    def _():
        sides(False)


def main(
    _, __, ___, ____, an, am, af, bf, g2, table_ref,
    fine_out, coarse_out, fe, fb, ce, cb, f1, c1, lift, work, tops, face,
):
    ox, oy = odd("gx"), odd("gy")
    near, far = ox == 0, ox == 1
    unpack_x(Joined(an, am), near, fe, fb, ce, cb)
    unpack_x(af, far, fe, fb, ce, cb)

    def sides(near_high):
        for s, high in ((0, near_high), (1, not near_high)):
            unpack_corner(bf, s, far, high, fe, fb, ce, cb)
        unpack_relay(bf, C_ROWS, far, near_high, ce)
        unpack_relay(g2.at[1 - ox], 0, near, near_high, ce)

    @pl.when(oy == 0)
    def _():
        sides(True)

    @pl.when(oy == 1)
    def _():
        sides(False)

    table = table_ref[...]
    lane = lax.broadcasted_iota(jnp.int32, (24, NL), 1)

    def view(ref, i, off):
        def get(x, count):
            return ref[i, x + off] if count is None else ref[i, x + off : x + off + count]

        return get

    def views(ref, off):
        def get(i, x, count=None):
            return view(ref, i, off)(x, count)

        return get

    def gather_top(src, n, t0):
        for x in range(n):
            v = jnp.where(lane == 0, pltpu.roll(src[0, x], 1, 1), 0.0)
            v = jnp.where(lane == 1, pltpu.roll(src[1, x], 2, 1), v)
            v = jnp.where(lane == 2, pltpu.roll(src[2, x], 3, 1), v)
            tops[t0 + x] = v[4:20]

    def mixed(x0, n, t0):
        w = rows(fb[5, x0 : x0 + n])
        plane = tops[t0 : t0 + 8].reshape(128, NL)
        return jnp.dot(w, plane, precision=lax.Precision.HIGHEST, preferred_element_type=F32).reshape(n, 24, NL)

    def with_face(c, x, v):
        return jnp.where(lane == 0, pltpu.roll(face[x], (NL - c) % NL, 1), v)

    tops[0:2] = jnp.zeros((2, 16, NL), F32)
    tops[14:16] = jnp.zeros((2, 16, NL), F32)

    def store_c1(c, x, v):
        c1[c, x] = v

    advance(12, views(ce, 0), view(ce, 3, 0), views(cb, 0), view_row(cb, 3, 0), view_row(cb, 4, 0),
            lift, work, table, 2.0, store_c1)
    gather_top(c1, 12, 2)
    face[0:2] = mixed(0, 2, 0)
    face[2:10] = mixed(2, 8, 4)
    face[10:12] = mixed(10, 2, 8)

    def store_f1(c, x, v):
        f1[c, x] = with_face(c, x, v)

    advance(12, views(fe, 0), view(fe, 3, 0), views(fb, 0), view_row(fb, 3, 0), view_row(fb, 4, 0),
            lift, work, table, 1.0, store_f1)

    def store_c2(c, x, v):
        cb[c, x] = v
        if 2 <= x < 6:
            coarse_out[c, x - 2] = v[8:16]

    advance(8, views(c1, 0), view(ce, 3, 2), views(ce, 4), view_row(cb, 3, 2), view_row(cb, 4, 2),
            lift, work, table, 2.0, store_c2)
    gather_top(cb, 8, 4)
    face[0:8] = mixed(2, 8, 4)

    def store_f2(c, x, v):
        fine_out[c, x] = with_face(c, x, v)[4:20]

    advance(8, views(f1, 0), view(fe, 3, 2), views(fe, 4), view_row(fb, 3, 2), view_row(fb, 4, 2),
            lift, work, table, 1.0, store_f2)


def view_row(ref, i, off):
    def get(x):
        return ref[i, x + off]

    return get


def pairs(size, start):
    out = []
    for i in range(start, size - 1, 2):
        out += [(i, i + 1), (i + 1, i)]
    return out


INTERPRET = False


def call(body, shapes, *operands, scratch=(), local=True, alias={}):
    vmem = pl.BlockSpec(memory_space=pltpu.VMEM)
    away = 0 if local else 2
    return pl.pallas_call(
        body,
        out_shape=[jax.ShapeDtypeStruct(s, F32) if k < away else pltpu.VMEM(s, F32) for k, s in enumerate(shapes)],
        in_specs=[vmem] * len(operands),
        out_specs=[vmem] * len(shapes),
        scratch_shapes=[pltpu.VMEM(s, F32) for s in scratch],
        input_output_aliases=alias,
        compiler_params=pltpu.CompilerParams(vmem_limit_bytes=56 << 20),
        interpret=INTERPRET,
    )(*operands)


def keep(v):
    return v if INTERPRET else pltpu.with_memory_space_constraint(v, pltpu.VMEM)


def on_device(
    fine_now, fine_prev, coarse_now, coarse_prev, fine_rho, fine_mu, fine_lam, fine_metric,
    coarse_rho, coarse_mu, coarse_lam, coarse_metric, couple_index, couple_weight,
):
    gx, gy = lax.axis_size("gx"), lax.axis_size("gy")
    near_x, far_x, near_y, far_y = pairs(gx, 0), pairs(gx, 1), pairs(gy, 0), pairs(gy, 1)
    groups = [[i, i + 1] for i in range(0, gx, 2)]
    table = jnp.asarray(vertical_matrix(), jnp.bfloat16)

    blocks = [(4, 16, 24, NL), (6, 12, 24, NL), (4, 16, 24, NL), (5, 12, 24, NL)]
    *wide, yf, yn, ro = call(
        pack_y,
        blocks + [(Y_ROWS + 8, NL), (Y_ROWS, NL), (O_ROWS, NL)],
        fine_now, fine_prev, fine_rho, fine_mu, fine_lam, fine_metric,
        coarse_now, coarse_prev, coarse_rho, coarse_mu, coarse_lam, coarse_metric,
        couple_index, couple_weight,
        scratch=[(72, NL), (3, 8, 16, NL), (2, 4, 8, NL)],
    )
    wide, ro = [keep(w) for w in wide], keep(ro)
    yf = keep(lax.ppermute(yf, "gy", far_y))
    yn = keep(lax.ppermute(yn, "gy", near_y))
    an, am, af = call(pack_x, [(AB, NL), (A_ROWS - AB, NL), (A_ROWS, NL)], *wide)
    af = keep(lax.ppermute(af, "gx", far_x))
    an = keep(lax.ppermute(an, "gx", near_x))
    am = keep(lax.ppermute(am, "gx", near_x))
    (cn,) = call(pack_near, [(C_ROWS + O_ROWS, NL)], yn, yf, ro)
    gn = keep(lax.all_gather(cn, "gx", axis_index_groups=groups))
    (bp,) = call(pack_far, [(C_ROWS + R_ROWS, NL)], yn, yf, gn)
    bp = keep(bp)
    bf = keep(lax.ppermute(bp, "gx", far_x))
    wide = call(fill, blocks, *wide, yn, yf, gn, bp, alias={0: 0, 1: 1, 2: 2, 3: 3})
    wide = [keep(w) for w in wide]
    (r2,) = call(pack_second, [(R_ROWS, NL)], af, bf)
    g2 = keep(lax.all_gather(r2, "gx", axis_index_groups=groups))
    return tuple(
        call(
            main,
            [(3, 8, 16, NL), (3, 4, 8, NL)] + blocks,
            *wide, an, am, af, bf, g2, table,
            local=False,
            alias={0: 2, 1: 3, 2: 4, 3: 5},
            scratch=[
                (3, 12, 24, NL), (3, 12, 24, NL), (16, 24, NL), (4, 12, 24, NL), (16, 16, NL), (12, 24, NL),
            ],
        )[:2]
    )


def solution(mesh):
    wide, flat = P(None, "gx", "gy", None), P("gx", "gy", None)
    return jax.shard_map(
        on_device,
        mesh=mesh,
        in_specs=(wide,) * 4 + (flat,) * 10,
        out_specs=(wide, wide),
        check_vma=False,
    )
```

```python
import jax
import jax.numpy as jnp
import numpy as np
from jax import lax
from jax.experimental import pallas as pl
from jax.experimental.pallas import tpu as pltpu
from jax.sharding import PartitionSpec as P


DT2 = 0.0625
NL = 128
Y_ROWS, A_ROWS, C_ROWS, R_ROWS, O_ROWS = 336, 664, 400, 24, 8
YB, YC, YD, YT = 128, 224, 288, 328
AB, AC, AD, AT = 256, 448, 576, 656
CB_, CC, CD, CT, CS = 64, 88, 152, 192, 200
F32 = jnp.float32


def vertical_matrix():
    m = np.zeros((NL, NL))
    for k in range(2, NL - 2):
        m[k, k - 2], m[k, k - 1], m[k, k + 1], m[k, k + 2] = 1, -8, 8, -1
    m[0, 0:3] = -18, 24, -6
    m[1, 0], m[1, 2] = -6, 6
    m[NL - 2, NL - 3], m[NL - 2, NL - 1] = -6, 6
    m[NL - 1, NL - 3 :] = 6, -24, 18
    return np.concatenate([m.T, m.T], 0)


class Joined:
    def __init__(self, one, two):
        self.one, self.two = one, two

    def at(self, s):
        if s.stop <= AB:
            return self.one, s
        return self.two, slice(s.start - AB, s.stop - AB)

    def __getitem__(self, s):
        ref, s = self.at(s)
        return ref[s]

    def __setitem__(self, s, v):
        ref, s = self.at(s)
        ref[s] = v


def odd(axis):
    return lax.axis_index(axis) % 2


def rows(v):
    return v.reshape(-1, NL)


def tops_of(groups, first_slot=0):
    lane = lax.broadcasted_iota(jnp.int32, (8, NL), 1)
    acc = jnp.zeros((8, NL), F32)
    for k, v in enumerate(groups, first_slot):
        acc = jnp.where(lane // 8 == k, pltpu.roll(v, (8 * k + 8) % NL, 1), acc)
    return acc


def top_of(packed, slot):
    lane = lax.broadcasted_iota(jnp.int32, (8, NL), 1)
    return jnp.where(lane >= NL - 8, pltpu.roll(packed, (NL - 8 - 8 * slot) % NL, 1), 0.0)


def y_edge(out, stage, low, fn, fp, fj, fo, cn, cp, cj, co):
    for i in range(4):
        for x in range(8):
            v = fn[i, x] if i < 3 else fj[x] * (1.0 / 12.0)
            out[i * 32 + x * 4 : i * 32 + x * 4 + 4] = v[0:4] if low else v[12:16]
    for i in range(6):
        for x in range(8):
            v = fp[i, x] if i < 3 else fo[i - 3, x]
            v = v[0:2] if low else v[14:16]
            if i == 5:
                v = pltpu.roll(v, 8 if low else 120, 1)
            out[YB + i * 16 + x * 2 : YB + i * 16 + x * 2 + 2] = v
    for i in range(4):
        for x in range(4):
            v = cn[i, x] if i < 3 else cj[x] * (1.0 / 12.0)
            out[YC + i * 16 + x * 4 : YC + i * 16 + x * 4 + 4] = v[0:4] if low else v[4:8]
            stage[i * 8 + x * 2 : i * 8 + x * 2 + 2] = v[4:6] if low else v[2:4]
    for i in range(5):
        for x in range(4):
            v = cp[i, x] if i < 3 else co[i - 3, x]
            out[YD + i * 8 + x * 2 : YD + i * 8 + x * 2 + 2] = v[0:2] if low else v[6:8]
            stage[32 + i * 8 + x * 2 : 32 + i * 8 + x * 2 + 2] = v[2:4] if low else v[4:6]
    out[YT:Y_ROWS] = tops_of([stage[k * 8 : k * 8 + 8] for k in range(9)])


def pack_y(*refs):
    inputs, outputs, rest = refs[:14], refs[14:21], refs[21:]
    local, sems, (stage, fo, co) = rest[:14], rest[14], rest[15:]
    copies = [pltpu.make_async_copy(i, v, sems.at[k]) for k, (i, v) in enumerate(zip(inputs, local))]
    for k in PACK_ORDER:
        copies[k].start()
    fn, fp, fr, fm, fl, fj, cn, cp, cr, cm, cl, cj, ix, wt = local
    fe, fb, ce, cb, yf, yn, ro = outputs
    for half in (slice(0, 8), slice(16, 24)):
        ce[:, :, half] = jnp.zeros((4, 16, 8, NL), F32)
        cb[:, :, half] = jnp.zeros((5, 12, 8, NL), F32)
        fb[:, :, half] = jnp.zeros((6, 12, 8, NL), F32)
    lane = lax.broadcasted_iota(jnp.int32, (128, NL), 1)
    for k in PACK_ORDER[:2]:
        copies[k].wait()
    index = ix[...].reshape(128, 16)
    weight = wt[...].reshape(128, 16)
    slot = index + 2 + 4 * ((index * 171) >> 11)
    acc = jnp.zeros((128, NL), F32)
    for k in range(16):
        acc = acc + jnp.where(lane == slot[:, k : k + 1], weight[:, k : k + 1], 0.0)
    fo[2] = acc.reshape(8, 16, NL)
    for k in PACK_ORDER[2:]:
        copies[k].wait()
    inv = DT2 / fr[...]
    fo[0] = fm[...] * inv
    fo[1] = (fl[...] + fm[...]) * inv
    inv = DT2 / cr[...]
    co[0] = cm[...] * inv
    co[1] = (cl[...] + cm[...]) * inv
    oy = odd("gy")

    @pl.when(oy == 0)
    def _():
        y_edge(yf, stage, True, fn, fp, fj, fo, cn, cp, cj, co)
        y_edge(yn, stage, False, fn, fp, fj, fo, cn, cp, cj, co)

    @pl.when(oy == 1)
    def _():
        y_edge(yf, stage, False, fn, fp, fj, fo, cn, cp, cj, co)
        y_edge(yn, stage, True, fn, fp, fj, fo, cn, cp, cj, co)

    yf[Y_ROWS:] = jnp.zeros((8, NL), F32)
    x0 = 2 - 2 * odd("gx")
    ro[...] = tops_of([cn[i, x0 + x] if i < 3 else cj[x0 + x] * (1.0 / 12.0) for i in range(4) for x in range(2)])
    for x in range(8):
        for i in range(3):
            fe[i, 4 + x, 4:20] = fn[i, x]
            fb[i, 2 + x, 4:20] = fp[i, x]
            fb[3 + i, 2 + x, 4:20] = fo[i, x]
        fe[3, 4 + x, 4:20] = fj[x] * (1.0 / 12.0)
    for x in range(4):
        for i in range(3):
            ce[i, 6 + x, 8:16] = cn[i, x]
            cb[i, 4 + x, 8:16] = cp[i, x]
        for i in range(2):
            cb[3 + i, 4 + x, 8:16] = co[i, x]
        ce[3, 6 + x, 8:16] = cj[x] * (1.0 / 12.0)


def pack_x(fe, fb, ce, cb, an, am, af):
    near = Joined(an, am)

    def x_edge(out, low):
        x0 = 4 if low else 8
        for i in range(4):
            out[i * 64 : i * 64 + 64] = rows(fe[i, x0 : x0 + 4, 4:20])
        x0 = 2 if low else 8
        for i in range(6):
            out[AB + i * 32 : AB + i * 32 + 32] = rows(fb[i, x0 : x0 + 2, 4:20])
        for i in range(4):
            out[AC + i * 32 : AC + i * 32 + 32] = rows(ce[i, 6:10, 8:16])
        x0, x1 = (4, 6) if low else (6, 4)
        for i in range(5):
            out[AD + i * 16 : AD + i * 16 + 16] = rows(cb[i, x0 : x0 + 2, 8:16])
        out[AT:A_ROWS] = tops_of([cb[i, x1 + x, 8:16] for i in range(5) for x in range(2)])

    ox = odd("gx")

    @pl.when(ox == 0)
    def _():
        x_edge(near, False)
        x_edge(af, True)

    @pl.when(ox == 1)
    def _():
        x_edge(near, True)
        x_edge(af, False)


def pack_corner(src, out, base, low):
    for i in range(4):
        o = i * 32 + (0 if low else 16)
        out[base + i * 16 : base + i * 16 + 16] = src[o : o + 16]
    for i in range(6):
        o = YB + i * 16 + (0 if low else 12)
        out[base + CB_ + i * 4 : base + CB_ + i * 4 + 4] = src[o : o + 4]
    out[base + CC : base + CS] = src[YC:Y_ROWS]


def pack_near(rn, rf, ro, out):
    out[C_ROWS : C_ROWS + O_ROWS] = ro[...]
    ox = odd("gx")

    @pl.when(ox == 0)
    def _():
        pack_corner(rn, out, 0, False)
        pack_corner(rf, out, CS, False)

    @pl.when(ox == 1)
    def _():
        pack_corner(rn, out, 0, True)
        pack_corner(rf, out, CS, True)


def pack_relay(own, c, out, base, x0):
    corners = [c[o : o + 8] for s in range(2) for i in range(4) for o in [s * CS + CC + i * 16 + x0 * 4]]
    out[base : base + 8] = own + tops_of(corners, 8)
    out[base + 8 : base + 16] = c[CT:CS]
    out[base + 16 : base + 24] = c[CS + CT : 2 * CS]


def pack_far(rn, rf, c, out):
    ox = odd("gx")

    @pl.when(ox == 0)
    def _():
        pack_corner(rn, out, 0, True)
        pack_corner(rf, out, CS, True)
        pack_relay(c[1, C_ROWS : C_ROWS + 8], c.at[1], out, C_ROWS, 0)

    @pl.when(ox == 1)
    def _():
        pack_corner(rn, out, 0, False)
        pack_corner(rf, out, CS, False)
        pack_relay(c[0, C_ROWS : C_ROWS + 8], c.at[0], out, C_ROWS, 2)


def pack_second(a, c, out):
    ox = odd("gx")

    def facing(x0):
        own = [a[o : o + 8] for i in range(4) for x in range(2) for o in [AC + i * 32 + (x0 + x) * 8]]
        pack_relay(tops_of(own), c, out, 0, x0)

    @pl.when(ox == 0)
    def _():
        facing(2)

    @pl.when(ox == 1)
    def _():
        facing(0)


def vertical(v, table):
    hi = v.astype(jnp.bfloat16)
    lo = (v - hi.astype(F32)).astype(jnp.bfloat16)
    return jnp.dot(jnp.concatenate([hi, lo], 1), table, preferred_element_type=F32)


def first(m2, m1, p1, p2, scale):
    return (m2 - p2) * (scale / 12.0) + (p1 - m1) * (scale * 8.0 / 12.0)


def second(m2, m1, c, p1, p2, scale):
    return (m1 + p1) * (scale * 16.0 / 12.0) - (m2 + p2) * (scale / 12.0) - c * (scale * 2.5)


def shifted(v):
    return [pltpu.roll(v, s % 24, 0) for s in (2, 1, -1, -2)]


def advance(n, u, j, prev, a, b, lift, work, table, spacing, store):
    s1, s2 = 1.0 / spacing, 1.0 / (spacing * spacing)
    half = (n + 4) // 2
    for x0 in (0, half):
        g = vertical(rows(u(2, x0, half)), table)
        lift[x0 : x0 + half] = (rows(j(x0, half)) * g).reshape(half, 24, NL)
    for c in range(2):
        g = vertical(rows(u(c, 2, n)), table)
        work[c, 0:n] = (rows(j(2, n)) * g).reshape(n, 24, NL)
    for x in range(n):
        f0 = [u(0, x + k, None) for k in (0, 1, 3, 4)]
        t = first(*f0, s1) + lift[x + 2]
        v = u(1, x + 2, None)
        m2, m1, p1, p2 = shifted(v)
        work[3, x] = t + first(m2, m1, p1, p2, s1)
        yy1 = second(m2, m1, v, p1, p2, s2)
        work[4, x] = yy1
        work[5, x] = yy1 + first(*shifted(t), s1)
    work[2, 0:n] = lift[2 : 2 + n]
    for c in range(4):
        g = vertical(rows(work[c, 0:n]), table)
        work[c, 0:n] = (rows(j(2, n)) * g).reshape(n, 24, NL)
    for x in range(n):
        col = [[u(c, x + k, None) for k in range(5)] for c in range(3)]
        lf = [lift[x + k] if k != 2 else None for k in range(5)]
        sh = [shifted(col[c][2]) if c != 1 else None for c in range(3)]
        xx = [second(*col[c], s2) for c in range(3)]
        yy = [
            second(sh[c][0], sh[c][1], col[c][2], sh[c][2], sh[c][3], s2) if c != 1 else work[4, x] for c in range(3)
        ]
        dx1 = first(col[1][0], col[1][1], col[1][3], col[1][4], s1)
        g0 = xx[0] + first(*shifted(dx1), s1) + first(lf[0], lf[1], lf[3], lf[4], s1)
        g1 = work[5, x]
        g2 = work[3, x]
        av, bv = a(x), b(x)
        for c, g in enumerate((g0, g1, g2)):
            lap = xx[c] + yy[c] + work[c, x]
            store(c, x, 2.0 * col[c][2] - prev(c, x) + av * lap + bv * g)


def bases(high):
    return (
        jnp.where(high, 12, 0), jnp.where(high, 10, 0), jnp.where(high, 10, 2), jnp.where(high, 14, 0),
        jnp.where(high, 8, 0), jnp.where(high, 8, 2), jnp.where(high, 10, 0),
    )


def y_places(high):
    return (20, 20, 16, 20, 16, 18) if high else (0, 2, 4, 2, 6, 4)


def unpack_y(src, high, fe, fb, ce, cb):
    t4, t2, k4, k2, k1, k3 = y_places(high)
    top = src[YT:Y_ROWS]
    for i in range(4):
        for x in range(8):
            fe[i, 4 + x, t4 : t4 + 4] = src[i * 32 + x * 4 : i * 32 + x * 4 + 4]
        v = top_of(top, i)
        for x in range(4):
            o = YC + i * 16 + x * 4
            ce[i, 6 + x, k4 : k4 + 4] = src[o : o + 4]
            ce[i, 6 + x, k2 : k2 + 2] = v[x * 2 : x * 2 + 2]
    for i in range(6):
        for x in range(8):
            o = YB + i * 16 + x * 2
            fb[i, 2 + x, t2 : t2 + 2] = src[o : o + 2]
    for i in range(5):
        v = top_of(top, 4 + i)
        for x in range(4):
            o = YD + i * 8 + x * 2
            cb[i, 4 + x, k1 : k1 + 2] = src[o : o + 2]
            cb[i, 4 + x, k3 : k3 + 2] = v[x * 2 : x * 2 + 2]


def unpack_corner(c, s, hx, high, fe, fb, ce, cb):
    t4, t2, k4, k2, k1, k3 = y_places(high)
    f4, f2, c4, _, b4, _, _ = bases(hx)
    q = s * CS
    top = c[q + CT : q + CS]
    for i in range(4):
        v = top_of(top, i)
        for x in range(4):
            o = q + i * 16 + x * 4
            fe[i, f4 + x, t4 : t4 + 4] = c[o : o + 4]
            o = q + CC + i * 16 + x * 4
            ce[i, c4 + x, k4 : k4 + 4] = c[o : o + 4]
            ce[i, c4 + x, k2 : k2 + 2] = v[x * 2 : x * 2 + 2]
    for i in range(6):
        for x in range(2):
            o = q + CB_ + i * 4 + x * 2
            fb[i, f2 + x, t2 : t2 + 2] = c[o : o + 2]
    for i in range(5):
        v = top_of(top, 4 + i)
        for x in range(4):
            o = q + CD + i * 8 + x * 2
            cb[i, b4 + x, k1 : k1 + 2] = c[o : o + 2]
            cb[i, b4 + x, k3 : k3 + 2] = v[x * 2 : x * 2 + 2]


def unpack_x(a, hx, fe, fb, ce, cb):
    f4, f2, c4, _, _, b2, b4 = bases(hx)
    top = a[AT:A_ROWS]
    for i in range(4):
        for x in range(4):
            fe[i, f4 + x, 4:20] = a[i * 64 + x * 16 : i * 64 + x * 16 + 16]
            ce[i, c4 + x, 8:16] = a[AC + i * 32 + x * 8 : AC + i * 32 + x * 8 + 8]
    for i in range(6):
        for x in range(2):
            fb[i, f2 + x, 4:20] = a[AB + i * 32 + x * 16 : AB + i * 32 + x * 16 + 16]
    for i in range(5):
        for x in range(2):
            cb[i, b2 + x, 8:16] = a[AD + i * 16 + x * 8 : AD + i * 16 + x * 8 + 8]
            cb[i, b4 + x, 8:16] = top_of(top, i * 2 + x)


def unpack_relay(r, base, hx, near_high, ce):
    c2 = bases(hx)[3]
    beyond = r[base : base + 8]
    for i in range(4):
        for x in range(2):
            ce[i, c2 + x, 8:16] = top_of(beyond, i * 2 + x)
        for s, high in ((0, near_high), (1, not near_high)):
            _, _, k4, k2, _, _ = y_places(high)
            v = top_of(beyond, 8 + s * 4 + i)
            w = top_of(r[base + 8 + s * 8 : base + 16 + s * 8], i)
            w = jnp.where(hx, w, pltpu.roll(w, 4, 0))
            for x in range(2):
                ce[i, c2 + x, k4 : k4 + 4] = v[x * 4 : x * 4 + 4]
                ce[i, c2 + x, k2 : k2 + 2] = w[x * 2 : x * 2 + 2]


def fill(_, __, ___, ____, yn, yf, gn, _____, fe, fb, ce, cb):
    ox, oy = odd("gx"), odd("gy")
    c, hx = gn.at[1 - ox], ox == 0

    def sides(near_high):
        for s, src, high in ((0, yn, near_high), (1, yf, not near_high)):
            unpack_y(src, high, fe, fb, ce, cb)
            unpack_corner(c, s, hx, high, fe, fb, ce, cb)

    @pl.when(oy == 0)
    def _():
        sides(True)

    @pl.when(oy == 1)
    def _():
        sides(False)


def main(
    _, __, ___, ____, an, am, af, bf, g2, table_ref,
    fine_out, coarse_out, fe, fb, ce, cb, f1, c1, lift, work, tops, face,
):
    ox, oy = odd("gx"), odd("gy")
    near, far = ox == 0, ox == 1
    unpack_x(Joined(an, am), near, fe, fb, ce, cb)
    unpack_x(af, far, fe, fb, ce, cb)

    def sides(near_high):
        for s, high in ((0, near_high), (1, not near_high)):
            unpack_corner(bf, s, far, high, fe, fb, ce, cb)
        unpack_relay(bf, C_ROWS, far, near_high, ce)
        unpack_relay(g2.at[1 - ox], 0, near, near_high, ce)

    @pl.when(oy == 0)
    def _():
        sides(True)

    @pl.when(oy == 1)
    def _():
        sides(False)

    table = table_ref[...]
    lane = lax.broadcasted_iota(jnp.int32, (24, NL), 1)

    def view(ref, i, off):
        def get(x, count):
            return ref[i, x + off] if count is None else ref[i, x + off : x + off + count]

        return get

    def views(ref, off):
        def get(i, x, count=None):
            return view(ref, i, off)(x, count)

        return get

    def gather_top(src, n, t0):
        for x in range(n):
            v = jnp.where(lane == 0, pltpu.roll(src[0, x], 1, 1), 0.0)
            v = jnp.where(lane == 1, pltpu.roll(src[1, x], 2, 1), v)
            v = jnp.where(lane == 2, pltpu.roll(src[2, x], 3, 1), v)
            tops[t0 + x] = v[4:20]

    def mixed(x0, n, t0):
        w = rows(fb[5, x0 : x0 + n])
        plane = tops[t0 : t0 + 8].reshape(128, NL)
        return jnp.dot(w, plane, precision=lax.Precision.HIGHEST, preferred_element_type=F32).reshape(n, 24, NL)

    def with_face(c, x, v):
        return jnp.where(lane == 0, pltpu.roll(face[x], (NL - c) % NL, 1), v)

    tops[0:2] = jnp.zeros((2, 16, NL), F32)
    tops[14:16] = jnp.zeros((2, 16, NL), F32)

    def store_c1(c, x, v):
        c1[c, x] = v

    advance(12, views(ce, 0), view(ce, 3, 0), views(cb, 0), view_row(cb, 3, 0), view_row(cb, 4, 0),
            lift, work, table, 2.0, store_c1)
    gather_top(c1, 12, 2)
    face[0:2] = mixed(0, 2, 0)
    face[2:10] = mixed(2, 8, 4)
    face[10:12] = mixed(10, 2, 8)

    def store_f1(c, x, v):
        f1[c, x] = with_face(c, x, v)

    advance(12, views(fe, 0), view(fe, 3, 0), views(fb, 0), view_row(fb, 3, 0), view_row(fb, 4, 0),
            lift, work, table, 1.0, store_f1)

    def store_c2(c, x, v):
        cb[c, x] = v
        if 2 <= x < 6:
            coarse_out[c, x - 2] = v[8:16]

    advance(8, views(c1, 0), view(ce, 3, 2), views(ce, 4), view_row(cb, 3, 2), view_row(cb, 4, 2),
            lift, work, table, 2.0, store_c2)
    gather_top(cb, 8, 4)
    face[0:8] = mixed(2, 8, 4)

    def store_f2(c, x, v):
        fine_out[c, x] = with_face(c, x, v)[4:20]

    advance(8, views(f1, 0), view(fe, 3, 2), views(fe, 4), view_row(fb, 3, 2), view_row(fb, 4, 2),
            lift, work, table, 1.0, store_f2)


def view_row(ref, i, off):
    def get(x):
        return ref[i, x + off]

    return get


def pairs(size, start):
    out = []
    for i in range(start, size - 1, 2):
        out += [(i, i + 1), (i + 1, i)]
    return out


INTERPRET = False


def call(body, shapes, *operands, scratch=(), local=True, alias={}):
    vmem = pl.BlockSpec(memory_space=pltpu.VMEM)
    away = 0 if local else 2
    return pl.pallas_call(
        body,
        out_shape=[jax.ShapeDtypeStruct(s, F32) if k < away else pltpu.VMEM(s, F32) for k, s in enumerate(shapes)],
        in_specs=[vmem] * len(operands),
        out_specs=[vmem] * len(shapes),
        scratch_shapes=[pltpu.VMEM(s, F32) for s in scratch],
        input_output_aliases=alias,
        compiler_params=pltpu.CompilerParams(vmem_limit_bytes=56 << 20),
        interpret=INTERPRET,
    )(*operands)


def keep(v):
    return v if INTERPRET else pltpu.with_memory_space_constraint(v, pltpu.VMEM)


PACK_ORDER = (12, 13, 0, 1, 5, 2, 3, 4, 6, 7, 11, 8, 9, 10)


def pack_call(*operands):
    blocks = [(4, 16, 24, NL), (6, 12, 24, NL), (4, 16, 24, NL), (5, 12, 24, NL)]
    shapes = blocks + [(Y_ROWS + 8, NL), (Y_ROWS, NL), (O_ROWS, NL)]
    return pl.pallas_call(
        pack_y,
        out_shape=[pltpu.VMEM(s, F32) for s in shapes],
        in_specs=[pl.BlockSpec(memory_space=pl.ANY)] * len(operands),
        out_specs=[pl.BlockSpec(memory_space=pltpu.VMEM)] * len(shapes),
        scratch_shapes=[pltpu.VMEM(o.shape, o.dtype) for o in operands]
        + [pltpu.SemaphoreType.DMA((len(operands),))]
        + [pltpu.VMEM(s, F32) for s in ((72, NL), (3, 8, 16, NL), (2, 4, 8, NL))],
        compiler_params=pltpu.CompilerParams(vmem_limit_bytes=56 << 20),
        interpret=INTERPRET,
    )(*operands)


def main_call(*operands):
    blocks = [(4, 16, 24, NL), (6, 12, 24, NL), (4, 16, 24, NL), (5, 12, 24, NL)]
    return call(
        main,
        [(3, 8, 16, NL), (3, 4, 8, NL)] + blocks,
        *operands,
        keep(jnp.asarray(vertical_matrix(), jnp.bfloat16)),
        local=False,
        alias={0: 2, 1: 3, 2: 4, 3: 5},
        scratch=[(3, 12, 24, NL), (3, 12, 24, NL), (16, 24, NL), (6, 12, 24, NL), (16, 16, NL), (12, 24, NL)],
    )


def on_device(
    fine_now, fine_prev, coarse_now, coarse_prev, fine_rho, fine_mu, fine_lam, fine_metric,
    coarse_rho, coarse_mu, coarse_lam, coarse_metric, couple_index, couple_weight,
):
    gx, gy = lax.axis_size("gx"), lax.axis_size("gy")
    near_x, far_x, near_y, far_y = pairs(gx, 0), pairs(gx, 1), pairs(gy, 0), pairs(gy, 1)
    groups = [[i, i + 1] for i in range(0, gx, 2)]

    blocks = [(4, 16, 24, NL), (6, 12, 24, NL), (4, 16, 24, NL), (5, 12, 24, NL)]
    *wide, yf, yn, ro = pack_call(
        fine_now, fine_prev, fine_rho, fine_mu, fine_lam, fine_metric,
        coarse_now, coarse_prev, coarse_rho, coarse_mu, coarse_lam, coarse_metric,
        couple_index, couple_weight,
    )
    wide, ro = [keep(w) for w in wide], keep(ro)
    yf = keep(lax.ppermute(yf, "gy", far_y))
    yn = keep(lax.ppermute(yn, "gy", near_y))
    an, am, af = call(pack_x, [(AB, NL), (A_ROWS - AB, NL), (A_ROWS, NL)], *wide)
    af = keep(lax.ppermute(af, "gx", far_x))
    an = keep(lax.ppermute(an, "gx", near_x))
    am = keep(lax.ppermute(am, "gx", near_x))
    (cn,) = call(pack_near, [(C_ROWS + O_ROWS, NL)], yn, yf, ro)
    gn = keep(lax.all_gather(cn, "gx", axis_index_groups=groups))
    (bp,) = call(pack_far, [(C_ROWS + R_ROWS, NL)], yn, yf, gn)
    bp = keep(bp)
    bf = keep(lax.ppermute(bp, "gx", far_x))
    wide = call(fill, blocks, *wide, yn, yf, gn, bp, alias={0: 0, 1: 1, 2: 2, 3: 3})
    wide = [keep(w) for w in wide]
    (r2,) = call(pack_second, [(R_ROWS, NL)], af, bf)
    g2 = keep(lax.all_gather(r2, "gx", axis_index_groups=groups))
    return tuple(main_call(*wide, an, am, af, bf, g2)[:2])


def solution(mesh):
    wide, flat = P(None, "gx", "gy", None), P("gx", "gy", None)
    return jax.shard_map(
        on_device,
        mesh=mesh,
        in_specs=(wide,) * 4 + (flat,) * 10,
        out_specs=(wide, wide),
        check_vma=False,
    )
```

```python
import jax
import jax.numpy as jnp
import numpy as np
from jax import lax
from jax.experimental import pallas as pl
from jax.experimental.pallas import tpu as pltpu
from jax.sharding import PartitionSpec as P


DT2 = 0.0625
NL = 128
Y_ROWS, A_ROWS, C_ROWS, R_ROWS, O_ROWS = 336, 664, 400, 24, 8
YB, YC, YD, YT = 128, 224, 288, 328
AB, AC, AD, AT = 256, 448, 576, 656
CB_, CC, CD, CT, CS = 64, 88, 152, 192, 200
F32 = jnp.float32


def vertical_matrix():
    m = np.zeros((NL, NL))
    for k in range(2, NL - 2):
        m[k, k - 2], m[k, k - 1], m[k, k + 1], m[k, k + 2] = 1, -8, 8, -1
    m[0, 0:3] = -18, 24, -6
    m[1, 0], m[1, 2] = -6, 6
    m[NL - 2, NL - 3], m[NL - 2, NL - 1] = -6, 6
    m[NL - 1, NL - 3 :] = 6, -24, 18
    return np.concatenate([m.T, m.T], 0)


class Joined:
    def __init__(self, one, two):
        self.one, self.two = one, two

    def at(self, s):
        if s.stop <= AB:
            return self.one, s
        return self.two, slice(s.start - AB, s.stop - AB)

    def __getitem__(self, s):
        ref, s = self.at(s)
        return ref[s]

    def __setitem__(self, s, v):
        ref, s = self.at(s)
        ref[s] = v


def odd(axis):
    return lax.axis_index(axis) % 2


def rows(v):
    return v.reshape(-1, NL)


def tops_of(groups, first_slot=0):
    lane = lax.broadcasted_iota(jnp.int32, (8, NL), 1)
    acc = jnp.zeros((8, NL), F32)
    for k, v in enumerate(groups, first_slot):
        acc = jnp.where(lane // 8 == k, pltpu.roll(v, (8 * k + 8) % NL, 1), acc)
    return acc


def top_of(packed, slot):
    lane = lax.broadcasted_iota(jnp.int32, (8, NL), 1)
    return jnp.where(lane >= NL - 8, pltpu.roll(packed, (NL - 8 - 8 * slot) % NL, 1), 0.0)


def y_edge(out, stage, low, fn, fp, fj, fo, cn, cp, cj, co):
    for i in range(4):
        for x in range(8):
            v = fn[i, x] if i < 3 else fj[x] * (1.0 / 12.0)
            out[i * 32 + x * 4 : i * 32 + x * 4 + 4] = v[0:4] if low else v[12:16]
    for i in range(6):
        for x in range(8):
            v = fp[i, x] if i < 3 else fo[i - 3, x]
            v = v[0:2] if low else v[14:16]
            if i == 5:
                v = pltpu.roll(v, 8 if low else 120, 1)
            out[YB + i * 16 + x * 2 : YB + i * 16 + x * 2 + 2] = v
    for i in range(4):
        for x in range(4):
            v = cn[i, x] if i < 3 else cj[x] * (1.0 / 12.0)
            out[YC + i * 16 + x * 4 : YC + i * 16 + x * 4 + 4] = v[0:4] if low else v[4:8]
            stage[i * 8 + x * 2 : i * 8 + x * 2 + 2] = v[4:6] if low else v[2:4]
    for i in range(5):
        for x in range(4):
            v = cp[i, x] if i < 3 else co[i - 3, x]
            out[YD + i * 8 + x * 2 : YD + i * 8 + x * 2 + 2] = v[0:2] if low else v[6:8]
            stage[32 + i * 8 + x * 2 : 32 + i * 8 + x * 2 + 2] = v[2:4] if low else v[4:6]
    out[YT:Y_ROWS] = tops_of([stage[k * 8 : k * 8 + 8] for k in range(9)])


def pack_y(*refs):
    inputs, kept, (fo, co, yf, yn, ro), rest = refs[:14], refs[14:20], refs[20:25], refs[25:]
    passing, sems, stage = rest[:8], rest[8], rest[9]
    local = list(passing)
    for place, ref in zip(KEPT, kept):
        local.insert(place, ref)
    copies = [pltpu.make_async_copy(i, v, sems.at[k]) for k, (i, v) in enumerate(zip(inputs, local))]
    for k in PACK_ORDER:
        copies[k].start()
    fn, fp, fr, fm, fl, fj, cn, cp, cr, cm, cl, cj, ix, wt = local
    lane = lax.broadcasted_iota(jnp.int32, (128, NL), 1)
    for k in PACK_ORDER[:2]:
        copies[k].wait()
    index = ix[...].reshape(128, 16)
    weight = wt[...].reshape(128, 16)
    slot = index + 2 + 4 * ((index * 171) >> 11)
    acc = jnp.zeros((128, NL), F32)
    for k in range(16):
        acc = acc + jnp.where(lane == slot[:, k : k + 1], weight[:, k : k + 1], 0.0)
    fo[2] = acc.reshape(8, 16, NL)
    for k in PACK_ORDER[2:]:
        copies[k].wait()
    inv = DT2 / fr[...]
    fo[0] = fm[...] * inv
    fo[1] = (fl[...] + fm[...]) * inv
    inv = DT2 / cr[...]
    co[0] = cm[...] * inv
    co[1] = (cl[...] + cm[...]) * inv
    oy = odd("gy")

    @pl.when(oy == 0)
    def _():
        y_edge(yf, stage, True, fn, fp, fj, fo, cn, cp, cj, co)
        y_edge(yn, stage, False, fn, fp, fj, fo, cn, cp, cj, co)

    @pl.when(oy == 1)
    def _():
        y_edge(yf, stage, False, fn, fp, fj, fo, cn, cp, cj, co)
        y_edge(yn, stage, True, fn, fp, fj, fo, cn, cp, cj, co)

    yf[Y_ROWS:] = jnp.zeros((8, NL), F32)
    x0 = 2 - 2 * odd("gx")
    ro[...] = tops_of([cn[i, x0 + x] if i < 3 else cj[x0 + x] * (1.0 / 12.0) for i in range(4) for x in range(2)])


def pack_x(fn, fp, fj, cn, cp, cj, fo, co, fe, fb, ce, cb, an, am, af):
    for half in (slice(0, 8), slice(16, 24)):
        ce[:, :, half] = jnp.zeros((4, 16, 8, NL), F32)
        cb[:, :, half] = jnp.zeros((5, 12, 8, NL), F32)
        fb[:, :, half] = jnp.zeros((6, 12, 8, NL), F32)
    for x in range(8):
        for i in range(3):
            fe[i, 4 + x, 4:20] = fn[i, x]
            fb[i, 2 + x, 4:20] = fp[i, x]
            fb[3 + i, 2 + x, 4:20] = fo[i, x]
        fe[3, 4 + x, 4:20] = fj[x] * (1.0 / 12.0)
    for x in range(4):
        for i in range(3):
            ce[i, 6 + x, 8:16] = cn[i, x]
            cb[i, 4 + x, 8:16] = cp[i, x]
        for i in range(2):
            cb[3 + i, 4 + x, 8:16] = co[i, x]
        ce[3, 6 + x, 8:16] = cj[x] * (1.0 / 12.0)
    near = Joined(an, am)

    def x_edge(out, low):
        x0 = 4 if low else 8
        for i in range(4):
            out[i * 64 : i * 64 + 64] = rows(fe[i, x0 : x0 + 4, 4:20])
        x0 = 2 if low else 8
        for i in range(6):
            out[AB + i * 32 : AB + i * 32 + 32] = rows(fb[i, x0 : x0 + 2, 4:20])
        for i in range(4):
            out[AC + i * 32 : AC + i * 32 + 32] = rows(ce[i, 6:10, 8:16])
        x0, x1 = (4, 6) if low else (6, 4)
        for i in range(5):
            out[AD + i * 16 : AD + i * 16 + 16] = rows(cb[i, x0 : x0 + 2, 8:16])
        out[AT:A_ROWS] = tops_of([cb[i, x1 + x, 8:16] for i in range(5) for x in range(2)])

    ox = odd("gx")

    @pl.when(ox == 0)
    def _():
        x_edge(near, False)
        x_edge(af, True)

    @pl.when(ox == 1)
    def _():
        x_edge(near, True)
        x_edge(af, False)


def pack_corner(src, out, base, low):
    for i in range(4):
        o = i * 32 + (0 if low else 16)
        out[base + i * 16 : base + i * 16 + 16] = src[o : o + 16]
    for i in range(6):
        o = YB + i * 16 + (0 if low else 12)
        out[base + CB_ + i * 4 : base + CB_ + i * 4 + 4] = src[o : o + 4]
    out[base + CC : base + CS] = src[YC:Y_ROWS]


def pack_near(rn, rf, ro, out):
    out[C_ROWS : C_ROWS + O_ROWS] = ro[...]
    ox = odd("gx")

    @pl.when(ox == 0)
    def _():
        pack_corner(rn, out, 0, False)
        pack_corner(rf, out, CS, False)

    @pl.when(ox == 1)
    def _():
        pack_corner(rn, out, 0, True)
        pack_corner(rf, out, CS, True)


def pack_relay(own, c, out, base, x0):
    corners = [c[o : o + 8] for s in range(2) for i in range(4) for o in [s * CS + CC + i * 16 + x0 * 4]]
    out[base : base + 8] = own + tops_of(corners, 8)
    out[base + 8 : base + 16] = c[CT:CS]
    out[base + 16 : base + 24] = c[CS + CT : 2 * CS]


def pack_far(rn, rf, c, out):
    ox = odd("gx")

    @pl.when(ox == 0)
    def _():
        pack_corner(rn, out, 0, True)
        pack_corner(rf, out, CS, True)
        pack_relay(c[1, C_ROWS : C_ROWS + 8], c.at[1], out, C_ROWS, 0)

    @pl.when(ox == 1)
    def _():
        pack_corner(rn, out, 0, False)
        pack_corner(rf, out, CS, False)
        pack_relay(c[0, C_ROWS : C_ROWS + 8], c.at[0], out, C_ROWS, 2)


def pack_second(a, c, out):
    ox = odd("gx")

    def facing(x0):
        own = [a[o : o + 8] for i in range(4) for x in range(2) for o in [AC + i * 32 + (x0 + x) * 8]]
        pack_relay(tops_of(own), c, out, 0, x0)

    @pl.when(ox == 0)
    def _():
        facing(2)

    @pl.when(ox == 1)
    def _():
        facing(0)


def vertical(v, table):
    hi = v.astype(jnp.bfloat16)
    lo = (v - hi.astype(F32)).astype(jnp.bfloat16)
    return jnp.dot(jnp.concatenate([hi, lo], 1), table, preferred_element_type=F32)


def first(m2, m1, p1, p2, scale):
    return (m2 - p2) * (scale / 12.0) + (p1 - m1) * (scale * 8.0 / 12.0)


def second(m2, m1, c, p1, p2, scale):
    return (m1 + p1) * (scale * 16.0 / 12.0) - (m2 + p2) * (scale / 12.0) - c * (scale * 2.5)


def shifted(v):
    return [pltpu.roll(v, s % 24, 0) for s in (2, 1, -1, -2)]


def advance(n, u, j, prev, a, b, lift, work, table, spacing, store):
    s1, s2 = 1.0 / spacing, 1.0 / (spacing * spacing)
    half = (n + 4) // 2
    for x0 in (0, half):
        g = vertical(rows(u(2, x0, half)), table)
        lift[x0 : x0 + half] = (rows(j(x0, half)) * g).reshape(half, 24, NL)
    for c in range(2):
        g = vertical(rows(u(c, 2, n)), table)
        work[c, 0:n] = (rows(j(2, n)) * g).reshape(n, 24, NL)
    for x in range(n):
        f0 = [u(0, x + k, None) for k in (0, 1, 3, 4)]
        t = first(*f0, s1) + lift[x + 2]
        v = u(1, x + 2, None)
        m2, m1, p1, p2 = shifted(v)
        work[3, x] = t + first(m2, m1, p1, p2, s1)
        yy1 = second(m2, m1, v, p1, p2, s2)
        work[4, x] = yy1
        work[5, x] = yy1 + first(*shifted(t), s1)
    work[2, 0:n] = lift[2 : 2 + n]
    for c in range(4):
        g = vertical(rows(work[c, 0:n]), table)
        work[c, 0:n] = (rows(j(2, n)) * g).reshape(n, 24, NL)
    for x in range(n):
        col = [[u(c, x + k, None) for k in range(5)] for c in range(3)]
        lf = [lift[x + k] if k != 2 else None for k in range(5)]
        sh = [shifted(col[c][2]) if c != 1 else None for c in range(3)]
        xx = [second(*col[c], s2) for c in range(3)]
        yy = [
            second(sh[c][0], sh[c][1], col[c][2], sh[c][2], sh[c][3], s2) if c != 1 else work[4, x] for c in range(3)
        ]
        dx1 = first(col[1][0], col[1][1], col[1][3], col[1][4], s1)
        g0 = xx[0] + first(*shifted(dx1), s1) + first(lf[0], lf[1], lf[3], lf[4], s1)
        g1 = work[5, x]
        g2 = work[3, x]
        av, bv = a(x), b(x)
        for c, g in enumerate((g0, g1, g2)):
            lap = xx[c] + yy[c] + work[c, x]
            store(c, x, 2.0 * col[c][2] - prev(c, x) + av * lap + bv * g)


def bases(high):
    return (
        jnp.where(high, 12, 0), jnp.where(high, 10, 0), jnp.where(high, 10, 2), jnp.where(high, 14, 0),
        jnp.where(high, 8, 0), jnp.where(high, 8, 2), jnp.where(high, 10, 0),
    )


def y_places(high):
    return (20, 20, 16, 20, 16, 18) if high else (0, 2, 4, 2, 6, 4)


def unpack_y(src, high, fe, fb, ce, cb):
    t4, t2, k4, k2, k1, k3 = y_places(high)
    top = src[YT:Y_ROWS]
    for i in range(4):
        for x in range(8):
            fe[i, 4 + x, t4 : t4 + 4] = src[i * 32 + x * 4 : i * 32 + x * 4 + 4]
        v = top_of(top, i)
        for x in range(4):
            o = YC + i * 16 + x * 4
            ce[i, 6 + x, k4 : k4 + 4] = src[o : o + 4]
            ce[i, 6 + x, k2 : k2 + 2] = v[x * 2 : x * 2 + 2]
    for i in range(6):
        for x in range(8):
            o = YB + i * 16 + x * 2
            fb[i, 2 + x, t2 : t2 + 2] = src[o : o + 2]
    for i in range(5):
        v = top_of(top, 4 + i)
        for x in range(4):
            o = YD + i * 8 + x * 2
            cb[i, 4 + x, k1 : k1 + 2] = src[o : o + 2]
            cb[i, 4 + x, k3 : k3 + 2] = v[x * 2 : x * 2 + 2]


def unpack_corner(c, s, hx, high, fe, fb, ce, cb):
    t4, t2, k4, k2, k1, k3 = y_places(high)
    f4, f2, c4, _, b4, _, _ = bases(hx)
    q = s * CS
    top = c[q + CT : q + CS]
    for i in range(4):
        v = top_of(top, i)
        for x in range(4):
            o = q + i * 16 + x * 4
            fe[i, f4 + x, t4 : t4 + 4] = c[o : o + 4]
            o = q + CC + i * 16 + x * 4
            ce[i, c4 + x, k4 : k4 + 4] = c[o : o + 4]
            ce[i, c4 + x, k2 : k2 + 2] = v[x * 2 : x * 2 + 2]
    for i in range(6):
        for x in range(2):
            o = q + CB_ + i * 4 + x * 2
            fb[i, f2 + x, t2 : t2 + 2] = c[o : o + 2]
    for i in range(5):
        v = top_of(top, 4 + i)
        for x in range(4):
            o = q + CD + i * 8 + x * 2
            cb[i, b4 + x, k1 : k1 + 2] = c[o : o + 2]
            cb[i, b4 + x, k3 : k3 + 2] = v[x * 2 : x * 2 + 2]


def unpack_x(a, hx, fe, fb, ce, cb):
    f4, f2, c4, _, _, b2, b4 = bases(hx)
    top = a[AT:A_ROWS]
    for i in range(4):
        for x in range(4):
            fe[i, f4 + x, 4:20] = a[i * 64 + x * 16 : i * 64 + x * 16 + 16]
            ce[i, c4 + x, 8:16] = a[AC + i * 32 + x * 8 : AC + i * 32 + x * 8 + 8]
    for i in range(6):
        for x in range(2):
            fb[i, f2 + x, 4:20] = a[AB + i * 32 + x * 16 : AB + i * 32 + x * 16 + 16]
    for i in range(5):
        for x in range(2):
            cb[i, b2 + x, 8:16] = a[AD + i * 16 + x * 8 : AD + i * 16 + x * 8 + 8]
            cb[i, b4 + x, 8:16] = top_of(top, i * 2 + x)


def unpack_relay(r, base, hx, near_high, ce):
    c2 = bases(hx)[3]
    beyond = r[base : base + 8]
    for i in range(4):
        for x in range(2):
            ce[i, c2 + x, 8:16] = top_of(beyond, i * 2 + x)
        for s, high in ((0, near_high), (1, not near_high)):
            _, _, k4, k2, _, _ = y_places(high)
            v = top_of(beyond, 8 + s * 4 + i)
            w = top_of(r[base + 8 + s * 8 : base + 16 + s * 8], i)
            w = jnp.where(hx, w, pltpu.roll(w, 4, 0))
            for x in range(2):
                ce[i, c2 + x, k4 : k4 + 4] = v[x * 4 : x * 4 + 4]
                ce[i, c2 + x, k2 : k2 + 2] = w[x * 2 : x * 2 + 2]


def fill(_, __, ___, ____, yn, yf, gn, _____, fe, fb, ce, cb):
    ox, oy = odd("gx"), odd("gy")
    c, hx = gn.at[1 - ox], ox == 0

    def sides(near_high):
        for s, src, high in ((0, yn, near_high), (1, yf, not near_high)):
            unpack_y(src, high, fe, fb, ce, cb)
            unpack_corner(c, s, hx, high, fe, fb, ce, cb)

    @pl.when(oy == 0)
    def _():
        sides(True)

    @pl.when(oy == 1)
    def _():
        sides(False)


def main(
    _, __, ___, ____, an, am, af, bf, g2, table_ref,
    fine_out, coarse_out, fe, fb, ce, cb, f1, c1, lift, work, tops, face,
):
    ox, oy = odd("gx"), odd("gy")
    near, far = ox == 0, ox == 1
    unpack_x(Joined(an, am), near, fe, fb, ce, cb)
    unpack_x(af, far, fe, fb, ce, cb)

    def sides(near_high):
        for s, high in ((0, near_high), (1, not near_high)):
            unpack_corner(bf, s, far, high, fe, fb, ce, cb)
        unpack_relay(bf, C_ROWS, far, near_high, ce)
        unpack_relay(g2.at[1 - ox], 0, near, near_high, ce)

    @pl.when(oy == 0)
    def _():
        sides(True)

    @pl.when(oy == 1)
    def _():
        sides(False)

    table = table_ref[...]
    lane = lax.broadcasted_iota(jnp.int32, (24, NL), 1)

    def view(ref, i, off):
        def get(x, count):
            return ref[i, x + off] if count is None else ref[i, x + off : x + off + count]

        return get

    def views(ref, off):
        def get(i, x, count=None):
            return view(ref, i, off)(x, count)

        return get

    def gather_top(src, n, t0):
        for x in range(n):
            v = jnp.where(lane == 0, pltpu.roll(src[0, x], 1, 1), 0.0)
            v = jnp.where(lane == 1, pltpu.roll(src[1, x], 2, 1), v)
            v = jnp.where(lane == 2, pltpu.roll(src[2, x], 3, 1), v)
            tops[t0 + x] = v[4:20]

    def mixed(x0, n, t0):
        w = rows(fb[5, x0 : x0 + n])
        plane = tops[t0 : t0 + 8].reshape(128, NL)
        return jnp.dot(w, plane, precision=lax.Precision.HIGHEST, preferred_element_type=F32).reshape(n, 24, NL)

    def with_face(c, x, v):
        return jnp.where(lane == 0, pltpu.roll(face[x], (NL - c) % NL, 1), v)

    tops[0:2] = jnp.zeros((2, 16, NL), F32)
    tops[14:16] = jnp.zeros((2, 16, NL), F32)

    def store_c1(c, x, v):
        c1[c, x] = v

    advance(12, views(ce, 0), view(ce, 3, 0), views(cb, 0), view_row(cb, 3, 0), view_row(cb, 4, 0),
            lift, work, table, 2.0, store_c1)
    gather_top(c1, 12, 2)
    face[0:2] = mixed(0, 2, 0)
    face[2:10] = mixed(2, 8, 4)
    face[10:12] = mixed(10, 2, 8)

    def store_f1(c, x, v):
        f1[c, x] = with_face(c, x, v)

    advance(12, views(fe, 0), view(fe, 3, 0), views(fb, 0), view_row(fb, 3, 0), view_row(fb, 4, 0),
            lift, work, table, 1.0, store_f1)

    def store_c2(c, x, v):
        cb[c, x] = v
        if 2 <= x < 6:
            coarse_out[c, x - 2] = v[8:16]

    advance(8, views(c1, 0), view(ce, 3, 2), views(ce, 4), view_row(cb, 3, 2), view_row(cb, 4, 2),
            lift, work, table, 2.0, store_c2)
    gather_top(cb, 8, 4)
    face[0:8] = mixed(2, 8, 4)

    def store_f2(c, x, v):
        fine_out[c, x] = with_face(c, x, v)[4:20]

    advance(8, views(f1, 0), view(fe, 3, 2), views(fe, 4), view_row(fb, 3, 2), view_row(fb, 4, 2),
            lift, work, table, 1.0, store_f2)


def view_row(ref, i, off):
    def get(x):
        return ref[i, x + off]

    return get


def pairs(size, start):
    out = []
    for i in range(start, size - 1, 2):
        out += [(i, i + 1), (i + 1, i)]
    return out


INTERPRET = False


def call(body, shapes, *operands, scratch=(), local=True, alias={}):
    vmem = pl.BlockSpec(memory_space=pltpu.VMEM)
    away = 0 if local else 2
    return pl.pallas_call(
        body,
        out_shape=[jax.ShapeDtypeStruct(s, F32) if k < away else pltpu.VMEM(s, F32) for k, s in enumerate(shapes)],
        in_specs=[vmem] * len(operands),
        out_specs=[vmem] * len(shapes),
        scratch_shapes=[pltpu.VMEM(s, F32) for s in scratch],
        input_output_aliases=alias,
        compiler_params=pltpu.CompilerParams(vmem_limit_bytes=56 << 20),
        interpret=INTERPRET,
    )(*operands)


def keep(v):
    return v if INTERPRET else pltpu.with_memory_space_constraint(v, pltpu.VMEM)


PACK_ORDER = (12, 13, 0, 1, 5, 2, 3, 4, 6, 7, 11, 8, 9, 10)


KEPT = (0, 1, 5, 6, 7, 11)
BLOCKS = [(4, 16, 24, NL), (6, 12, 24, NL), (4, 16, 24, NL), (5, 12, 24, NL)]


def pack_call(*operands):
    shapes = [operands[k].shape for k in KEPT]
    shapes += [(3, 8, 16, NL), (2, 4, 8, NL), (Y_ROWS + 8, NL), (Y_ROWS, NL), (O_ROWS, NL)]
    return pl.pallas_call(
        pack_y,
        out_shape=[pltpu.VMEM(s, F32) for s in shapes],
        in_specs=[pl.BlockSpec(memory_space=pl.ANY)] * len(operands),
        out_specs=[pl.BlockSpec(memory_space=pltpu.VMEM)] * len(shapes),
        scratch_shapes=[pltpu.VMEM(o.shape, o.dtype) for k, o in enumerate(operands) if k not in KEPT]
        + [pltpu.SemaphoreType.DMA((len(operands),)), pltpu.VMEM((72, NL), F32)],
        compiler_params=pltpu.CompilerParams(vmem_limit_bytes=56 << 20),
        interpret=INTERPRET,
    )(*operands)


def main_call(*operands):
    return call(
        main,
        [(3, 8, 16, NL), (3, 4, 8, NL)] + BLOCKS,
        *operands,
        keep(jnp.asarray(vertical_matrix(), jnp.bfloat16)),
        local=False,
        alias={0: 2, 1: 3, 2: 4, 3: 5},
        scratch=[(3, 12, 24, NL), (3, 12, 24, NL), (16, 24, NL), (6, 12, 24, NL), (16, 16, NL), (12, 24, NL)],
    )


def on_device(
    fine_now, fine_prev, coarse_now, coarse_prev, fine_rho, fine_mu, fine_lam, fine_metric,
    coarse_rho, coarse_mu, coarse_lam, coarse_metric, couple_index, couple_weight,
):
    gx, gy = lax.axis_size("gx"), lax.axis_size("gy")
    near_x, far_x, near_y, far_y = pairs(gx, 0), pairs(gx, 1), pairs(gy, 0), pairs(gy, 1)
    groups = [[i, i + 1] for i in range(0, gx, 2)]

    *own, yf, yn, ro = pack_call(
        fine_now, fine_prev, fine_rho, fine_mu, fine_lam, fine_metric,
        coarse_now, coarse_prev, coarse_rho, coarse_mu, coarse_lam, coarse_metric,
        couple_index, couple_weight,
    )
    own, ro = [keep(w) for w in own], keep(ro)
    yf = keep(lax.ppermute(yf, "gy", far_y))
    yn = keep(lax.ppermute(yn, "gy", near_y))
    *wide, an, am, af = call(pack_x, BLOCKS + [(AB, NL), (A_ROWS - AB, NL), (A_ROWS, NL)], *own)
    wide = [keep(w) for w in wide]
    af = keep(lax.ppermute(af, "gx", far_x))
    an = keep(lax.ppermute(an, "gx", near_x))
    am = keep(lax.ppermute(am, "gx", near_x))
    (cn,) = call(pack_near, [(C_ROWS + O_ROWS, NL)], yn, yf, ro)
    gn = keep(lax.all_gather(cn, "gx", axis_index_groups=groups))
    (bp,) = call(pack_far, [(C_ROWS + R_ROWS, NL)], yn, yf, gn)
    bp = keep(bp)
    bf = keep(lax.ppermute(bp, "gx", far_x))
    wide = call(fill, BLOCKS, *wide, yn, yf, gn, bp, alias={0: 0, 1: 1, 2: 2, 3: 3})
    wide = [keep(w) for w in wide]
    (r2,) = call(pack_second, [(R_ROWS, NL)], af, bf)
    g2 = keep(lax.all_gather(r2, "gx", axis_index_groups=groups))
    return tuple(main_call(*wide, an, am, af, bf, g2)[:2])


def solution(mesh):
    wide, flat = P(None, "gx", "gy", None), P("gx", "gy", None)
    return jax.shard_map(
        on_device,
        mesh=mesh,
        in_specs=(wide,) * 4 + (flat,) * 10,
        out_specs=(wide, wide),
        check_vma=False,
    )
```

```python
import jax
import jax.numpy as jnp
import numpy as np
from jax import lax
from jax.experimental import pallas as pl
from jax.experimental.pallas import tpu as pltpu
from jax.sharding import PartitionSpec as P


DT2 = 0.0625
NL = 128
Y_ROWS, A_ROWS, C_ROWS, R_ROWS, O_ROWS = 336, 664, 400, 24, 8
YB, YC, YD, YT = 128, 224, 288, 328
AB, AC, AD, AT = 256, 448, 576, 656
CB_, CC, CD, CT, CS = 64, 88, 152, 192, 200
F32 = jnp.float32


def vertical_matrix():
    m = np.zeros((NL, NL))
    for k in range(2, NL - 2):
        m[k, k - 2], m[k, k - 1], m[k, k + 1], m[k, k + 2] = 1, -8, 8, -1
    m[0, 0:3] = -18, 24, -6
    m[1, 0], m[1, 2] = -6, 6
    m[NL - 2, NL - 3], m[NL - 2, NL - 1] = -6, 6
    m[NL - 1, NL - 3 :] = 6, -24, 18
    return np.concatenate([m.T, m.T], 0)


class Joined:
    def __init__(self, one, two):
        self.one, self.two = one, two

    def at(self, s):
        if s.stop <= AB:
            return self.one, s
        return self.two, slice(s.start - AB, s.stop - AB)

    def __getitem__(self, s):
        ref, s = self.at(s)
        return ref[s]

    def __setitem__(self, s, v):
        ref, s = self.at(s)
        ref[s] = v


def odd(axis):
    return lax.axis_index(axis) % 2


def rows(v):
    return v.reshape(-1, NL)


def tops_of(groups, first_slot=0):
    lane = lax.broadcasted_iota(jnp.int32, (8, NL), 1)
    acc = jnp.zeros((8, NL), F32)
    for k, v in enumerate(groups, first_slot):
        acc = jnp.where(lane // 8 == k, pltpu.roll(v, (8 * k + 8) % NL, 1), acc)
    return acc


def top_of(packed, slot):
    lane = lax.broadcasted_iota(jnp.int32, (8, NL), 1)
    return jnp.where(lane >= NL - 8, pltpu.roll(packed, (NL - 8 - 8 * slot) % NL, 1), 0.0)


def one_hot_rows(index, weight):
    lane = lax.broadcasted_iota(jnp.int32, (index.shape[0], NL), 1)
    slot = index + 2 + 4 * ((index * 171) >> 11)
    acc = jnp.zeros((index.shape[0], NL), F32)
    for k in range(16):
        acc = acc + jnp.where(lane == slot[:, k : k + 1], weight[:, k : k + 1], 0.0)
    return acc


def y_edge(out, stage, low, fn, fp, fj, fo, cn, cp, cj, co, edge):
    for i in range(4):
        for x in range(8):
            v = fn[i, x] if i < 3 else fj[x] * (1.0 / 12.0)
            out[i * 32 + x * 4 : i * 32 + x * 4 + 4] = v[0:4] if low else v[12:16]
    for i in range(6):
        for x in range(8):
            if i < 5:
                v = fp[i, x] if i < 3 else fo[i - 3, x]
                v = v[0:2] if low else v[14:16]
            else:
                v = edge[x * 4 : x * 4 + 2] if low else edge[x * 4 + 2 : x * 4 + 4]
                v = pltpu.roll(v, 8 if low else 120, 1)
            out[YB + i * 16 + x * 2 : YB + i * 16 + x * 2 + 2] = v
    for i in range(4):
        for x in range(4):
            v = cn[i, x] if i < 3 else cj[x] * (1.0 / 12.0)
            out[YC + i * 16 + x * 4 : YC + i * 16 + x * 4 + 4] = v[0:4] if low else v[4:8]
            stage[i * 8 + x * 2 : i * 8 + x * 2 + 2] = v[4:6] if low else v[2:4]
    for i in range(5):
        for x in range(4):
            v = cp[i, x] if i < 3 else co[i - 3, x]
            out[YD + i * 8 + x * 2 : YD + i * 8 + x * 2 + 2] = v[0:2] if low else v[6:8]
            stage[32 + i * 8 + x * 2 : 32 + i * 8 + x * 2 + 2] = v[2:4] if low else v[4:6]
    out[YT:Y_ROWS] = tops_of([stage[k * 8 : k * 8 + 8] for k in range(9)])


def pack_y(*refs):
    inputs, kept, (fo, co, yf, yn, ro), rest = refs[:14], refs[14:22], refs[22:27], refs[27:]
    passing, (sems, stage, edge, edge_index, edge_weight) = rest[:6], rest[6:]
    local = list(passing)
    for place, ref in zip(KEPT, kept):
        local.insert(place, ref)
    copies = [pltpu.make_async_copy(i, v, sems.at[k]) for k, (i, v) in enumerate(zip(inputs, local))]
    for k in PACK_ORDER:
        copies[k].start()
    fn, fp, fr, fm, fl, fj, cn, cp, cr, cm, cl, cj, ix, wt = local
    for k in PACK_ORDER[:2]:
        copies[k].wait()
    for x in range(8):
        for o, y in ((0, 0), (2, 14)):
            edge_index[x * 4 + o : x * 4 + o + 2] = ix[x, y : y + 2]
            edge_weight[x * 4 + o : x * 4 + o + 2] = wt[x, y : y + 2]
    edge[...] = one_hot_rows(edge_index[...], edge_weight[...])
    for k in PACK_ORDER[2:]:
        copies[k].wait()
    inv = DT2 / fr[...]
    fo[0] = fm[...] * inv
    fo[1] = (fl[...] + fm[...]) * inv
    inv = DT2 / cr[...]
    co[0] = cm[...] * inv
    co[1] = (cl[...] + cm[...]) * inv
    oy = odd("gy")

    @pl.when(oy == 0)
    def _():
        y_edge(yf, stage, True, fn, fp, fj, fo, cn, cp, cj, co, edge)
        y_edge(yn, stage, False, fn, fp, fj, fo, cn, cp, cj, co, edge)

    @pl.when(oy == 1)
    def _():
        y_edge(yf, stage, False, fn, fp, fj, fo, cn, cp, cj, co, edge)
        y_edge(yn, stage, True, fn, fp, fj, fo, cn, cp, cj, co, edge)

    yf[Y_ROWS:] = jnp.zeros((8, NL), F32)
    x0 = 2 - 2 * odd("gx")
    ro[...] = tops_of([cn[i, x0 + x] if i < 3 else cj[x0 + x] * (1.0 / 12.0) for i in range(4) for x in range(2)])


def pack_x(fn, fp, fj, cn, cp, cj, ix, wt, fo, co, fe, fb, ce, cb, an, am, af):
    for half in (slice(0, 8), slice(16, 24)):
        ce[:, :, half] = jnp.zeros((4, 16, 8, NL), F32)
        cb[:, :, half] = jnp.zeros((5, 12, 8, NL), F32)
        fb[:, :, half] = jnp.zeros((6, 12, 8, NL), F32)
    mix = one_hot_rows(ix[...].reshape(128, 16), wt[...].reshape(128, 16))
    for x in range(8):
        fb[5, 2 + x, 4:20] = mix[x * 16 : x * 16 + 16]
    for x in range(8):
        for i in range(3):
            fe[i, 4 + x, 4:20] = fn[i, x]
            fb[i, 2 + x, 4:20] = fp[i, x]
        for i in range(2):
            fb[3 + i, 2 + x, 4:20] = fo[i, x]
        fe[3, 4 + x, 4:20] = fj[x] * (1.0 / 12.0)
    for x in range(4):
        for i in range(3):
            ce[i, 6 + x, 8:16] = cn[i, x]
            cb[i, 4 + x, 8:16] = cp[i, x]
        for i in range(2):
            cb[3 + i, 4 + x, 8:16] = co[i, x]
        ce[3, 6 + x, 8:16] = cj[x] * (1.0 / 12.0)
    near = Joined(an, am)

    def x_edge(out, low):
        x0 = 4 if low else 8
        for i in range(4):
            out[i * 64 : i * 64 + 64] = rows(fe[i, x0 : x0 + 4, 4:20])
        x0 = 2 if low else 8
        for i in range(6):
            out[AB + i * 32 : AB + i * 32 + 32] = rows(fb[i, x0 : x0 + 2, 4:20])
        for i in range(4):
            out[AC + i * 32 : AC + i * 32 + 32] = rows(ce[i, 6:10, 8:16])
        x0, x1 = (4, 6) if low else (6, 4)
        for i in range(5):
            out[AD + i * 16 : AD + i * 16 + 16] = rows(cb[i, x0 : x0 + 2, 8:16])
        out[AT:A_ROWS] = tops_of([cb[i, x1 + x, 8:16] for i in range(5) for x in range(2)])

    ox = odd("gx")

    @pl.when(ox == 0)
    def _():
        x_edge(near, False)
        x_edge(af, True)

    @pl.when(ox == 1)
    def _():
        x_edge(near, True)
        x_edge(af, False)


def pack_corner(src, out, base, low):
    for i in range(4):
        o = i * 32 + (0 if low else 16)
        out[base + i * 16 : base + i * 16 + 16] = src[o : o + 16]
    for i in range(6):
        o = YB + i * 16 + (0 if low else 12)
        out[base + CB_ + i * 4 : base + CB_ + i * 4 + 4] = src[o : o + 4]
    out[base + CC : base + CS] = src[YC:Y_ROWS]


def pack_near(rn, rf, ro, out):
    out[C_ROWS : C_ROWS + O_ROWS] = ro[...]
    ox = odd("gx")

    @pl.when(ox == 0)
    def _():
        pack_corner(rn, out, 0, False)
        pack_corner(rf, out, CS, False)

    @pl.when(ox == 1)
    def _():
        pack_corner(rn, out, 0, True)
        pack_corner(rf, out, CS, True)


def pack_relay(own, c, out, base, x0):
    corners = [c[o : o + 8] for s in range(2) for i in range(4) for o in [s * CS + CC + i * 16 + x0 * 4]]
    out[base : base + 8] = own + tops_of(corners, 8)
    out[base + 8 : base + 16] = c[CT:CS]
    out[base + 16 : base + 24] = c[CS + CT : 2 * CS]


def pack_far(rn, rf, c, out):
    ox = odd("gx")

    @pl.when(ox == 0)
    def _():
        pack_corner(rn, out, 0, True)
        pack_corner(rf, out, CS, True)
        pack_relay(c[1, C_ROWS : C_ROWS + 8], c.at[1], out, C_ROWS, 0)

    @pl.when(ox == 1)
    def _():
        pack_corner(rn, out, 0, False)
        pack_corner(rf, out, CS, False)
        pack_relay(c[0, C_ROWS : C_ROWS + 8], c.at[0], out, C_ROWS, 2)


def pack_second(a, c, out):
    ox = odd("gx")

    def facing(x0):
        own = [a[o : o + 8] for i in range(4) for x in range(2) for o in [AC + i * 32 + (x0 + x) * 8]]
        pack_relay(tops_of(own), c, out, 0, x0)

    @pl.when(ox == 0)
    def _():
        facing(2)

    @pl.when(ox == 1)
    def _():
        facing(0)


def vertical(v, table):
    hi = v.astype(jnp.bfloat16)
    lo = (v - hi.astype(F32)).astype(jnp.bfloat16)
    return jnp.dot(jnp.concatenate([hi, lo], 1), table, preferred_element_type=F32)


def first(m2, m1, p1, p2, scale):
    return (m2 - p2) * (scale / 12.0) + (p1 - m1) * (scale * 8.0 / 12.0)


def second(m2, m1, c, p1, p2, scale):
    return (m1 + p1) * (scale * 16.0 / 12.0) - (m2 + p2) * (scale / 12.0) - c * (scale * 2.5)


def shifted(v):
    return [pltpu.roll(v, s % 24, 0) for s in (2, 1, -1, -2)]


def advance(n, u, j, prev, a, b, lift, work, table, spacing, store):
    s1, s2 = 1.0 / spacing, 1.0 / (spacing * spacing)
    half = (n + 4) // 2
    for x0 in (0, half):
        g = vertical(rows(u(2, x0, half)), table)
        lift[x0 : x0 + half] = (rows(j(x0, half)) * g).reshape(half, 24, NL)
    for c in range(2):
        g = vertical(rows(u(c, 2, n)), table)
        work[c, 0:n] = (rows(j(2, n)) * g).reshape(n, 24, NL)
    for x in range(n):
        f0 = [u(0, x + k, None) for k in (0, 1, 3, 4)]
        t = first(*f0, s1) + lift[x + 2]
        v = u(1, x + 2, None)
        m2, m1, p1, p2 = shifted(v)
        work[3, x] = t + first(m2, m1, p1, p2, s1)
        yy1 = second(m2, m1, v, p1, p2, s2)
        work[4, x] = yy1
        work[5, x] = yy1 + first(*shifted(t), s1)
    work[2, 0:n] = lift[2 : 2 + n]
    for c in range(4):
        g = vertical(rows(work[c, 0:n]), table)
        work[c, 0:n] = (rows(j(2, n)) * g).reshape(n, 24, NL)
    for x in range(n):
        col = [[u(c, x + k, None) for k in range(5)] for c in range(3)]
        lf = [lift[x + k] if k != 2 else None for k in range(5)]
        sh = [shifted(col[c][2]) if c != 1 else None for c in range(3)]
        xx = [second(*col[c], s2) for c in range(3)]
        yy = [
            second(sh[c][0], sh[c][1], col[c][2], sh[c][2], sh[c][3], s2) if c != 1 else work[4, x] for c in range(3)
        ]
        dx1 = first(col[1][0], col[1][1], col[1][3], col[1][4], s1)
        g0 = xx[0] + first(*shifted(dx1), s1) + first(lf[0], lf[1], lf[3], lf[4], s1)
        g1 = work[5, x]
        g2 = work[3, x]
        av, bv = a(x), b(x)
        for c, g in enumerate((g0, g1, g2)):
            lap = xx[c] + yy[c] + work[c, x]
            store(c, x, 2.0 * col[c][2] - prev(c, x) + av * lap + bv * g)


def bases(high):
    return (
        jnp.where(high, 12, 0), jnp.where(high, 10, 0), jnp.where(high, 10, 2), jnp.where(high, 14, 0),
        jnp.where(high, 8, 0), jnp.where(high, 8, 2), jnp.where(high, 10, 0),
    )


def y_places(high):
    return (20, 20, 16, 20, 16, 18) if high else (0, 2, 4, 2, 6, 4)


def unpack_y(src, high, fe, fb, ce, cb):
    t4, t2, k4, k2, k1, k3 = y_places(high)
    top = src[YT:Y_ROWS]
    for i in range(4):
        for x in range(8):
            fe[i, 4 + x, t4 : t4 + 4] = src[i * 32 + x * 4 : i * 32 + x * 4 + 4]
        v = top_of(top, i)
        for x in range(4):
            o = YC + i * 16 + x * 4
            ce[i, 6 + x, k4 : k4 + 4] = src[o : o + 4]
            ce[i, 6 + x, k2 : k2 + 2] = v[x * 2 : x * 2 + 2]
    for i in range(6):
        for x in range(8):
            o = YB + i * 16 + x * 2
            fb[i, 2 + x, t2 : t2 + 2] = src[o : o + 2]
    for i in range(5):
        v = top_of(top, 4 + i)
        for x in range(4):
            o = YD + i * 8 + x * 2
            cb[i, 4 + x, k1 : k1 + 2] = src[o : o + 2]
            cb[i, 4 + x, k3 : k3 + 2] = v[x * 2 : x * 2 + 2]


def unpack_corner(c, s, hx, high, fe, fb, ce, cb):
    t4, t2, k4, k2, k1, k3 = y_places(high)
    f4, f2, c4, _, b4, _, _ = bases(hx)
    q = s * CS
    top = c[q + CT : q + CS]
    for i in range(4):
        v = top_of(top, i)
        for x in range(4):
            o = q + i * 16 + x * 4
            fe[i, f4 + x, t4 : t4 + 4] = c[o : o + 4]
            o = q + CC + i * 16 + x * 4
            ce[i, c4 + x, k4 : k4 + 4] = c[o : o + 4]
            ce[i, c4 + x, k2 : k2 + 2] = v[x * 2 : x * 2 + 2]
    for i in range(6):
        for x in range(2):
            o = q + CB_ + i * 4 + x * 2
            fb[i, f2 + x, t2 : t2 + 2] = c[o : o + 2]
    for i in range(5):
        v = top_of(top, 4 + i)
        for x in range(4):
            o = q + CD + i * 8 + x * 2
            cb[i, b4 + x, k1 : k1 + 2] = c[o : o + 2]
            cb[i, b4 + x, k3 : k3 + 2] = v[x * 2 : x * 2 + 2]


def unpack_x(a, hx, fe, fb, ce, cb):
    f4, f2, c4, _, _, b2, b4 = bases(hx)
    top = a[AT:A_ROWS]
    for i in range(4):
        for x in range(4):
            fe[i, f4 + x, 4:20] = a[i * 64 + x * 16 : i * 64 + x * 16 + 16]
            ce[i, c4 + x, 8:16] = a[AC + i * 32 + x * 8 : AC + i * 32 + x * 8 + 8]
    for i in range(6):
        for x in range(2):
            fb[i, f2 + x, 4:20] = a[AB + i * 32 + x * 16 : AB + i * 32 + x * 16 + 16]
    for i in range(5):
        for x in range(2):
            cb[i, b2 + x, 8:16] = a[AD + i * 16 + x * 8 : AD + i * 16 + x * 8 + 8]
            cb[i, b4 + x, 8:16] = top_of(top, i * 2 + x)


def unpack_relay(r, base, hx, near_high, ce):
    c2 = bases(hx)[3]
    beyond = r[base : base + 8]
    for i in range(4):
        for x in range(2):
            ce[i, c2 + x, 8:16] = top_of(beyond, i * 2 + x)
        for s, high in ((0, near_high), (1, not near_high)):
            _, _, k4, k2, _, _ = y_places(high)
            v = top_of(beyond, 8 + s * 4 + i)
            w = top_of(r[base + 8 + s * 8 : base + 16 + s * 8], i)
            w = jnp.where(hx, w, pltpu.roll(w, 4, 0))
            for x in range(2):
                ce[i, c2 + x, k4 : k4 + 4] = v[x * 4 : x * 4 + 4]
                ce[i, c2 + x, k2 : k2 + 2] = w[x * 2 : x * 2 + 2]


def fill(_, __, ___, ____, yn, yf, gn, _____, fe, fb, ce, cb):
    ox, oy = odd("gx"), odd("gy")
    c, hx = gn.at[1 - ox], ox == 0

    def sides(near_high):
        for s, src, high in ((0, yn, near_high), (1, yf, not near_high)):
            unpack_y(src, high, fe, fb, ce, cb)
            unpack_corner(c, s, hx, high, fe, fb, ce, cb)

    @pl.when(oy == 0)
    def _():
        sides(True)

    @pl.when(oy == 1)
    def _():
        sides(False)


def main(
    _, __, ___, ____, an, am, af, bf, g2, table_ref,
    fine_out, coarse_out, fe, fb, ce, cb, f1, c1, lift, work, tops, face,
):
    ox, oy = odd("gx"), odd("gy")
    near, far = ox == 0, ox == 1
    unpack_x(Joined(an, am), near, fe, fb, ce, cb)
    unpack_x(af, far, fe, fb, ce, cb)

    def sides(near_high):
        for s, high in ((0, near_high), (1, not near_high)):
            unpack_corner(bf, s, far, high, fe, fb, ce, cb)
        unpack_relay(bf, C_ROWS, far, near_high, ce)
        unpack_relay(g2.at[1 - ox], 0, near, near_high, ce)

    @pl.when(oy == 0)
    def _():
        sides(True)

    @pl.when(oy == 1)
    def _():
        sides(False)

    table = table_ref[...]
    lane = lax.broadcasted_iota(jnp.int32, (24, NL), 1)

    def view(ref, i, off):
        def get(x, count):
            return ref[i, x + off] if count is None else ref[i, x + off : x + off + count]

        return get

    def views(ref, off):
        def get(i, x, count=None):
            return view(ref, i, off)(x, count)

        return get

    def gather_top(src, n, t0):
        for x in range(n):
            v = jnp.where(lane == 0, pltpu.roll(src[0, x], 1, 1), 0.0)
            v = jnp.where(lane == 1, pltpu.roll(src[1, x], 2, 1), v)
            v = jnp.where(lane == 2, pltpu.roll(src[2, x], 3, 1), v)
            tops[t0 + x] = v[4:20]

    def mixed(x0, n, t0):
        w = rows(fb[5, x0 : x0 + n])
        plane = tops[t0 : t0 + 8].reshape(128, NL)
        return jnp.dot(w, plane, precision=lax.Precision.HIGHEST, preferred_element_type=F32).reshape(n, 24, NL)

    def with_face(c, x, v):
        return jnp.where(lane == 0, pltpu.roll(face[x], (NL - c) % NL, 1), v)

    tops[0:2] = jnp.zeros((2, 16, NL), F32)
    tops[14:16] = jnp.zeros((2, 16, NL), F32)

    def store_c1(c, x, v):
        c1[c, x] = v

    advance(12, views(ce, 0), view(ce, 3, 0), views(cb, 0), view_row(cb, 3, 0), view_row(cb, 4, 0),
            lift, work, table, 2.0, store_c1)
    gather_top(c1, 12, 2)
    face[0:2] = mixed(0, 2, 0)
    face[2:10] = mixed(2, 8, 4)
    face[10:12] = mixed(10, 2, 8)

    def store_f1(c, x, v):
        f1[c, x] = with_face(c, x, v)

    advance(12, views(fe, 0), view(fe, 3, 0), views(fb, 0), view_row(fb, 3, 0), view_row(fb, 4, 0),
            lift, work, table, 1.0, store_f1)

    def store_c2(c, x, v):
        cb[c, x] = v
        if 2 <= x < 6:
            coarse_out[c, x - 2] = v[8:16]

    advance(8, views(c1, 0), view(ce, 3, 2), views(ce, 4), view_row(cb, 3, 2), view_row(cb, 4, 2),
            lift, work, table, 2.0, store_c2)
    gather_top(cb, 8, 4)
    face[0:8] = mixed(2, 8, 4)

    def store_f2(c, x, v):
        fine_out[c, x] = with_face(c, x, v)[4:20]

    advance(8, views(f1, 0), view(fe, 3, 2), views(fe, 4), view_row(fb, 3, 2), view_row(fb, 4, 2),
            lift, work, table, 1.0, store_f2)


def view_row(ref, i, off):
    def get(x):
        return ref[i, x + off]

    return get


def pairs(size, start):
    out = []
    for i in range(start, size - 1, 2):
        out += [(i, i + 1), (i + 1, i)]
    return out


INTERPRET = False


def call(body, shapes, *operands, scratch=(), local=True, alias={}):
    vmem = pl.BlockSpec(memory_space=pltpu.VMEM)
    away = 0 if local else 2
    return pl.pallas_call(
        body,
        out_shape=[jax.ShapeDtypeStruct(s, F32) if k < away else pltpu.VMEM(s, F32) for k, s in enumerate(shapes)],
        in_specs=[vmem] * len(operands),
        out_specs=[vmem] * len(shapes),
        scratch_shapes=[pltpu.VMEM(s, F32) for s in scratch],
        input_output_aliases=alias,
        compiler_params=pltpu.CompilerParams(vmem_limit_bytes=56 << 20),
        interpret=INTERPRET,
    )(*operands)


def keep(v):
    return v if INTERPRET else pltpu.with_memory_space_constraint(v, pltpu.VMEM)


PACK_ORDER = (12, 13, 0, 1, 5, 2, 3, 4, 6, 7, 11, 8, 9, 10)


KEPT = (0, 1, 5, 6, 7, 11, 12, 13)
BLOCKS = [(4, 16, 24, NL), (6, 12, 24, NL), (4, 16, 24, NL), (5, 12, 24, NL)]


def pack_call(*operands):
    shapes = [(2, 8, 16, NL), (2, 4, 8, NL), (Y_ROWS + 8, NL), (Y_ROWS, NL), (O_ROWS, NL)]
    return pl.pallas_call(
        pack_y,
        out_shape=[pltpu.VMEM(operands[k].shape, operands[k].dtype) for k in KEPT] + [pltpu.VMEM(s, F32) for s in shapes],
        in_specs=[pl.BlockSpec(memory_space=pl.ANY)] * len(operands),
        out_specs=[pl.BlockSpec(memory_space=pltpu.VMEM)] * (len(KEPT) + len(shapes)),
        scratch_shapes=[pltpu.VMEM(o.shape, o.dtype) for k, o in enumerate(operands) if k not in KEPT]
        + [pltpu.SemaphoreType.DMA((len(operands),)), pltpu.VMEM((72, NL), F32)]
        + [pltpu.VMEM((32, NL), F32), pltpu.VMEM((32, 16), jnp.int32), pltpu.VMEM((32, 16), F32)],
        compiler_params=pltpu.CompilerParams(vmem_limit_bytes=56 << 20),
        interpret=INTERPRET,
    )(*operands)


def main_call(*operands):
    return call(
        main,
        [(3, 8, 16, NL), (3, 4, 8, NL)] + BLOCKS,
        *operands,
        keep(jnp.asarray(vertical_matrix(), jnp.bfloat16)),
        local=False,
        alias={0: 2, 1: 3, 2: 4, 3: 5},
        scratch=[(3, 12, 24, NL), (3, 12, 24, NL), (16, 24, NL), (6, 12, 24, NL), (16, 16, NL), (12, 24, NL)],
    )


def on_device(
    fine_now, fine_prev, coarse_now, coarse_prev, fine_rho, fine_mu, fine_lam, fine_metric,
    coarse_rho, coarse_mu, coarse_lam, coarse_metric, couple_index, couple_weight,
):
    gx, gy = lax.axis_size("gx"), lax.axis_size("gy")
    near_x, far_x, near_y, far_y = pairs(gx, 0), pairs(gx, 1), pairs(gy, 0), pairs(gy, 1)
    groups = [[i, i + 1] for i in range(0, gx, 2)]

    *own, yf, yn, ro = pack_call(
        fine_now, fine_prev, fine_rho, fine_mu, fine_lam, fine_metric,
        coarse_now, coarse_prev, coarse_rho, coarse_mu, coarse_lam, coarse_metric,
        couple_index, couple_weight,
    )
    own, ro = [keep(w) for w in own], keep(ro)
    yf = keep(lax.ppermute(yf, "gy", far_y))
    yn = keep(lax.ppermute(yn, "gy", near_y))
    *wide, an, am, af = call(pack_x, BLOCKS + [(AB, NL), (A_ROWS - AB, NL), (A_ROWS, NL)], *own)
    wide = [keep(w) for w in wide]
    af = keep(lax.ppermute(af, "gx", far_x))
    an = keep(lax.ppermute(an, "gx", near_x))
    am = keep(lax.ppermute(am, "gx", near_x))
    (cn,) = call(pack_near, [(C_ROWS + O_ROWS, NL)], yn, yf, ro)
    gn = keep(lax.all_gather(cn, "gx", axis_index_groups=groups))
    (bp,) = call(pack_far, [(C_ROWS + R_ROWS, NL)], yn, yf, gn)
    bp = keep(bp)
    bf = keep(lax.ppermute(bp, "gx", far_x))
    wide = call(fill, BLOCKS, *wide, yn, yf, gn, bp, alias={0: 0, 1: 1, 2: 2, 3: 3})
    wide = [keep(w) for w in wide]
    (r2,) = call(pack_second, [(R_ROWS, NL)], af, bf)
    g2 = keep(lax.all_gather(r2, "gx", axis_index_groups=groups))
    return tuple(main_call(*wide, an, am, af, bf, g2)[:2])


def solution(mesh):
    wide, flat = P(None, "gx", "gy", None), P("gx", "gy", None)
    return jax.shard_map(
        on_device,
        mesh=mesh,
        in_specs=(wide,) * 4 + (flat,) * 10,
        out_specs=(wide, wide),
        check_vma=False,
    )
```

```python
import jax
import jax.numpy as jnp
import numpy as np
from jax import lax
from jax.experimental import pallas as pl
from jax.experimental.pallas import tpu as pltpu
from jax.sharding import PartitionSpec as P


DT2 = 0.0625
NL = 128
Y_ROWS, A_ROWS, C_ROWS, R_ROWS, O_ROWS = 328, 664, 400, 24, 8
YB, YW, YC, YD, YT = 128, 208, 216, 280, 320
AB, AC, AD, AT = 256, 448, 576, 656
CB_, CW, CC, CD, CT, CS = 64, 84, 88, 152, 192, 200
F32 = jnp.float32


def vertical_matrix():
    m = np.zeros((NL, NL))
    for k in range(2, NL - 2):
        m[k, k - 2], m[k, k - 1], m[k, k + 1], m[k, k + 2] = 1, -8, 8, -1
    m[0, 0:3] = -18, 24, -6
    m[1, 0], m[1, 2] = -6, 6
    m[NL - 2, NL - 3], m[NL - 2, NL - 1] = -6, 6
    m[NL - 1, NL - 3 :] = 6, -24, 18
    return np.concatenate([m.T, m.T], 0)


class Joined:
    def __init__(self, one, two):
        self.one, self.two = one, two

    def at(self, s):
        if s.stop <= AB:
            return self.one, s
        return self.two, slice(s.start - AB, s.stop - AB)

    def __getitem__(self, s):
        ref, s = self.at(s)
        return ref[s]

    def __setitem__(self, s, v):
        ref, s = self.at(s)
        ref[s] = v


def odd(axis):
    return lax.axis_index(axis) % 2


def rows(v):
    return v.reshape(-1, NL)


def tops_of(groups, first_slot=0):
    lane = lax.broadcasted_iota(jnp.int32, (8, NL), 1)
    acc = jnp.zeros((8, NL), F32)
    for k, v in enumerate(groups, first_slot):
        acc = jnp.where(lane // 8 == k, pltpu.roll(v, (8 * k + 8) % NL, 1), acc)
    return acc


def top_of(packed, slot):
    lane = lax.broadcasted_iota(jnp.int32, (8, NL), 1)
    return jnp.where(lane >= NL - 8, pltpu.roll(packed, (NL - 8 - 8 * slot) % NL, 1), 0.0)


def one_hot_rows(index, weight):
    lane = lax.broadcasted_iota(jnp.int32, (index.shape[0], NL), 1)
    slot = index + 2 + 4 * ((index * 171) >> 11)
    acc = jnp.zeros((index.shape[0], NL), F32)
    for k in range(16):
        acc = acc + jnp.where(lane == slot[:, k : k + 1], weight[:, k : k + 1], 0.0)
    return acc


def y_edge(out, stage, low, fn, fp, fj, fo, cn, cp, cj, co, edge):
    for i in range(4):
        for x in range(8):
            v = fn[i, x] if i < 3 else fj[x] * (1.0 / 12.0)
            out[i * 32 + x * 4 : i * 32 + x * 4 + 4] = v[0:4] if low else v[12:16]
    for i in range(5):
        for x in range(8):
            v = fp[i, x] if i < 3 else fo[i - 3, x]
            out[YB + i * 16 + x * 2 : YB + i * 16 + x * 2 + 2] = v[0:2] if low else v[14:16]
    for x in range(8):
        o = x * 4 if low else x * 4 + 2
        one, two = edge[o : o + 1], edge[o + 1 : o + 2]
        out[YW + x : YW + x + 1] = one + pltpu.roll(two, 8, 1) if low else pltpu.roll(one, NL - 8, 1) + two
    for i in range(4):
        for x in range(4):
            v = cn[i, x] if i < 3 else cj[x] * (1.0 / 12.0)
            out[YC + i * 16 + x * 4 : YC + i * 16 + x * 4 + 4] = v[0:4] if low else v[4:8]
            stage[i * 8 + x * 2 : i * 8 + x * 2 + 2] = v[4:6] if low else v[2:4]
    for i in range(5):
        for x in range(4):
            v = cp[i, x] if i < 3 else co[i - 3, x]
            out[YD + i * 8 + x * 2 : YD + i * 8 + x * 2 + 2] = v[0:2] if low else v[6:8]
            stage[32 + i * 8 + x * 2 : 32 + i * 8 + x * 2 + 2] = v[2:4] if low else v[4:6]
    out[YT:Y_ROWS] = tops_of([stage[k * 8 : k * 8 + 8] for k in range(9)])


def pack_y(*refs):
    inputs, kept, (fo, co, yf, yn, ro), rest = refs[:14], refs[14:22], refs[22:27], refs[27:]
    passing, (sems, stage, edge, edge_index, edge_weight) = rest[:6], rest[6:]
    local = list(passing)
    for place, ref in zip(KEPT, kept):
        local.insert(place, ref)
    copies = [pltpu.make_async_copy(i, v, sems.at[k]) for k, (i, v) in enumerate(zip(inputs, local))]
    for k in PACK_ORDER:
        copies[k].start()
    fn, fp, fr, fm, fl, fj, cn, cp, cr, cm, cl, cj, ix, wt = local
    for k in PACK_ORDER[:2]:
        copies[k].wait()
    for x in range(8):
        for o, y in ((0, 0), (2, 14)):
            edge_index[x * 4 + o : x * 4 + o + 2] = ix[x, y : y + 2]
            edge_weight[x * 4 + o : x * 4 + o + 2] = wt[x, y : y + 2]
    edge[...] = one_hot_rows(edge_index[...], edge_weight[...])
    for k in PACK_ORDER[2:]:
        copies[k].wait()
    inv = DT2 / fr[...]
    fo[0] = fm[...] * inv
    fo[1] = (fl[...] + fm[...]) * inv
    inv = DT2 / cr[...]
    co[0] = cm[...] * inv
    co[1] = (cl[...] + cm[...]) * inv
    oy = odd("gy")

    @pl.when(oy == 0)
    def _():
        y_edge(yf, stage, True, fn, fp, fj, fo, cn, cp, cj, co, edge)
        y_edge(yn, stage, False, fn, fp, fj, fo, cn, cp, cj, co, edge)

    @pl.when(oy == 1)
    def _():
        y_edge(yf, stage, False, fn, fp, fj, fo, cn, cp, cj, co, edge)
        y_edge(yn, stage, True, fn, fp, fj, fo, cn, cp, cj, co, edge)

    yf[Y_ROWS:] = jnp.zeros((8, NL), F32)
    x0 = 2 - 2 * odd("gx")
    ro[...] = tops_of([cn[i, x0 + x] if i < 3 else cj[x0 + x] * (1.0 / 12.0) for i in range(4) for x in range(2)])


def pack_x(fn, fp, fj, cn, cp, cj, ix, wt, fo, co, fe, fb, ce, cb, an, am, af):
    for half in (slice(0, 8), slice(16, 24)):
        ce[:, :, half] = jnp.zeros((4, 16, 8, NL), F32)
        cb[:, :, half] = jnp.zeros((5, 12, 8, NL), F32)
        fb[:, :, half] = jnp.zeros((6, 12, 8, NL), F32)
    mix = one_hot_rows(ix[...].reshape(128, 16), wt[...].reshape(128, 16))
    for x in range(8):
        fb[5, 2 + x, 4:20] = mix[x * 16 : x * 16 + 16]
    for x in range(8):
        for i in range(3):
            fe[i, 4 + x, 4:20] = fn[i, x]
            fb[i, 2 + x, 4:20] = fp[i, x]
        for i in range(2):
            fb[3 + i, 2 + x, 4:20] = fo[i, x]
        fe[3, 4 + x, 4:20] = fj[x] * (1.0 / 12.0)
    for x in range(4):
        for i in range(3):
            ce[i, 6 + x, 8:16] = cn[i, x]
            cb[i, 4 + x, 8:16] = cp[i, x]
        for i in range(2):
            cb[3 + i, 4 + x, 8:16] = co[i, x]
        ce[3, 6 + x, 8:16] = cj[x] * (1.0 / 12.0)
    near = Joined(an, am)

    def x_edge(out, low):
        x0 = 4 if low else 8
        for i in range(4):
            out[i * 64 : i * 64 + 64] = rows(fe[i, x0 : x0 + 4, 4:20])
        x0 = 2 if low else 8
        for i in range(6):
            out[AB + i * 32 : AB + i * 32 + 32] = rows(fb[i, x0 : x0 + 2, 4:20])
        for i in range(4):
            out[AC + i * 32 : AC + i * 32 + 32] = rows(ce[i, 6:10, 8:16])
        x0, x1 = (4, 6) if low else (6, 4)
        for i in range(5):
            out[AD + i * 16 : AD + i * 16 + 16] = rows(cb[i, x0 : x0 + 2, 8:16])
        out[AT:A_ROWS] = tops_of([cb[i, x1 + x, 8:16] for i in range(5) for x in range(2)])

    ox = odd("gx")

    @pl.when(ox == 0)
    def _():
        x_edge(near, False)
        x_edge(af, True)

    @pl.when(ox == 1)
    def _():
        x_edge(near, True)
        x_edge(af, False)


def pack_corner(src, out, base, low):
    for i in range(4):
        o = i * 32 + (0 if low else 16)
        out[base + i * 16 : base + i * 16 + 16] = src[o : o + 16]
    for i in range(5):
        o = YB + i * 16 + (0 if low else 12)
        out[base + CB_ + i * 4 : base + CB_ + i * 4 + 4] = src[o : o + 4]
    o = YW + (0 if low else 6)
    out[base + CW : base + CC] = jnp.concatenate([src[o : o + 2]] * 2, 0)
    out[base + CC : base + CS] = src[YC:Y_ROWS]


def pack_near(rn, rf, ro, out):
    out[C_ROWS : C_ROWS + O_ROWS] = ro[...]
    ox = odd("gx")

    @pl.when(ox == 0)
    def _():
        pack_corner(rn, out, 0, False)
        pack_corner(rf, out, CS, False)

    @pl.when(ox == 1)
    def _():
        pack_corner(rn, out, 0, True)
        pack_corner(rf, out, CS, True)


def pack_relay(own, c, out, base, x0):
    corners = [c[o : o + 8] for s in range(2) for i in range(4) for o in [s * CS + CC + i * 16 + x0 * 4]]
    out[base : base + 8] = own + tops_of(corners, 8)
    out[base + 8 : base + 16] = c[CT:CS]
    out[base + 16 : base + 24] = c[CS + CT : 2 * CS]


def pack_far(rn, rf, c, out):
    ox = odd("gx")

    @pl.when(ox == 0)
    def _():
        pack_corner(rn, out, 0, True)
        pack_corner(rf, out, CS, True)
        pack_relay(c[1, C_ROWS : C_ROWS + 8], c.at[1], out, C_ROWS, 0)

    @pl.when(ox == 1)
    def _():
        pack_corner(rn, out, 0, False)
        pack_corner(rf, out, CS, False)
        pack_relay(c[0, C_ROWS : C_ROWS + 8], c.at[0], out, C_ROWS, 2)


def pack_second(a, c, out):
    ox = odd("gx")

    def facing(x0):
        own = [a[o : o + 8] for i in range(4) for x in range(2) for o in [AC + i * 32 + (x0 + x) * 8]]
        pack_relay(tops_of(own), c, out, 0, x0)

    @pl.when(ox == 0)
    def _():
        facing(2)

    @pl.when(ox == 1)
    def _():
        facing(0)


def vertical(v, table):
    hi = v.astype(jnp.bfloat16)
    lo = (v - hi.astype(F32)).astype(jnp.bfloat16)
    return jnp.dot(jnp.concatenate([hi, lo], 1), table, preferred_element_type=F32)


def first(m2, m1, p1, p2, scale):
    return (m2 - p2) * (scale / 12.0) + (p1 - m1) * (scale * 8.0 / 12.0)


def second(m2, m1, c, p1, p2, scale):
    return (m1 + p1) * (scale * 16.0 / 12.0) - (m2 + p2) * (scale / 12.0) - c * (scale * 2.5)


def shifted(v):
    return [pltpu.roll(v, s % 24, 0) for s in (2, 1, -1, -2)]


def advance(n, u, j, prev, a, b, lift, work, table, spacing, store):
    s1, s2 = 1.0 / spacing, 1.0 / (spacing * spacing)
    half = (n + 4) // 2
    for x0 in (0, half):
        g = vertical(rows(u(2, x0, half)), table)
        lift[x0 : x0 + half] = (rows(j(x0, half)) * g).reshape(half, 24, NL)
    for c in range(2):
        g = vertical(rows(u(c, 2, n)), table)
        work[c, 0:n] = (rows(j(2, n)) * g).reshape(n, 24, NL)
    for x in range(n):
        f0 = [u(0, x + k, None) for k in (0, 1, 3, 4)]
        t = first(*f0, s1) + lift[x + 2]
        v = u(1, x + 2, None)
        m2, m1, p1, p2 = shifted(v)
        work[3, x] = t + first(m2, m1, p1, p2, s1)
        yy1 = second(m2, m1, v, p1, p2, s2)
        work[4, x] = yy1
        work[5, x] = yy1 + first(*shifted(t), s1)
    work[2, 0:n] = lift[2 : 2 + n]
    for c in range(4):
        g = vertical(rows(work[c, 0:n]), table)
        work[c, 0:n] = (rows(j(2, n)) * g).reshape(n, 24, NL)
    for x in range(n):
        col = [[u(c, x + k, None) for k in range(5)] for c in range(3)]
        lf = [lift[x + k] if k != 2 else None for k in range(5)]
        sh = [shifted(col[c][2]) if c != 1 else None for c in range(3)]
        xx = [second(*col[c], s2) for c in range(3)]
        yy = [
            second(sh[c][0], sh[c][1], col[c][2], sh[c][2], sh[c][3], s2) if c != 1 else work[4, x] for c in range(3)
        ]
        dx1 = first(col[1][0], col[1][1], col[1][3], col[1][4], s1)
        g0 = xx[0] + first(*shifted(dx1), s1) + first(lf[0], lf[1], lf[3], lf[4], s1)
        g1 = work[5, x]
        g2 = work[3, x]
        av, bv = a(x), b(x)
        for c, g in enumerate((g0, g1, g2)):
            lap = xx[c] + yy[c] + work[c, x]
            store(c, x, 2.0 * col[c][2] - prev(c, x) + av * lap + bv * g)


def bases(high):
    return (
        jnp.where(high, 12, 0), jnp.where(high, 10, 0), jnp.where(high, 10, 2), jnp.where(high, 14, 0),
        jnp.where(high, 8, 0), jnp.where(high, 8, 2), jnp.where(high, 10, 0),
    )


def y_places(high):
    return (20, 20, 16, 20, 16, 18) if high else (0, 2, 4, 2, 6, 4)


def mixing_rows(row, high):
    first_half = lax.broadcasted_iota(jnp.int32, (1, NL), 1) % 16 < 8
    one, two = jnp.where(first_half, row, 0.0), jnp.where(first_half, 0.0, row)
    if high:
        return pltpu.roll(one, 8, 1), two
    return one, pltpu.roll(two, NL - 8, 1)


def unpack_y(src, high, fe, fb, ce, cb):
    t4, t2, k4, k2, k1, k3 = y_places(high)
    top = src[YT:Y_ROWS]
    for i in range(4):
        for x in range(8):
            fe[i, 4 + x, t4 : t4 + 4] = src[i * 32 + x * 4 : i * 32 + x * 4 + 4]
        v = top_of(top, i)
        for x in range(4):
            o = YC + i * 16 + x * 4
            ce[i, 6 + x, k4 : k4 + 4] = src[o : o + 4]
            ce[i, 6 + x, k2 : k2 + 2] = v[x * 2 : x * 2 + 2]
    for x in range(8):
        for i in range(5):
            o = YB + i * 16 + x * 2
            fb[i, 2 + x, t2 : t2 + 2] = src[o : o + 2]
        for y, v in enumerate(mixing_rows(src[YW + x : YW + x + 1], high)):
            fb[5, 2 + x, t2 + y : t2 + y + 1] = v
    for i in range(5):
        v = top_of(top, 4 + i)
        for x in range(4):
            o = YD + i * 8 + x * 2
            cb[i, 4 + x, k1 : k1 + 2] = src[o : o + 2]
            cb[i, 4 + x, k3 : k3 + 2] = v[x * 2 : x * 2 + 2]


def unpack_corner(c, s, hx, high, fe, fb, ce, cb):
    t4, t2, k4, k2, k1, k3 = y_places(high)
    f4, f2, c4, _, b4, _, _ = bases(hx)
    q = s * CS
    top = c[q + CT : q + CS]
    for i in range(4):
        v = top_of(top, i)
        for x in range(4):
            o = q + i * 16 + x * 4
            fe[i, f4 + x, t4 : t4 + 4] = c[o : o + 4]
            o = q + CC + i * 16 + x * 4
            ce[i, c4 + x, k4 : k4 + 4] = c[o : o + 4]
            ce[i, c4 + x, k2 : k2 + 2] = v[x * 2 : x * 2 + 2]
    for x in range(2):
        for i in range(5):
            o = q + CB_ + i * 4 + x * 2
            fb[i, f2 + x, t2 : t2 + 2] = c[o : o + 2]
        for y, v in enumerate(mixing_rows(c[q + CW + x : q + CW + x + 1], high)):
            fb[5, f2 + x, t2 + y : t2 + y + 1] = v
    for i in range(5):
        v = top_of(top, 4 + i)
        for x in range(4):
            o = q + CD + i * 8 + x * 2
            cb[i, b4 + x, k1 : k1 + 2] = c[o : o + 2]
            cb[i, b4 + x, k3 : k3 + 2] = v[x * 2 : x * 2 + 2]


def unpack_x(a, hx, fe, fb, ce, cb):
    f4, f2, c4, _, _, b2, b4 = bases(hx)
    top = a[AT:A_ROWS]
    for i in range(4):
        for x in range(4):
            fe[i, f4 + x, 4:20] = a[i * 64 + x * 16 : i * 64 + x * 16 + 16]
            ce[i, c4 + x, 8:16] = a[AC + i * 32 + x * 8 : AC + i * 32 + x * 8 + 8]
    for i in range(6):
        for x in range(2):
            fb[i, f2 + x, 4:20] = a[AB + i * 32 + x * 16 : AB + i * 32 + x * 16 + 16]
    for i in range(5):
        for x in range(2):
            cb[i, b2 + x, 8:16] = a[AD + i * 16 + x * 8 : AD + i * 16 + x * 8 + 8]
            cb[i, b4 + x, 8:16] = top_of(top, i * 2 + x)


def unpack_relay(r, base, hx, near_high, ce):
    c2 = bases(hx)[3]
    beyond = r[base : base + 8]
    for i in range(4):
        for x in range(2):
            ce[i, c2 + x, 8:16] = top_of(beyond, i * 2 + x)
        for s, high in ((0, near_high), (1, not near_high)):
            _, _, k4, k2, _, _ = y_places(high)
            v = top_of(beyond, 8 + s * 4 + i)
            w = top_of(r[base + 8 + s * 8 : base + 16 + s * 8], i)
            w = jnp.where(hx, w, pltpu.roll(w, 4, 0))
            for x in range(2):
                ce[i, c2 + x, k4 : k4 + 4] = v[x * 4 : x * 4 + 4]
                ce[i, c2 + x, k2 : k2 + 2] = w[x * 2 : x * 2 + 2]


def fill(_, __, ___, ____, yn, yf, gn, _____, fe, fb, ce, cb):
    ox, oy = odd("gx"), odd("gy")
    c, hx = gn.at[1 - ox], ox == 0

    def sides(near_high):
        for s, src, high in ((0, yn, near_high), (1, yf, not near_high)):
            unpack_y(src, high, fe, fb, ce, cb)
            unpack_corner(c, s, hx, high, fe, fb, ce, cb)

    @pl.when(oy == 0)
    def _():
        sides(True)

    @pl.when(oy == 1)
    def _():
        sides(False)


def main(
    _, __, ___, ____, an, am, af, bf, g2, table_ref,
    fine_out, coarse_out, fe, fb, ce, cb, f1, c1, lift, work, tops, face,
):
    ox, oy = odd("gx"), odd("gy")
    near, far = ox == 0, ox == 1
    unpack_x(Joined(an, am), near, fe, fb, ce, cb)
    unpack_x(af, far, fe, fb, ce, cb)

    def sides(near_high):
        for s, high in ((0, near_high), (1, not near_high)):
            unpack_corner(bf, s, far, high, fe, fb, ce, cb)
        unpack_relay(bf, C_ROWS, far, near_high, ce)
        unpack_relay(g2.at[1 - ox], 0, near, near_high, ce)

    @pl.when(oy == 0)
    def _():
        sides(True)

    @pl.when(oy == 1)
    def _():
        sides(False)

    table = table_ref[...]
    lane = lax.broadcasted_iota(jnp.int32, (24, NL), 1)

    def view(ref, i, off):
        def get(x, count):
            return ref[i, x + off] if count is None else ref[i, x + off : x + off + count]

        return get

    def views(ref, off):
        def get(i, x, count=None):
            return view(ref, i, off)(x, count)

        return get

    def gather_top(src, n, t0):
        for x in range(n):
            v = jnp.where(lane == 0, pltpu.roll(src[0, x], 1, 1), 0.0)
            v = jnp.where(lane == 1, pltpu.roll(src[1, x], 2, 1), v)
            v = jnp.where(lane == 2, pltpu.roll(src[2, x], 3, 1), v)
            tops[t0 + x] = v[4:20]

    def mixed(x0, n, t0):
        w = rows(fb[5, x0 : x0 + n])
        plane = tops[t0 : t0 + 8].reshape(128, NL)
        return jnp.dot(w, plane, precision=lax.Precision.HIGHEST, preferred_element_type=F32).reshape(n, 24, NL)

    def with_face(c, x, v):
        return jnp.where(lane == 0, pltpu.roll(face[x], (NL - c) % NL, 1), v)

    tops[0:2] = jnp.zeros((2, 16, NL), F32)
    tops[14:16] = jnp.zeros((2, 16, NL), F32)

    def store_c1(c, x, v):
        c1[c, x] = v

    advance(12, views(ce, 0), view(ce, 3, 0), views(cb, 0), view_row(cb, 3, 0), view_row(cb, 4, 0),
            lift, work, table, 2.0, store_c1)
    gather_top(c1, 12, 2)
    face[0:2] = mixed(0, 2, 0)
    face[2:10] = mixed(2, 8, 4)
    face[10:12] = mixed(10, 2, 8)

    def store_f1(c, x, v):
        f1[c, x] = with_face(c, x, v)

    advance(12, views(fe, 0), view(fe, 3, 0), views(fb, 0), view_row(fb, 3, 0), view_row(fb, 4, 0),
            lift, work, table, 1.0, store_f1)

    def store_c2(c, x, v):
        cb[c, x] = v
        if 2 <= x < 6:
            coarse_out[c, x - 2] = v[8:16]

    advance(8, views(c1, 0), view(ce, 3, 2), views(ce, 4), view_row(cb, 3, 2), view_row(cb, 4, 2),
            lift, work, table, 2.0, store_c2)
    gather_top(cb, 8, 4)
    face[0:8] = mixed(2, 8, 4)

    def store_f2(c, x, v):
        fine_out[c, x] = with_face(c, x, v)[4:20]

    advance(8, views(f1, 0), view(fe, 3, 2), views(fe, 4), view_row(fb, 3, 2), view_row(fb, 4, 2),
            lift, work, table, 1.0, store_f2)


def view_row(ref, i, off):
    def get(x):
        return ref[i, x + off]

    return get


def pairs(size, start):
    out = []
    for i in range(start, size - 1, 2):
        out += [(i, i + 1), (i + 1, i)]
    return out


INTERPRET = False


def call(body, shapes, *operands, scratch=(), local=True, alias={}):
    vmem = pl.BlockSpec(memory_space=pltpu.VMEM)
    away = 0 if local else 2
    return pl.pallas_call(
        body,
        out_shape=[jax.ShapeDtypeStruct(s, F32) if k < away else pltpu.VMEM(s, F32) for k, s in enumerate(shapes)],
        in_specs=[vmem] * len(operands),
        out_specs=[vmem] * len(shapes),
        scratch_shapes=[pltpu.VMEM(s, F32) for s in scratch],
        input_output_aliases=alias,
        compiler_params=pltpu.CompilerParams(vmem_limit_bytes=56 << 20),
        interpret=INTERPRET,
    )(*operands)


def keep(v):
    return v if INTERPRET else pltpu.with_memory_space_constraint(v, pltpu.VMEM)


PACK_ORDER = (12, 13, 0, 1, 5, 2, 3, 4, 6, 7, 11, 8, 9, 10)


KEPT = (0, 1, 5, 6, 7, 11, 12, 13)
BLOCKS = [(4, 16, 24, NL), (6, 12, 24, NL), (4, 16, 24, NL), (5, 12, 24, NL)]


def pack_call(*operands):
    shapes = [(2, 8, 16, NL), (2, 4, 8, NL), (Y_ROWS + 8, NL), (Y_ROWS, NL), (O_ROWS, NL)]
    return pl.pallas_call(
        pack_y,
        out_shape=[pltpu.VMEM(operands[k].shape, operands[k].dtype) for k in KEPT] + [pltpu.VMEM(s, F32) for s in shapes],
        in_specs=[pl.BlockSpec(memory_space=pl.ANY)] * len(operands),
        out_specs=[pl.BlockSpec(memory_space=pltpu.VMEM)] * (len(KEPT) + len(shapes)),
        scratch_shapes=[pltpu.VMEM(o.shape, o.dtype) for k, o in enumerate(operands) if k not in KEPT]
        + [pltpu.SemaphoreType.DMA((len(operands),)), pltpu.VMEM((72, NL), F32)]
        + [pltpu.VMEM((32, NL), F32), pltpu.VMEM((32, 16), jnp.int32), pltpu.VMEM((32, 16), F32)],
        compiler_params=pltpu.CompilerParams(vmem_limit_bytes=56 << 20),
        interpret=INTERPRET,
    )(*operands)


def main_call(*operands):
    return call(
        main,
        [(3, 8, 16, NL), (3, 4, 8, NL)] + BLOCKS,
        *operands,
        keep(jnp.asarray(vertical_matrix(), jnp.bfloat16)),
        local=False,
        alias={0: 2, 1: 3, 2: 4, 3: 5},
        scratch=[(3, 12, 24, NL), (3, 12, 24, NL), (16, 24, NL), (6, 12, 24, NL), (16, 16, NL), (12, 24, NL)],
    )


def on_device(
    fine_now, fine_prev, coarse_now, coarse_prev, fine_rho, fine_mu, fine_lam, fine_metric,
    coarse_rho, coarse_mu, coarse_lam, coarse_metric, couple_index, couple_weight,
):
    gx, gy = lax.axis_size("gx"), lax.axis_size("gy")
    near_x, far_x, near_y, far_y = pairs(gx, 0), pairs(gx, 1), pairs(gy, 0), pairs(gy, 1)
    groups = [[i, i + 1] for i in range(0, gx, 2)]

    *own, yf, yn, ro = pack_call(
        fine_now, fine_prev, fine_rho, fine_mu, fine_lam, fine_metric,
        coarse_now, coarse_prev, coarse_rho, coarse_mu, coarse_lam, coarse_metric,
        couple_index, couple_weight,
    )
    own, ro = [keep(w) for w in own], keep(ro)
    yf = keep(lax.ppermute(yf, "gy", far_y))
    yn = keep(lax.ppermute(yn, "gy", near_y))
    *wide, an, am, af = call(pack_x, BLOCKS + [(AB, NL), (A_ROWS - AB, NL), (A_ROWS, NL)], *own)
    wide = [keep(w) for w in wide]
    af = keep(lax.ppermute(af, "gx", far_x))
    an = keep(lax.ppermute(an, "gx", near_x))
    am = keep(lax.ppermute(am, "gx", near_x))
    (cn,) = call(pack_near, [(C_ROWS + O_ROWS, NL)], yn, yf, ro)
    gn = keep(lax.all_gather(cn, "gx", axis_index_groups=groups))
    (bp,) = call(pack_far, [(C_ROWS + R_ROWS, NL)], yn, yf, gn)
    bp = keep(bp)
    bf = keep(lax.ppermute(bp, "gx", far_x))
    wide = call(fill, BLOCKS, *wide, yn, yf, gn, bp, alias={0: 0, 1: 1, 2: 2, 3: 3})
    wide = [keep(w) for w in wide]
    (r2,) = call(pack_second, [(R_ROWS, NL)], af, bf)
    g2 = keep(lax.all_gather(r2, "gx", axis_index_groups=groups))
    return tuple(main_call(*wide, an, am, af, bf, g2)[:2])


def solution(mesh):
    wide, flat = P(None, "gx", "gy", None), P("gx", "gy", None)
    return jax.shard_map(
        on_device,
        mesh=mesh,
        in_specs=(wide,) * 4 + (flat,) * 10,
        out_specs=(wide, wide),
        check_vma=False,
    )
```

```python
import jax
import jax.numpy as jnp
import numpy as np
from jax import lax
from jax.experimental import pallas as pl
from jax.experimental.pallas import tpu as pltpu
from jax.sharding import PartitionSpec as P


DT2 = 0.0625
NL = 128
Y_ROWS, A_ROWS, C_ROWS, R_ROWS, O_ROWS = 328, 664, 400, 24, 8
YB, YW, YC, YD, YT = 128, 208, 216, 280, 320
AB, AC, AD, AT = 256, 448, 576, 656
CB_, CW, CC, CD, CT, CS = 64, 84, 88, 152, 192, 200
F32 = jnp.float32


def vertical_matrix():
    m = np.zeros((NL, NL))
    for k in range(2, NL - 2):
        m[k, k - 2], m[k, k - 1], m[k, k + 1], m[k, k + 2] = 1, -8, 8, -1
    m[0, 0:3] = -18, 24, -6
    m[1, 0], m[1, 2] = -6, 6
    m[NL - 2, NL - 3], m[NL - 2, NL - 1] = -6, 6
    m[NL - 1, NL - 3 :] = 6, -24, 18
    return np.concatenate([m.T, m.T], 0)


class Joined:
    def __init__(self, one, two):
        self.one, self.two = one, two

    def at(self, s):
        if s.stop <= AB:
            return self.one, s
        return self.two, slice(s.start - AB, s.stop - AB)

    def __getitem__(self, s):
        ref, s = self.at(s)
        return ref[s]

    def __setitem__(self, s, v):
        ref, s = self.at(s)
        ref[s] = v


def odd(axis):
    return lax.axis_index(axis) % 2


def rows(v):
    return v.reshape(-1, NL)


def tops_of(groups, first_slot=0):
    lane = lax.broadcasted_iota(jnp.int32, (8, NL), 1)
    acc = jnp.zeros((8, NL), F32)
    for k, v in enumerate(groups, first_slot):
        acc = jnp.where(lane // 8 == k, pltpu.roll(v, (8 * k + 8) % NL, 1), acc)
    return acc


def top_of(packed, slot):
    lane = lax.broadcasted_iota(jnp.int32, (8, NL), 1)
    return jnp.where(lane >= NL - 8, pltpu.roll(packed, (NL - 8 - 8 * slot) % NL, 1), 0.0)


def one_hot_rows(index, weight):
    lane = lax.broadcasted_iota(jnp.int32, (index.shape[0], NL), 1)
    slot = index + 2 + 4 * ((index * 171) >> 11)
    acc = jnp.zeros((index.shape[0], NL), F32)
    for k in range(16):
        acc = acc + jnp.where(lane == slot[:, k : k + 1], weight[:, k : k + 1], 0.0)
    return acc


def y_edge(out, stage, low, fn, fp, fj, fo, cn, cp, cj, co, edge):
    for i in range(4):
        for x in range(8):
            v = fn[i, x] if i < 3 else fj[x] * (1.0 / 12.0)
            out[i * 32 + x * 4 : i * 32 + x * 4 + 4] = v[0:4] if low else v[12:16]
    for i in range(5):
        for x in range(8):
            v = fp[i, x] if i < 3 else fo[i - 3, x]
            out[YB + i * 16 + x * 2 : YB + i * 16 + x * 2 + 2] = v[0:2] if low else v[14:16]
    for x in range(8):
        o = x * 4 if low else x * 4 + 2
        one, two = edge[o : o + 1], edge[o + 1 : o + 2]
        out[YW + x : YW + x + 1] = one + pltpu.roll(two, 8, 1) if low else pltpu.roll(one, NL - 8, 1) + two
    for i in range(4):
        for x in range(4):
            v = cn[i, x] if i < 3 else cj[x] * (1.0 / 12.0)
            out[YC + i * 16 + x * 4 : YC + i * 16 + x * 4 + 4] = v[0:4] if low else v[4:8]
            stage[i * 8 + x * 2 : i * 8 + x * 2 + 2] = v[4:6] if low else v[2:4]
    for i in range(5):
        for x in range(4):
            v = cp[i, x] if i < 3 else co[i - 3, x]
            out[YD + i * 8 + x * 2 : YD + i * 8 + x * 2 + 2] = v[0:2] if low else v[6:8]
            stage[32 + i * 8 + x * 2 : 32 + i * 8 + x * 2 + 2] = v[2:4] if low else v[4:6]
    out[YT:Y_ROWS] = tops_of([stage[k * 8 : k * 8 + 8] for k in range(9)])


def pack_y(*refs):
    inputs, kept, (fo, co, yf, yn, ro), rest = refs[:14], refs[14:22], refs[22:27], refs[27:]
    passing, (sems, stage, edge, edge_index, edge_weight) = rest[:6], rest[6:]
    local = list(passing)
    for place, ref in zip(KEPT, kept):
        local.insert(place, ref)
    copies = [pltpu.make_async_copy(i, v, sems.at[k]) for k, (i, v) in enumerate(zip(inputs, local))]
    for k in PACK_ORDER:
        copies[k].start()
    fn, fp, fr, fm, fl, fj, cn, cp, cr, cm, cl, cj, ix, wt = local
    for k in PACK_ORDER[:2]:
        copies[k].wait()
    for x in range(8):
        for o, y in ((0, 0), (2, 14)):
            edge_index[x * 4 + o : x * 4 + o + 2] = ix[x, y : y + 2]
            edge_weight[x * 4 + o : x * 4 + o + 2] = wt[x, y : y + 2]
    edge[...] = one_hot_rows(edge_index[...], edge_weight[...])
    for k in PACK_ORDER[2:]:
        copies[k].wait()
    inv = DT2 / fr[...]
    fo[0] = fm[...] * inv
    fo[1] = (fl[...] + fm[...]) * inv
    inv = DT2 / cr[...]
    co[0] = cm[...] * inv
    co[1] = (cl[...] + cm[...]) * inv
    oy = odd("gy")

    @pl.when(oy == 0)
    def _():
        y_edge(yf, stage, True, fn, fp, fj, fo, cn, cp, cj, co, edge)
        y_edge(yn, stage, False, fn, fp, fj, fo, cn, cp, cj, co, edge)

    @pl.when(oy == 1)
    def _():
        y_edge(yf, stage, False, fn, fp, fj, fo, cn, cp, cj, co, edge)
        y_edge(yn, stage, True, fn, fp, fj, fo, cn, cp, cj, co, edge)

    yf[Y_ROWS:] = jnp.zeros((8, NL), F32)
    x0 = 2 - 2 * odd("gx")
    ro[...] = tops_of([cn[i, x0 + x] if i < 3 else cj[x0 + x] * (1.0 / 12.0) for i in range(4) for x in range(2)])


def pack_x(fn, fp, fj, cn, cp, cj, ix, wt, fo, co, fe, fb, ce, cb, an, am, af):
    for half in (slice(0, 8), slice(16, 24)):
        ce[:, :, half] = jnp.zeros((4, 16, 8, NL), F32)
        cb[:, :, half] = jnp.zeros((5, 12, 8, NL), F32)
        fb[:, :, half] = jnp.zeros((6, 12, 8, NL), F32)
    mix = one_hot_rows(ix[...].reshape(128, 16), wt[...].reshape(128, 16))
    for x in range(8):
        fb[5, 2 + x, 4:20] = mix[x * 16 : x * 16 + 16]
    for x in range(8):
        for i in range(3):
            fe[i, 4 + x, 4:20] = fn[i, x]
            fb[i, 2 + x, 4:20] = fp[i, x]
        for i in range(2):
            fb[3 + i, 2 + x, 4:20] = fo[i, x]
        fe[3, 4 + x, 4:20] = fj[x] * (1.0 / 12.0)
    for x in range(4):
        for i in range(3):
            ce[i, 6 + x, 8:16] = cn[i, x]
            cb[i, 4 + x, 8:16] = cp[i, x]
        for i in range(2):
            cb[3 + i, 4 + x, 8:16] = co[i, x]
        ce[3, 6 + x, 8:16] = cj[x] * (1.0 / 12.0)
    near = Joined(an, am)

    def x_edge(out, low):
        x0 = 4 if low else 8
        for i in range(4):
            out[i * 64 : i * 64 + 64] = rows(fe[i, x0 : x0 + 4, 4:20])
        x0 = 2 if low else 8
        for i in range(6):
            out[AB + i * 32 : AB + i * 32 + 32] = rows(fb[i, x0 : x0 + 2, 4:20])
        for i in range(4):
            out[AC + i * 32 : AC + i * 32 + 32] = rows(ce[i, 6:10, 8:16])
        x0, x1 = (4, 6) if low else (6, 4)
        for i in range(5):
            out[AD + i * 16 : AD + i * 16 + 16] = rows(cb[i, x0 : x0 + 2, 8:16])
        out[AT:A_ROWS] = tops_of([cb[i, x1 + x, 8:16] for i in range(5) for x in range(2)])

    ox = odd("gx")

    @pl.when(ox == 0)
    def _():
        x_edge(near, False)
        x_edge(af, True)

    @pl.when(ox == 1)
    def _():
        x_edge(near, True)
        x_edge(af, False)


def pack_corner(src, out, base, low):
    for i in range(4):
        o = i * 32 + (0 if low else 16)
        out[base + i * 16 : base + i * 16 + 16] = src[o : o + 16]
    for i in range(5):
        o = YB + i * 16 + (0 if low else 12)
        out[base + CB_ + i * 4 : base + CB_ + i * 4 + 4] = src[o : o + 4]
    o = YW + (0 if low else 6)
    out[base + CW : base + CC] = jnp.concatenate([src[o : o + 2]] * 2, 0)
    out[base + CC : base + CS] = src[YC:Y_ROWS]


def pack_near(rn, rf, ro, out):
    out[C_ROWS : C_ROWS + O_ROWS] = ro[...]
    ox = odd("gx")

    @pl.when(ox == 0)
    def _():
        pack_corner(rn, out, 0, False)
        pack_corner(rf, out, CS, False)

    @pl.when(ox == 1)
    def _():
        pack_corner(rn, out, 0, True)
        pack_corner(rf, out, CS, True)


def pack_relay(own, c, out, base, x0):
    corners = [c[o : o + 8] for s in range(2) for i in range(4) for o in [s * CS + CC + i * 16 + x0 * 4]]
    out[base : base + 8] = own + tops_of(corners, 8)
    out[base + 8 : base + 16] = c[CT:CS]
    out[base + 16 : base + 24] = c[CS + CT : 2 * CS]


def pack_far(rn, rf, c, out):
    ox = odd("gx")

    @pl.when(ox == 0)
    def _():
        pack_corner(rn, out, 0, True)
        pack_corner(rf, out, CS, True)
        pack_relay(c[1, C_ROWS : C_ROWS + 8], c.at[1], out, C_ROWS, 0)

    @pl.when(ox == 1)
    def _():
        pack_corner(rn, out, 0, False)
        pack_corner(rf, out, CS, False)
        pack_relay(c[0, C_ROWS : C_ROWS + 8], c.at[0], out, C_ROWS, 2)


def pack_second(a, c, out):
    ox = odd("gx")

    def facing(x0):
        own = [a[o : o + 8] for i in range(4) for x in range(2) for o in [AC + i * 32 + (x0 + x) * 8]]
        pack_relay(tops_of(own), c, out, 0, x0)

    @pl.when(ox == 0)
    def _():
        facing(2)

    @pl.when(ox == 1)
    def _():
        facing(0)


def vertical(v, table):
    hi = v.astype(jnp.bfloat16)
    lo = (v - hi.astype(F32)).astype(jnp.bfloat16)
    return jnp.dot(jnp.concatenate([hi, lo], 1), table, preferred_element_type=F32)


def first(m2, m1, p1, p2, scale):
    return (m2 - p2) * (scale / 12.0) + (p1 - m1) * (scale * 8.0 / 12.0)


def second(m2, m1, c, p1, p2, scale):
    return (m1 + p1) * (scale * 16.0 / 12.0) - (m2 + p2) * (scale / 12.0) - c * (scale * 2.5)


def shifted(v):
    return [pltpu.roll(v, s % 24, 0) for s in (2, 1, -1, -2)]


def advance(n, u, j, prev, a, b, lift, work, table, spacing, store):
    s1, s2 = 1.0 / spacing, 1.0 / (spacing * spacing)
    half = (n + 4) // 2
    for x0 in (0, half):
        g = vertical(rows(u(2, x0, half)), table)
        lift[x0 : x0 + half] = (rows(j(x0, half)) * g).reshape(half, 24, NL)
    for c in range(2):
        g = vertical(rows(u(c, 2, n)), table)
        work[c, 0:n] = (rows(j(2, n)) * g).reshape(n, 24, NL)
    for x in range(n):
        f0 = [u(0, x + k, None) for k in (0, 1, 3, 4)]
        t = first(*f0, s1) + lift[x + 2]
        v = u(1, x + 2, None)
        m2, m1, p1, p2 = shifted(v)
        work[3, x] = t + first(m2, m1, p1, p2, s1)
        yy1 = second(m2, m1, v, p1, p2, s2)
        work[4, x] = yy1
        work[5, x] = yy1 + first(*shifted(t), s1)
    for c in range(4):
        g = vertical(rows(lift[2 : 2 + n] if c == 2 else work[c, 0:n]), table)
        work[c, 0:n] = (rows(j(2, n)) * g).reshape(n, 24, NL)
    for x in range(n):
        col = [[u(c, x + k, None) for k in range(5)] for c in range(3)]
        lf = [lift[x + k] if k != 2 else None for k in range(5)]
        sh = [shifted(col[c][2]) if c != 1 else None for c in range(3)]
        xx = [second(*col[c], s2) for c in range(3)]
        yy = [
            second(sh[c][0], sh[c][1], col[c][2], sh[c][2], sh[c][3], s2) if c != 1 else work[4, x] for c in range(3)
        ]
        dx1 = first(col[1][0], col[1][1], col[1][3], col[1][4], s1)
        g0 = xx[0] + first(*shifted(dx1), s1) + first(lf[0], lf[1], lf[3], lf[4], s1)
        g1 = work[5, x]
        g2 = work[3, x]
        av, bv = a(x), b(x)
        for c, g in enumerate((g0, g1, g2)):
            lap = xx[c] + yy[c] + work[c, x]
            store(c, x, 2.0 * col[c][2] - prev(c, x) + av * lap + bv * g)


def bases(high):
    return (
        jnp.where(high, 12, 0), jnp.where(high, 10, 0), jnp.where(high, 10, 2), jnp.where(high, 14, 0),
        jnp.where(high, 8, 0), jnp.where(high, 8, 2), jnp.where(high, 10, 0),
    )


def y_places(high):
    return (20, 20, 16, 20, 16, 18) if high else (0, 2, 4, 2, 6, 4)


def mixing_rows(row, high):
    first_half = lax.broadcasted_iota(jnp.int32, (1, NL), 1) % 16 < 8
    one, two = jnp.where(first_half, row, 0.0), jnp.where(first_half, 0.0, row)
    if high:
        return pltpu.roll(one, 8, 1), two
    return one, pltpu.roll(two, NL - 8, 1)


def unpack_y(src, high, fe, fb, ce, cb):
    t4, t2, k4, k2, k1, k3 = y_places(high)
    top = src[YT:Y_ROWS]
    for i in range(4):
        for x in range(8):
            fe[i, 4 + x, t4 : t4 + 4] = src[i * 32 + x * 4 : i * 32 + x * 4 + 4]
        v = top_of(top, i)
        for x in range(4):
            o = YC + i * 16 + x * 4
            ce[i, 6 + x, k4 : k4 + 4] = src[o : o + 4]
            ce[i, 6 + x, k2 : k2 + 2] = v[x * 2 : x * 2 + 2]
    for x in range(8):
        for i in range(5):
            o = YB + i * 16 + x * 2
            fb[i, 2 + x, t2 : t2 + 2] = src[o : o + 2]
        for y, v in enumerate(mixing_rows(src[YW + x : YW + x + 1], high)):
            fb[5, 2 + x, t2 + y : t2 + y + 1] = v
    for i in range(5):
        v = top_of(top, 4 + i)
        for x in range(4):
            o = YD + i * 8 + x * 2
            cb[i, 4 + x, k1 : k1 + 2] = src[o : o + 2]
            cb[i, 4 + x, k3 : k3 + 2] = v[x * 2 : x * 2 + 2]


def unpack_corner(c, s, hx, high, fe, fb, ce, cb):
    t4, t2, k4, k2, k1, k3 = y_places(high)
    f4, f2, c4, _, b4, _, _ = bases(hx)
    q = s * CS
    top = c[q + CT : q + CS]
    for i in range(4):
        v = top_of(top, i)
        for x in range(4):
            o = q + i * 16 + x * 4
            fe[i, f4 + x, t4 : t4 + 4] = c[o : o + 4]
            o = q + CC + i * 16 + x * 4
            ce[i, c4 + x, k4 : k4 + 4] = c[o : o + 4]
            ce[i, c4 + x, k2 : k2 + 2] = v[x * 2 : x * 2 + 2]
    for x in range(2):
        for i in range(5):
            o = q + CB_ + i * 4 + x * 2
            fb[i, f2 + x, t2 : t2 + 2] = c[o : o + 2]
        for y, v in enumerate(mixing_rows(c[q + CW + x : q + CW + x + 1], high)):
            fb[5, f2 + x, t2 + y : t2 + y + 1] = v
    for i in range(5):
        v = top_of(top, 4 + i)
        for x in range(4):
            o = q + CD + i * 8 + x * 2
            cb[i, b4 + x, k1 : k1 + 2] = c[o : o + 2]
            cb[i, b4 + x, k3 : k3 + 2] = v[x * 2 : x * 2 + 2]


def unpack_x(a, hx, fe, fb, ce, cb):
    f4, f2, c4, _, _, b2, b4 = bases(hx)
    top = a[AT:A_ROWS]
    for i in range(4):
        for x in range(4):
            fe[i, f4 + x, 4:20] = a[i * 64 + x * 16 : i * 64 + x * 16 + 16]
            ce[i, c4 + x, 8:16] = a[AC + i * 32 + x * 8 : AC + i * 32 + x * 8 + 8]
    for i in range(6):
        for x in range(2):
            fb[i, f2 + x, 4:20] = a[AB + i * 32 + x * 16 : AB + i * 32 + x * 16 + 16]
    for i in range(5):
        for x in range(2):
            cb[i, b2 + x, 8:16] = a[AD + i * 16 + x * 8 : AD + i * 16 + x * 8 + 8]
            cb[i, b4 + x, 8:16] = top_of(top, i * 2 + x)


def unpack_relay(r, base, hx, near_high, ce):
    c2 = bases(hx)[3]
    beyond = r[base : base + 8]
    for i in range(4):
        for x in range(2):
            ce[i, c2 + x, 8:16] = top_of(beyond, i * 2 + x)
        for s, high in ((0, near_high), (1, not near_high)):
            _, _, k4, k2, _, _ = y_places(high)
            v = top_of(beyond, 8 + s * 4 + i)
            w = top_of(r[base + 8 + s * 8 : base + 16 + s * 8], i)
            w = jnp.where(hx, w, pltpu.roll(w, 4, 0))
            for x in range(2):
                ce[i, c2 + x, k4 : k4 + 4] = v[x * 4 : x * 4 + 4]
                ce[i, c2 + x, k2 : k2 + 2] = w[x * 2 : x * 2 + 2]


def fill(_, __, ___, ____, yn, yf, gn, _____, fe, fb, ce, cb):
    ox, oy = odd("gx"), odd("gy")
    c, hx = gn.at[1 - ox], ox == 0

    def sides(near_high):
        for s, src, high in ((0, yn, near_high), (1, yf, not near_high)):
            unpack_y(src, high, fe, fb, ce, cb)
            unpack_corner(c, s, hx, high, fe, fb, ce, cb)

    @pl.when(oy == 0)
    def _():
        sides(True)

    @pl.when(oy == 1)
    def _():
        sides(False)


def main(
    _, __, ___, ____, an, am, af, bf, g2, table_ref,
    fine_out, coarse_out, fe, fb, ce, cb, f1, c1, lift, work, tops, face,
):
    ox, oy = odd("gx"), odd("gy")
    near, far = ox == 0, ox == 1
    unpack_x(Joined(an, am), near, fe, fb, ce, cb)
    unpack_x(af, far, fe, fb, ce, cb)

    def sides(near_high):
        for s, high in ((0, near_high), (1, not near_high)):
            unpack_corner(bf, s, far, high, fe, fb, ce, cb)
        unpack_relay(bf, C_ROWS, far, near_high, ce)
        unpack_relay(g2.at[1 - ox], 0, near, near_high, ce)

    @pl.when(oy == 0)
    def _():
        sides(True)

    @pl.when(oy == 1)
    def _():
        sides(False)

    table = table_ref[...]
    lane = lax.broadcasted_iota(jnp.int32, (24, NL), 1)

    def view(ref, i, off):
        def get(x, count):
            return ref[i, x + off] if count is None else ref[i, x + off : x + off + count]

        return get

    def views(ref, off):
        def get(i, x, count=None):
            return view(ref, i, off)(x, count)

        return get

    def gather_top(src, n, t0):
        for x in range(n):
            v = jnp.where(lane == 0, pltpu.roll(src[0, x], 1, 1), 0.0)
            v = jnp.where(lane == 1, pltpu.roll(src[1, x], 2, 1), v)
            v = jnp.where(lane == 2, pltpu.roll(src[2, x], 3, 1), v)
            tops[t0 + x] = v[4:20]

    def mixed(x0, n, t0):
        w = rows(fb[5, x0 : x0 + n])
        plane = tops[t0 : t0 + 8].reshape(128, NL)
        return jnp.dot(w, plane, precision=lax.Precision.HIGHEST, preferred_element_type=F32).reshape(n, 24, NL)

    def with_face(c, x, v):
        return jnp.where(lane == 0, pltpu.roll(face[x], (NL - c) % NL, 1), v)

    tops[0:2] = jnp.zeros((2, 16, NL), F32)
    tops[14:16] = jnp.zeros((2, 16, NL), F32)

    def store_c1(c, x, v):
        c1[c, x] = v

    advance(12, views(ce, 0), view(ce, 3, 0), views(cb, 0), view_row(cb, 3, 0), view_row(cb, 4, 0),
            lift, work, table, 2.0, store_c1)
    gather_top(c1, 12, 2)
    face[0:2] = mixed(0, 2, 0)
    face[2:10] = mixed(2, 8, 4)
    face[10:12] = mixed(10, 2, 8)

    def store_f1(c, x, v):
        f1[c, x] = with_face(c, x, v)

    advance(12, views(fe, 0), view(fe, 3, 0), views(fb, 0), view_row(fb, 3, 0), view_row(fb, 4, 0),
            lift, work, table, 1.0, store_f1)

    def store_c2(c, x, v):
        cb[c, x] = v
        if 2 <= x < 6:
            coarse_out[c, x - 2] = v[8:16]

    advance(8, views(c1, 0), view(ce, 3, 2), views(ce, 4), view_row(cb, 3, 2), view_row(cb, 4, 2),
            lift, work, table, 2.0, store_c2)
    gather_top(cb, 8, 4)
    face[0:8] = mixed(2, 8, 4)

    def store_f2(c, x, v):
        fine_out[c, x] = with_face(c, x, v)[4:20]

    advance(8, views(f1, 0), view(fe, 3, 2), views(fe, 4), view_row(fb, 3, 2), view_row(fb, 4, 2),
            lift, work, table, 1.0, store_f2)


def view_row(ref, i, off):
    def get(x):
        return ref[i, x + off]

    return get


def pairs(size, start):
    out = []
    for i in range(start, size - 1, 2):
        out += [(i, i + 1), (i + 1, i)]
    return out


INTERPRET = False


def call(body, shapes, *operands, scratch=(), local=True, alias={}):
    vmem = pl.BlockSpec(memory_space=pltpu.VMEM)
    away = 0 if local else 2
    return pl.pallas_call(
        body,
        out_shape=[jax.ShapeDtypeStruct(s, F32) if k < away else pltpu.VMEM(s, F32) for k, s in enumerate(shapes)],
        in_specs=[vmem] * len(operands),
        out_specs=[vmem] * len(shapes),
        scratch_shapes=[pltpu.VMEM(s, F32) for s in scratch],
        input_output_aliases=alias,
        compiler_params=pltpu.CompilerParams(vmem_limit_bytes=56 << 20),
        interpret=INTERPRET,
    )(*operands)


def keep(v):
    return v if INTERPRET else pltpu.with_memory_space_constraint(v, pltpu.VMEM)


PACK_ORDER = (12, 13, 0, 1, 5, 2, 3, 4, 6, 7, 11, 8, 9, 10)


KEPT = (0, 1, 5, 6, 7, 11, 12, 13)
BLOCKS = [(4, 16, 24, NL), (6, 12, 24, NL), (4, 16, 24, NL), (5, 12, 24, NL)]


def pack_call(*operands):
    shapes = [(2, 8, 16, NL), (2, 4, 8, NL), (Y_ROWS + 8, NL), (Y_ROWS, NL), (O_ROWS, NL)]
    return pl.pallas_call(
        pack_y,
        out_shape=[pltpu.VMEM(operands[k].shape, operands[k].dtype) for k in KEPT] + [pltpu.VMEM(s, F32) for s in shapes],
        in_specs=[pl.BlockSpec(memory_space=pl.ANY)] * len(operands),
        out_specs=[pl.BlockSpec(memory_space=pltpu.VMEM)] * (len(KEPT) + len(shapes)),
        scratch_shapes=[pltpu.VMEM(o.shape, o.dtype) for k, o in enumerate(operands) if k not in KEPT]
        + [pltpu.SemaphoreType.DMA((len(operands),)), pltpu.VMEM((72, NL), F32)]
        + [pltpu.VMEM((32, NL), F32), pltpu.VMEM((32, 16), jnp.int32), pltpu.VMEM((32, 16), F32)],
        compiler_params=pltpu.CompilerParams(vmem_limit_bytes=56 << 20),
        interpret=INTERPRET,
    )(*operands)


def main_call(*operands):
    return call(
        main,
        [(3, 8, 16, NL), (3, 4, 8, NL)] + BLOCKS,
        *operands,
        keep(jnp.asarray(vertical_matrix(), jnp.bfloat16)),
        local=False,
        alias={0: 2, 1: 3, 2: 4, 3: 5},
        scratch=[(3, 12, 24, NL), (3, 12, 24, NL), (16, 24, NL), (6, 12, 24, NL), (16, 16, NL), (12, 24, NL)],
    )


def on_device(
    fine_now, fine_prev, coarse_now, coarse_prev, fine_rho, fine_mu, fine_lam, fine_metric,
    coarse_rho, coarse_mu, coarse_lam, coarse_metric, couple_index, couple_weight,
):
    gx, gy = lax.axis_size("gx"), lax.axis_size("gy")
    near_x, far_x, near_y, far_y = pairs(gx, 0), pairs(gx, 1), pairs(gy, 0), pairs(gy, 1)
    groups = [[i, i + 1] for i in range(0, gx, 2)]

    *own, yf, yn, ro = pack_call(
        fine_now, fine_prev, fine_rho, fine_mu, fine_lam, fine_metric,
        coarse_now, coarse_prev, coarse_rho, coarse_mu, coarse_lam, coarse_metric,
        couple_index, couple_weight,
    )
    own, ro = [keep(w) for w in own], keep(ro)
    yf = keep(lax.ppermute(yf, "gy", far_y))
    yn = keep(lax.ppermute(yn, "gy", near_y))
    *wide, an, am, af = call(pack_x, BLOCKS + [(AB, NL), (A_ROWS - AB, NL), (A_ROWS, NL)], *own)
    wide = [keep(w) for w in wide]
    af = keep(lax.ppermute(af, "gx", far_x))
    an = keep(lax.ppermute(an, "gx", near_x))
    am = keep(lax.ppermute(am, "gx", near_x))
    (cn,) = call(pack_near, [(C_ROWS + O_ROWS, NL)], yn, yf, ro)
    gn = keep(lax.all_gather(cn, "gx", axis_index_groups=groups))
    (bp,) = call(pack_far, [(C_ROWS + R_ROWS, NL)], yn, yf, gn)
    bp = keep(bp)
    bf = keep(lax.ppermute(bp, "gx", far_x))
    wide = call(fill, BLOCKS, *wide, yn, yf, gn, bp, alias={0: 0, 1: 1, 2: 2, 3: 3})
    wide = [keep(w) for w in wide]
    (r2,) = call(pack_second, [(R_ROWS, NL)], af, bf)
    g2 = keep(lax.all_gather(r2, "gx", axis_index_groups=groups))
    return tuple(main_call(*wide, an, am, af, bf, g2)[:2])


def solution(mesh):
    wide, flat = P(None, "gx", "gy", None), P("gx", "gy", None)
    return jax.shard_map(
        on_device,
        mesh=mesh,
        in_specs=(wide,) * 4 + (flat,) * 10,
        out_specs=(wide, wide),
        check_vma=False,
    )
```
